256 devices in a mesh: ctx: 32 (over x_hi, z, core), head: 8 (over x_lo, y).
Axes of the slice: x: 4 (x_hi: 2, x_lo: 2; x = x_hi * 2 + x_lo), y: 4, z: 8, core: 2. Of those that a mesh axis runs over, the one named last changes fastest.
Arguments:
- queries: bfloat16 [2, 4096, 8192], P(None, ('ctx', 'head')), as said below
- keys: bfloat16 [2, 4096, 1024], P(None, ('ctx', 'head')), as said below
- values: bfloat16 [2, 4096, 1024], P(None, ('ctx', 'head')), may hold values from -6 to 6
- outputs: bfloat16 [2, 4096, 8192], P(None, ('ctx', 'head')), may hold values from -4 to 4
- cotangent: bfloat16 [2, 4096, 8192], P(None, ('ctx', 'head')), may hold values from -4 to 4
- lengths: int32 [256], replicated, may hold values from 1 to 32, 4096 in all
Outputs:
- grad_queries: bfloat16 [2, 4096, 8192], P(None, ('ctx', 'head'))
- grad_keys: float32 [2, 4096, 1024], P(None, ('ctx', 'head'))
- grad_values: float32 [2, 4096, 1024], P(None, ('ctx', 'head'))
The draws below stay inside these ranges and needn't reach their ends.
Inputs may be any that keep to these rules, and one draw needn't show every extreme that they name: `lengths`: they sum to 4096, and one of them is exactly 32. `queries`: real-valued entries. `keys`: real-valued entries.
All inputs are finite; a program needn't handle non-finite values.
Results may differ from the reference program's by a relative error of at most 0.0025.
The reference program's roundings to bfloat16 on the way (of `prob_low` and `dscore`) count: a program that leaves them out, or rounds other values in their place, can miss the bound.
Values may be sent and summed in bfloat16 or wider, within the bound.
A program may use at most 64 MiB of HBM per device.

```python
import math
import jax
import jax.numpy as jnp
import numpy as np
from jax import lax

HD = 128
QHEADS = 64
KVHEADS = 8
QLEN = 16
DOC = 4096
QUESTIONS = 256
QMOST = 32


def drawn_pair(key):
    query_shape = (2, DOC, QHEADS * HD)
    key_shape = (2, DOC, KVHEADS * HD)
    key_keys = jax.random.fold_in(key, 11)
    key_queries = jax.random.fold_in(key, 23)
    base_keys = jnp.clip(jax.random.normal(key_keys, key_shape, jnp.float32), -6.0, 6.0)
    base_queries = jnp.clip(jax.random.normal(key_queries, query_shape, jnp.float32), -6.0, 6.0)
    return (base_queries, base_keys)


def draw_queries(key, part):
    return drawn_pair(key)[0].astype(jnp.bfloat16)


def draw_keys(key, part):
    return drawn_pair(key)[1].astype(jnp.bfloat16)


def level_of(own_key, extent, split, least, high):
    factor_of, own = 1.0, jax.random.fold_in(own_key, 6)
    for position, parts in split:
        steps = jnp.exp(jax.random.uniform(jax.random.fold_in(own, position), (parts,), jnp.float32, least / len(split), high / len(split)))
        factor_of = factor_of * jnp.repeat(steps, extent[position] // parts).reshape([-1 if axis == position else 1 for axis in range(len(extent))])
    return factor_of


def length_profile(count, total, reach, skew):
    loads = [(1 << 20) // math.isqrt(standing ** skew) + 1 for standing in range(2, count + 1)]
    spare, given = total - reach - (count - 1), [1] * (count - 1)
    while spare > 0:
        movable = [i for i in range(count - 1) if given[i] < reach]
        mass, remaining = sum([loads[i] for i in movable]), spare
        for i in movable:
            addition = min(reach - given[i], max(1, remaining * loads[i] // mass), spare)
            given[i] = given[i] + addition
            spare = spare - addition
    return np.array([reach] + given)


def ragged_sizes(own_key, count, total, limit, lean):
    if count == 2:
        one = jax.random.randint(own_key, (), max(1, total - limit), min(limit, total - 1) + 1)
        return jnp.stack([one, total - one])
    sizes = jnp.asarray(length_profile(count, total, limit, lean), jnp.int32)
    pairs = (count - 1) // 2
    giver, taker = sizes[1:1 + 2 * pairs:2], sizes[2:2 + 2 * pairs:2]
    room = jnp.minimum(giver - 1, limit - taker)
    shifted = jax.random.randint(jax.random.fold_in(own_key, 1), (pairs,), 0, 1 << 20) % (room + 1)
    sizes = sizes.at[1:1 + 2 * pairs:2].set(giver - shifted).at[2:2 + 2 * pairs:2].set(taker + shifted)
    return sizes[jax.random.permutation(jax.random.fold_in(own_key, 2), count)]


def scatter_about(own_key, dims, spread, bound, split=(), kind=jnp.bfloat16):
    values = spread * jax.random.normal(own_key, dims, jnp.float32)
    if split:
        values = values * level_of(own_key, dims, split, -0.22, 0.18)
    return jnp.clip(values, -bound, bound).astype(kind)


def setup_inputs(seed: int = 0) -> dict:
    seeds = jax.random.split(jax.random.key(seed), 7)
    return {
        "queries": draw_queries(jax.random.fold_in(seeds[6], 71), 0),
        "keys": draw_keys(jax.random.fold_in(seeds[6], 71), 0),
        "values": scatter_about(seeds[2], (2, DOC, KVHEADS * HD), 1.0, 6.0, ((1, 256),)),
        "outputs": scatter_about(seeds[3], (2, DOC, QHEADS * HD), 0.25, 4.0, ((1, 256),)),
        "cotangent": scatter_about(seeds[4], (2, DOC, QHEADS * HD), 0.25, 4.0, ((1, 256),)),
        "lengths": ragged_sizes(seeds[5], QUESTIONS, DOC, 2 * QLEN, 2).astype(jnp.int32),
    }


NEG_FILL = -1.0e30


def question_segments(lengths, offsets):
    starts = jnp.cumsum(lengths) - lengths
    matched = (starts[None, :] <= offsets[:, None]).astype(jnp.int32)
    return jnp.sum(matched, axis=1).astype(jnp.int32)


def allowed(query_pos, query_seg, key_pos, key_seg):
    same_doc = (key_seg[None, :] == 0) | (key_seg[None, :] == query_seg[:, None])
    return (key_pos[None, :] <= query_pos[:, None]) & same_doc


def head_block(query_blk, out_blk, cot_blk, key_blk, value_blk, visible, score_scale):
    query_f = query_blk.astype(jnp.float32)
    cot_f = cot_blk.astype(jnp.float32)
    key_f = key_blk.astype(jnp.float32)
    value_f = value_blk.astype(jnp.float32)
    scores = jnp.einsum("rgd,sd->grs", query_f, key_f) * score_scale
    mask_b = visible[None]
    run_max = jnp.max(jnp.where(mask_b, scores, NEG_FILL), axis=-1)
    run_sum = jnp.sum(jnp.where(mask_b, jnp.exp(scores - run_max[..., None]), 0.0), axis=-1)
    log_sum = run_max + jnp.log(run_sum)
    attn_prob = jnp.where(mask_b, jnp.exp(scores - log_sum[..., None]), 0.0)
    prob_low = attn_prob.astype(jnp.bfloat16)
    row_delta = jnp.transpose(jnp.sum(cot_f * out_blk.astype(jnp.float32), axis=-1))
    d_prob = jnp.einsum("rgd,sd->grs", cot_f, value_f)
    dscore = (attn_prob * (d_prob - row_delta[..., None])).astype(jnp.bfloat16)
    dscore_f = dscore.astype(jnp.float32)
    dquery = jnp.einsum("grs,sd->rgd", dscore_f, key_f) * score_scale
    d_key = jnp.einsum("grs,rgd->sd", dscore_f, query_f) * score_scale
    dvalue = jnp.einsum("grs,rgd->sd", prob_low.astype(jnp.float32), cot_f)
    return dquery, d_key, dvalue


def reference(queries, keys, values, outputs, cotangent, lengths):
    seq_len = 2 * DOC
    group_size = QHEADS // KVHEADS
    score_scale = HD ** -0.5
    query_all = jnp.moveaxis(queries.reshape(seq_len, KVHEADS, group_size, HD), 1, 0)
    out_all = jnp.moveaxis(outputs.reshape(seq_len, KVHEADS, group_size, HD), 1, 0)
    cot_all = jnp.moveaxis(cotangent.reshape(seq_len, KVHEADS, group_size, HD), 1, 0)
    key_all = jnp.moveaxis(keys.reshape(seq_len, KVHEADS, HD), 1, 0)
    value_all = jnp.moveaxis(values.reshape(seq_len, KVHEADS, HD), 1, 0)
    offsets = jnp.arange(DOC, dtype=jnp.int32)
    segment = jnp.concatenate([jnp.zeros((DOC,), jnp.int32), question_segments(lengths, offsets)])
    positions = jnp.arange(seq_len, dtype=jnp.int32)
    block_len = math.gcd(512, DOC)
    plans = []
    for block_no in range(DOC // block_len):
        plans.append((block_no * block_len, [(0, (block_no + 1) * block_len)]))
    for block_no in range(DOC // block_len):
        low_key = max(DOC, DOC + block_no * block_len - QMOST)
        plans.append((DOC + block_no * block_len, [(0, DOC), (low_key, DOC + (block_no + 1) * block_len)]))

    def one_head(inputs):
        head_q, head_k, head_v, head_o, head_c = inputs
        grad_q = jnp.zeros((seq_len, group_size, HD), jnp.float32)
        grad_k = jnp.zeros((seq_len, HD), jnp.float32)
        grad_v = jnp.zeros((seq_len, HD), jnp.float32)
        for first_row, spans in plans:
            last_row = first_row + block_len
            key_blk = jnp.concatenate([head_k[low:high] for low, high in spans], axis=0)
            value_blk = jnp.concatenate([head_v[low:high] for low, high in spans], axis=0)
            key_pos = jnp.concatenate([positions[low:high] for low, high in spans], axis=0)
            key_seg = jnp.concatenate([segment[low:high] for low, high in spans], axis=0)
            visible = allowed(positions[first_row:last_row], segment[first_row:last_row], key_pos, key_seg)
            dquery, d_key, dvalue = head_block(head_q[first_row:last_row], head_o[first_row:last_row],
                                               head_c[first_row:last_row], key_blk, value_blk, visible, score_scale)
            grad_q = grad_q.at[first_row:last_row].add(dquery)
            shift_at = 0
            for low, high in spans:
                grad_k = grad_k.at[low:high].add(d_key[shift_at:shift_at + high - low])
                grad_v = grad_v.at[low:high].add(dvalue[shift_at:shift_at + high - low])
                shift_at = shift_at + high - low
        return grad_q, grad_k, grad_v

    grad_q, grad_k, grad_v = lax.map(one_head, (query_all, key_all, value_all, out_all, cot_all))
    grad_queries = jnp.moveaxis(grad_q, 0, 1).reshape(2, DOC, QHEADS * HD).astype(jnp.bfloat16)
    grad_keys = jnp.moveaxis(grad_k, 0, 1).reshape(2, DOC, KVHEADS * HD)
    grad_values = jnp.moveaxis(grad_v, 0, 1).reshape(2, DOC, KVHEADS * HD)
    return grad_queries, grad_keys, grad_values
```

```python
import functools
import math

import jax
import jax.numpy as jnp
from jax import lax
from jax.experimental import pallas as pl
from jax.experimental.pallas import tpu as pltpu
from jax.sharding import PartitionSpec as P

HD = 128
NEG_FILL = -1e30
QMOST = 32
SCALE = HD ** (-0.5)
EXP2_SCALE = SCALE * math.log2(math.e)
MESH = pl.DeviceIdType.MESH
CHUNK = 256


def remote(src, dst, send_sem, recv_sem, device):
    return pltpu.make_async_remote_copy(
        src_ref=src,
        dst_ref=dst,
        send_sem=send_sem,
        recv_sem=recv_sem,
        device_id=device,
        device_id_type=MESH,
    )


class Place:
    def __init__(self, ctx_count, head_count):
        self.nctx = ctx_count
        self.nh = head_count
        self.nz = ctx_count // 4
        self.ctx = lax.axis_index("ctx")
        self.h = lax.axis_index("head")
        self.c = lax.rem(self.ctx, 2)
        self.z = lax.rem(self.ctx // 2, self.nz)
        self.xh = self.ctx // (2 * self.nz)
        half = self.nz // 2
        self.up = (half, half - 1)
        self.down = (half - 1, half)

    def zmod(self, z):
        return lax.rem(z + self.nz, self.nz)

    def block(self, xh, z, c):
        return (xh * self.nz + self.zmod(z)) * 2 + c

    def pair(self, xh, z):
        return xh * self.nz + self.zmod(z)

    def dev(self, xh, z, c):
        return (self.block(xh, z, c), self.h)

    def z_up(self):
        return self.dev(self.xh, self.z + 1, self.c)

    def z_down(self):
        return self.dev(self.xh, self.z - 1, self.c)

    def x_partner(self):
        return self.dev(1 - self.xh, self.z, self.c)

    def sibling(self):
        return self.dev(self.xh, self.z, 1 - self.c)

    def ctx_next(self):
        return (lax.rem(self.ctx + 1, self.nctx), self.h)

    def ctx_prev(self):
        return (lax.rem(self.ctx + self.nctx - 1, self.nctx), self.h)

    def head_peer(self, d):
        return lax.rem(self.h + d, self.nh)

    def head_source(self, d):
        return lax.rem(self.h + self.nh - d, self.nh)

    def barrier(self):
        barrier = pltpu.get_barrier_semaphore()

        def greet(d, _):
            pl.semaphore_signal(
                barrier, inc=1, device_id=(self.ctx, self.head_peer(d)), device_id_type=MESH
            )
            return 0

        lax.fori_loop(1, self.nh, greet, 0)
        near = (
            self.z_up(),
            self.z_down(),
            self.x_partner(),
            self.sibling(),
            self.ctx_next(),
            self.ctx_prev(),
        )
        for device in near:
            pl.semaphore_signal(barrier, inc=1, device_id=device, device_id_type=MESH)
        pl.semaphore_wait(barrier, self.nh - 1 + len(near))


def kernel_in(
    dims,
    q_ref,
    k_ref,
    v_ref,
    o_ref,
    c_ref,
    q_in,
    c_in,
    d_in,
    kvd,
    kvq,
    delta,
    kv_send,
    kv_recv,
    q_send,
    q_recv,
    c_send,
    c_recv,
    d_send,
    d_recv,
    g_send,
    g_recv,
    x_send,
    x_recv,
    local_sem,
):
    nctx, nh, tok, gw, bl, nhead = dims
    me = Place(nctx, nh)
    me.barrier()
    own_rows = pl.ds(pl.multiple_of(me.h * tok, tok), tok)

    def head_slice(ref, p, width):
        return ref.at[:, :, pl.ds(pl.multiple_of(p * width, width), width)]

    def kv_copies(d, p, device):
        copies = []
        for i, ref in enumerate((k_ref, v_ref)):
            cols = pl.ds(pl.multiple_of(p * HD, HD), HD)
            copies.append(
                remote(
                    ref.at[0, :, cols],
                    kvd.at[i, me.ctx, own_rows],
                    kv_send.at[2 * i, d],
                    kv_recv.at[2 * i, d],
                    device,
                )
            )
            copies.append(
                remote(
                    ref.at[1, :, cols],
                    kvq.at[i, 1, own_rows],
                    kv_send.at[2 * i + 1, d],
                    kv_recv.at[2 * i + 1, d],
                    device,
                )
            )
        return copies

    def q_copy(d, p, device):
        return remote(
            head_slice(q_ref, p, gw), q_in.at[:, me.h], q_send.at[d], q_recv.at[d], device
        )

    def c_copy(d, p, device):
        return remote(
            head_slice(c_ref, p, gw), c_in.at[:, me.h], c_send.at[d], c_recv.at[d], device
        )

    def d_copy(d, p, device):
        return remote(delta, d_in.at[:, me.h], d_send.at[d], d_recv.at[d], device)

    def over_peers(make, act):
        def step(d, _):
            p = me.head_peer(d)
            made = make(d, p, (me.ctx, p))
            for copy in made if isinstance(made, list) else [made]:
                act(copy)
            return 0

        lax.fori_loop(1, nh, step, 0)

    over_peers(kv_copies, lambda x: x.start())
    over_peers(q_copy, lambda x: x.start())
    over_peers(c_copy, lambda x: x.start())

    locals_ = []
    cols = pl.ds(pl.multiple_of(me.h * HD, HD), HD)
    for i, ref in enumerate((k_ref, v_ref)):
        locals_.append(
            pltpu.make_async_copy(
                ref.at[0, :, cols], kvd.at[i, me.ctx, own_rows], local_sem.at[2 * i]
            )
        )
        locals_.append(
            pltpu.make_async_copy(
                ref.at[1, :, cols], kvq.at[i, 1, own_rows], local_sem.at[2 * i + 1]
            )
        )
    locals_.append(
        pltpu.make_async_copy(head_slice(q_ref, me.h, gw), q_in.at[:, me.h], local_sem.at[4])
    )
    locals_.append(
        pltpu.make_async_copy(head_slice(c_ref, me.h, gw), c_in.at[:, me.h], local_sem.at[5])
    )
    for copy in locals_:
        copy.start()

    lanes = lax.broadcasted_iota(jnp.int32, (2, tok, HD), 2)

    def one_head(j, acc):
        at = pl.ds(pl.multiple_of(j * HD, HD), HD)
        prod = c_ref[:, :, at].astype(jnp.float32) * o_ref[:, :, at].astype(jnp.float32)
        return jnp.where(lanes == j, jnp.sum(prod, axis=-1, keepdims=True), acc)

    delta[...] = lax.fori_loop(0, nhead, one_head, jnp.zeros((2, tok, HD), jnp.float32))
    over_peers(d_copy, lambda x: x.start())
    own_delta = pltpu.make_async_copy(delta, d_in.at[:, me.h], local_sem.at[6])
    own_delta.start()

    for copy in locals_[:4]:
        copy.wait()

    def kv_arrived(d, _):
        for i in range(2):
            for j in range(2):
                dst = kvd.at[i, me.ctx, own_rows] if j == 0 else kvq.at[i, 1, own_rows]
                remote(
                    dst,
                    dst,
                    kv_send.at[2 * i + j, d],
                    kv_recv.at[2 * i + j, d],
                    (me.ctx, me.head_peer(d)),
                ).wait_recv()
        return 0

    lax.fori_loop(1, nh, kv_arrived, 0)

    tail = pl.ds(bl - QMOST, QMOST)
    tail_copy = remote(
        kvq.at[:, 1, tail], kvq.at[:, 0, tail], x_send, x_recv, me.ctx_next()
    )
    tail_copy.start()

    started = []

    def send(block, kind, device):
        copy = remote(
            kvd.at[:, block], kvd.at[:, block], g_send.at[kind, block], g_recv.at[block], device
        )
        copy.start()
        started.append(copy)

    def arrived(block):
        remote(
            kvd.at[:, block], kvd.at[:, block], g_send.at[0, block], g_recv.at[block], me.sibling()
        ).wait_recv()

    own = me.block(me.xh, me.z, me.c)
    other = me.block(1 - me.xh, me.z, me.c)
    send(own, 3, me.x_partner())
    send(own, 0, me.z_up())
    send(own, 1, me.z_down())
    send(own, 2, me.sibling())
    arrived(other)
    send(other, 0, me.z_up())
    send(other, 1, me.z_down())
    send(other, 2, me.sibling())
    for s in range(1, me.nz // 2 + 1):
        for xs in range(2):
            if s <= me.up[xs]:
                b = me.block(xs, me.z - s, me.c)
                arrived(b)
                if s < me.up[xs]:
                    send(b, 0, me.z_up())
                send(b, 2, me.sibling())
            if s <= me.down[xs]:
                b = me.block(xs, me.z + s, me.c)
                arrived(b)
                if s < me.down[xs]:
                    send(b, 1, me.z_down())
                send(b, 2, me.sibling())

    def from_sibling(i, _):
        arrived(2 * i + 1 - me.c)
        return 0

    lax.fori_loop(0, nctx // 2, from_sibling, 0)
    for copy in started:
        copy.wait_send()
    tail_copy.wait()
    for copy in locals_[4:]:
        copy.wait()
    own_delta.wait()
    over_peers(kv_copies, lambda x: x.wait_send())
    over_peers(q_copy, lambda x: x.wait())
    over_peers(c_copy, lambda x: x.wait())
    over_peers(d_copy, lambda x: x.wait())


def nt_dot(a, b):
    return lax.dot_general(a, b, (((1,), (1,)), ((), ())), preferred_element_type=jnp.float32)


def nn_dot(a, b):
    return jnp.dot(a, b, preferred_element_type=jnp.float32)


def kernel_mid(
    dims,
    len_ref,
    q_in,
    c_in,
    d_in,
    kvd,
    kvq,
    dq_out,
    dkv_out,
    dx_out,
    qs,
    cs,
    dd,
    weights,
    run_max,
    run_sum,
    tile_max,
    scale_inv,
    dqt,
    low_p,
    low_s,
    kx,
):
    nctx, nh, tok, gw, bl, nhead = dims
    ctx = lax.axis_index("ctx")
    h = lax.axis_index("head")
    group = gw // HD
    rows = group * bl
    npair = nctx // 2
    tile = 2 * bl
    own_pair = ctx // 2
    chunks = [pl.ds(r * CHUNK, CHUNK) for r in range(rows // CHUNK)]

    for s in range(2):
        for g in range(group):
            cols = slice(g * HD, (g + 1) * HD)
            qs[s, g * bl : (g + 1) * bl, :] = q_in[s, :, :, cols].reshape(bl, HD)
            cs[s, g * bl : (g + 1) * bl, :] = c_in[s, :, :, cols].reshape(bl, HD)
        turned = jnp.transpose(d_in[s].reshape(bl, HD))
        kx[0:HD, :] = turned
        mine = kx[pl.ds(pl.multiple_of(h * group, group), group), :]
        for g in range(group):
            dd[s, 0:1, g * bl : (g + 1) * bl] = mine[g : g + 1, :]

    count = len_ref.shape[1]
    lens = jnp.broadcast_to(len_ref[...].astype(jnp.float32), (8, count)).astype(jnp.bfloat16)
    i0 = lax.broadcasted_iota(jnp.int32, (count, count), 0)
    i1 = lax.broadcasted_iota(jnp.int32, (count, count), 1)
    before = jnp.where(i0 < i1, 1.0, 0.0).astype(jnp.bfloat16)
    after = jnp.where(i1 < i0, 1.0, 0.0).astype(jnp.bfloat16)
    starts_row = nn_dot(lens, before)[0:1, :]
    starts_col = nt_dot(after, lens)[:, 0:1]
    row_at = lax.broadcasted_iota(jnp.int32, (1, CHUNK), 1) % bl
    key_at = lax.broadcasted_iota(jnp.int32, (tile, 1), 0) - bl
    row_off = (row_at + ctx * bl).astype(jnp.float32)
    key_off = (key_at + ctx * bl).astype(jnp.float32)
    row_seg = jnp.sum(jnp.where(starts_col <= row_off, 1.0, 0.0), axis=0, keepdims=True)
    key_seg = jnp.sum(jnp.where(starts_row <= key_off, 1.0, 0.0), axis=1, keepdims=True)
    question_mask = (key_at <= row_at) & (key_seg == row_seg)
    doc_key = lax.broadcasted_iota(jnp.int32, (tile, 1), 0) + (own_pair * 2 - ctx) * bl
    doc_mask = doc_key <= row_at

    run_max[...] = jnp.full(run_max.shape, NEG_FILL, jnp.float32)
    run_sum[...] = jnp.zeros(run_sum.shape, jnp.float32)
    dqt[...] = jnp.zeros(dqt.shape, jnp.float32)

    def doc_kv(i, t):
        return kvd[i, pl.ds(2 * t, 2)].reshape(tile, HD)

    def question_kv(i):
        at = lax.broadcasted_iota(jnp.int32, (bl, HD), 0)
        prev = jnp.where(at >= bl - QMOST, kvq[i, 0].astype(jnp.float32), 0.0)
        return jnp.concatenate([prev.astype(jnp.bfloat16), kvq[i, 1]], axis=0)

    def first_pass(s, slot, keys, mask):
        for cols in chunks:
            scores = nt_dot(keys, qs[s, cols, :])
            if mask is not None:
                scores = jnp.where(mask, scores, NEG_FILL)
            old = run_max[s, 0:1, cols]
            new = jnp.maximum(old, jnp.max(scores, axis=0, keepdims=True))
            part = jnp.exp2((scores - new) * EXP2_SCALE)
            weights[slot, :, cols] = part
            run_sum[s, 0:1, cols] = run_sum[s, 0:1, cols] * jnp.exp2(
                (old - new) * EXP2_SCALE
            ) + jnp.sum(part, axis=0, keepdims=True)
            run_max[s, 0:1, cols] = new
            tile_max[slot, 0:1, cols] = new

    def slot_of(s, t):
        return s * (npair + 1) + t

    def pass_question(t, _):
        first_pass(1, npair + t, doc_kv(0, t), None)
        return 0

    def pass_doc(t, _):
        first_pass(0, t, doc_kv(0, t), None)
        return 0

    lax.fori_loop(0, npair, pass_question, 0)
    first_pass(1, 2 * npair, question_kv(0), question_mask)
    lax.fori_loop(0, own_pair, pass_doc, 0)
    first_pass(0, own_pair, doc_kv(0, own_pair), doc_mask)
    for s in range(2):
        scale_inv[s] = 1.0 / run_sum[s]

    def second_pass(s, slot, keys, values):
        for cols in chunks:
            factor = (
                jnp.exp2((tile_max[slot, 0:1, cols] - run_max[s, 0:1, cols]) * EXP2_SCALE)
                * scale_inv[s, 0:1, cols]
            )
            prob = weights[slot, :, cols] * factor
            d_prob = nt_dot(values, cs[s, cols, :])
            low_p[:, cols] = prob.astype(jnp.bfloat16)
            low_s[:, cols] = (prob * (d_prob - dd[s, 0:1, cols])).astype(jnp.bfloat16)
        d_value = nn_dot(low_p[...], cs[s])
        d_key = nn_dot(low_s[...], qs[s])
        keys_t = jnp.transpose(keys.astype(jnp.float32)).astype(jnp.bfloat16)
        dqt[s] += nn_dot(keys_t, low_s[...])
        return d_key, d_value

    def put(t, i, value, add):
        for c in range(2):
            part = value[c * bl : (c + 1) * bl]
            if add:
                part = dkv_out[t, i, c] + part
            dkv_out[t, i, c] = part

    def backward(t, _):
        keys, values = doc_kv(0, t), doc_kv(1, t)
        for i, value in enumerate(second_pass(1, npair + t, keys, values)):
            put(t, i, value, False)

        @pl.when(t <= own_pair)
        def _():
            for i, value in enumerate(second_pass(0, t, keys, values)):
                put(t, i, value, True)

        return 0

    lax.fori_loop(0, npair, backward, 0)
    d_key, d_value = second_pass(1, 2 * npair, question_kv(0), question_kv(1))
    dx_out[0] = d_key
    dx_out[1] = d_value
    for s in range(2):
        for g in range(group):
            part = jnp.transpose(dqt[s, :, g * bl : (g + 1) * bl])
            dq_out[s, :, g * HD : (g + 1) * HD] = (part * SCALE).astype(jnp.bfloat16)


def kernel_out(
    dims,
    dq,
    dkv,
    dx,
    gq,
    gk,
    gv,
    from_core,
    chain,
    from_x,
    from_next,
    sums,
    result,
    q_send,
    q_recv,
    core_send,
    core_recv,
    chain_send,
    chain_recv,
    x_send,
    x_recv,
    n_send,
    n_recv,
    r_send,
    r_recv,
    local_sem,
):
    nctx, nh, tok, gw, bl, nhead = dims
    npair = nctx // 2
    me = Place(nctx, nh)
    me.barrier()

    def rows_of(p):
        return pl.ds(pl.multiple_of(p * tok, tok), tok)

    q_cols = pl.ds(pl.multiple_of(me.h * gw, gw), gw)
    kv_cols = pl.ds(pl.multiple_of(me.h * HD, HD), HD)

    back = remote(
        dx.at[:, pl.ds(bl - QMOST, QMOST)], from_next, n_send, n_recv, me.ctx_prev()
    )
    back.start()
    core_copies = []

    def core_copy(t):
        return remote(
            dkv.at[t, :, 1 - me.c],
            from_core.at[t],
            core_send.at[t],
            core_recv.at[t],
            me.sibling(),
        )

    def core_start(t, _):
        core_copy(t).start()
        return 0

    lax.fori_loop(0, npair, core_start, 0)

    def q_copy(d):
        p = me.head_peer(d)
        return remote(
            dq.at[:, rows_of(p)], gq.at[:, :, q_cols], q_send.at[d], q_recv.at[d], (me.ctx, p)
        )

    def q_start(d, _):
        q_copy(d).start()
        return 0

    lax.fori_loop(1, nh, q_start, 0)
    own_q = pltpu.make_async_copy(dq.at[:, rows_of(me.h)], gq.at[:, :, q_cols], local_sem.at[0])
    own_q.start()

    def core_wait(t, _):
        core_copy(t).wait()
        sums[t] = dkv[t, :, me.c] + from_core[t]
        return 0

    lax.fori_loop(0, npair, core_wait, 0)

    started = []

    def hop(way, xs, j, src):
        copy = remote(
            src,
            chain.at[way, xs, j],
            chain_send.at[way, xs, j],
            chain_recv.at[way, xs, j],
            me.z_up() if way == 0 else me.z_down(),
        )
        copy.start()
        started.append(copy)

    def hop_arrived(way, xs, j):
        remote(
            chain.at[way, xs, j],
            chain.at[way, xs, j],
            chain_send.at[way, xs, j],
            chain_recv.at[way, xs, j],
            me.z_up(),
        ).wait_recv()

    length = (me.up, me.down)

    def target(way, xs, j):
        far = length[way][xs] - j
        return me.pair(xs, me.z + far if way == 0 else me.z - far)

    for way in range(2):
        for xs in range(2):
            hop(way, xs, 0, sums.at[target(way, xs, 0)])
    for j in range(1, me.nz // 2):
        for way in range(2):
            for xs in range(2):
                if j < length[way][xs]:
                    hop_arrived(way, xs, j - 1)
                    t = target(way, xs, j)
                    chain[way, xs, j - 1] += sums[t]
                    hop(way, xs, j, chain.at[way, xs, j - 1])
    for way in range(2):
        for xs in range(2):
            hop_arrived(way, xs, length[way][xs] - 1)
    for xs in range(2):
        t = me.pair(xs, me.z)
        sums[t] = (
            sums[t]
            + chain[0, xs, length[0][xs] - 1]
            + chain[1, xs, length[1][xs] - 1]
        )
    x_copy = remote(
        sums.at[me.pair(1 - me.xh, me.z)], from_x, x_send, x_recv, me.x_partner()
    )
    x_copy.start()
    back.wait()
    for i in range(2):
        factor = SCALE if i == 0 else 1.0
        result[i, 1, 0 : bl - QMOST] = dx[i, bl : 2 * bl - QMOST] * factor
        result[i, 1, bl - QMOST : bl] = (
            dx[i, 2 * bl - QMOST : 2 * bl] + from_next[i]
        ) * factor

    def r_copy(d, i, s):
        p = me.head_peer(d)
        return remote(
            result.at[i, s, rows_of(p)],
            (gk, gv)[i].at[s, :, kv_cols],
            r_send.at[2 * i + s, d],
            r_recv.at[2 * i + s, d],
            (me.ctx, p),
        )

    def own_r(i, s):
        return pltpu.make_async_copy(
            result.at[i, s, rows_of(me.h)],
            (gk, gv)[i].at[s, :, kv_cols],
            local_sem.at[1 + 2 * i + s],
        )

    def r_start(s):
        def step(d, _):
            for i in range(2):
                r_copy(d, i, s).start()
            return 0

        lax.fori_loop(1, nh, step, 0)
        for i in range(2):
            own_r(i, s).start()

    r_start(1)
    x_copy.wait()
    own = me.pair(me.xh, me.z)
    for i in range(2):
        factor = SCALE if i == 0 else 1.0
        result[i, 0] = (sums[own, i] + from_x[i]) * factor
    r_start(0)
    for copy in started:
        copy.wait_send()

    def ends(d, _):
        q_copy(d).wait()
        for i in range(2):
            for s in range(2):
                r_copy(d, i, s).wait()
        return 0

    lax.fori_loop(1, nh, ends, 0)
    own_q.wait()
    for i in range(2):
        for s in range(2):
            own_r(i, s).wait()


def shards(queries, keys, values, outputs, cotangent, lengths):
    nctx, nh = lax.axis_size("ctx"), lax.axis_size("head")
    tok = queries.shape[1]
    gw = queries.shape[2] // nh
    bl = tok * nh
    nhead = queries.shape[2] // HD
    dims = (nctx, nh, tok, gw, bl, nhead)
    npair = nctx // 2
    rows = gw // HD * bl
    hbm = pl.BlockSpec(memory_space=pl.ANY)
    vmem = pl.BlockSpec(memory_space=pltpu.VMEM)
    dma = pltpu.SemaphoreType.DMA
    f32, b16 = jnp.float32, jnp.bfloat16
    shape = jax.ShapeDtypeStruct
    q_in, c_in, d_in, kvd, kvq = pl.pallas_call(
        functools.partial(kernel_in, dims),
        out_shape=(
            shape((2, nh, tok, gw), b16),
            shape((2, nh, tok, gw), b16),
            shape((2, nh, tok, HD), f32),
            shape((2, nctx, bl, HD), b16),
            shape((2, 2, bl, HD), b16),
        ),
        in_specs=[hbm, hbm, hbm, vmem, vmem],
        out_specs=[hbm] * 5,
        scratch_shapes=[
            pltpu.VMEM((2, tok, HD), f32),
            dma((4, nh)),
            dma((4, nh)),
            dma((nh,)),
            dma((nh,)),
            dma((nh,)),
            dma((nh,)),
            dma((nh,)),
            dma((nh,)),
            dma((4, nctx)),
            dma((nctx,)),
            dma,
            dma,
            dma((7,)),
        ],
        compiler_params=pltpu.CompilerParams(collective_id=0, has_side_effects=True),
        name="exchange_in",
    )(queries, keys, values, outputs, cotangent)
    dq, dkv, dx = pl.pallas_call(
        functools.partial(kernel_mid, dims),
        out_shape=(
            shape((2, bl, gw), b16),
            shape((npair, 2, 2, bl, HD), f32),
            shape((2, 2 * bl, HD), f32),
        ),
        in_specs=[vmem] * 6,
        out_specs=[vmem] * 3,
        scratch_shapes=[
            pltpu.VMEM((2, rows, HD), b16),
            pltpu.VMEM((2, rows, HD), b16),
            pltpu.VMEM((2, 1, rows), f32),
            pltpu.VMEM((2 * npair + 1, 2 * bl, rows), f32),
            pltpu.VMEM((2, 1, rows), f32),
            pltpu.VMEM((2, 1, rows), f32),
            pltpu.VMEM((2 * npair + 1, 1, rows), f32),
            pltpu.VMEM((2, 1, rows), f32),
            pltpu.VMEM((2, HD, rows), f32),
            pltpu.VMEM((2 * bl, rows), b16),
            pltpu.VMEM((2 * bl, rows), b16),
            pltpu.VMEM((HD, bl), f32),
        ],
        compiler_params=pltpu.CompilerParams(vmem_limit_bytes=60 * 2**20),
        name="attention_backward",
    )(lengths.reshape(1, -1), q_in, c_in, d_in, kvd, kvq)
    steps = nctx // 8
    return pl.pallas_call(
        functools.partial(kernel_out, dims),
        out_shape=(
            shape((2, tok, nh * gw), b16),
            shape((2, tok, nh * HD), f32),
            shape((2, tok, nh * HD), f32),
        ),
        in_specs=[hbm, vmem, vmem],
        out_specs=[hbm] * 3,
        scratch_shapes=[
            pltpu.VMEM((npair, 2, bl, HD), f32),
            pltpu.VMEM((2, 2, steps, 2, bl, HD), f32),
            pltpu.VMEM((2, bl, HD), f32),
            pltpu.VMEM((2, QMOST, HD), f32),
            pltpu.VMEM((npair, 2, bl, HD), f32),
            pltpu.VMEM((2, 2, bl, HD), f32),
            dma((nh,)),
            dma((nh,)),
            dma((npair,)),
            dma((npair,)),
            dma((2, 2, steps)),
            dma((2, 2, steps)),
            dma,
            dma,
            dma,
            dma,
            dma((4, nh)),
            dma((4, nh)),
            dma((5,)),
        ],
        compiler_params=pltpu.CompilerParams(
            collective_id=1, has_side_effects=True, vmem_limit_bytes=40 * 2**20
        ),
        name="exchange_out",
    )(dq, dkv, dx)


def solution(mesh):
    spec = P(None, ("ctx", "head"), None)
    return jax.shard_map(
        shards,
        mesh=mesh,
        in_specs=(spec,) * 5 + (P(),),
        out_specs=(spec,) * 3,
        check_vma=False,
    )
```

```python
import functools
import math

import jax
import jax.numpy as jnp
from jax import lax
from jax.experimental import pallas as pl
from jax.experimental.pallas import tpu as pltpu
from jax.sharding import PartitionSpec as P

HD = 128
NEG_FILL = -1e30
QMOST = 32
SCALE = HD ** (-0.5)
EXP2_SCALE = SCALE * math.log2(math.e)
MESH = pl.DeviceIdType.MESH
CHUNK = 256
LAG = 2


def remote(src, dst, send_sem, recv_sem, device):
    return pltpu.make_async_remote_copy(
        src_ref=src,
        dst_ref=dst,
        send_sem=send_sem,
        recv_sem=recv_sem,
        device_id=device,
        device_id_type=MESH,
    )


class Place:
    def __init__(self, ctx_count, head_count):
        self.nctx = ctx_count
        self.nh = head_count
        self.nz = ctx_count // 4
        self.half = self.nz // 2
        self.npair = ctx_count // 2
        self.ctx = lax.axis_index("ctx")
        self.h = lax.axis_index("head")
        self.c = lax.rem(self.ctx, 2)
        self.z = lax.rem(self.ctx // 2, self.nz)
        self.xh = self.ctx // (2 * self.nz)

    def zmod(self, z):
        return lax.rem(z + self.nz, self.nz)

    def block(self, xh, z, c):
        return (xh * self.nz + self.zmod(z)) * 2 + c

    def pair(self, xh, z):
        return xh * self.nz + self.zmod(z)

    def dev(self, xh, z, c):
        return (self.block(xh, z, c), self.h)

    def z_up(self):
        return self.dev(self.xh, self.z + 1, self.c)

    def z_down(self):
        return self.dev(self.xh, self.z - 1, self.c)

    def x_partner(self):
        return self.dev(1 - self.xh, self.z, self.c)

    def sibling(self):
        return self.dev(self.xh, self.z, 1 - self.c)

    def ctx_next(self):
        return (lax.rem(self.ctx + 1, self.nctx), self.h)

    def ctx_prev(self):
        return (lax.rem(self.ctx + self.nctx - 1, self.nctx), self.h)

    def head_peer(self, d):
        return lax.rem(self.h + d, self.nh)

    def far(self, q):
        return self.half - q // 4

    def way(self, q):
        return q % 2

    def xs(self, q):
        return (q // 2 + q) % 2

    def reach(self, q):
        return self.half - (self.way(q) + self.xs(q) + 1) % 2

    def z_of(self, q):
        return self.z + self.far(q) * (1 - 2 * self.way(q))

    def pair_of(self, q):
        return self.pair(self.xs(q), self.z_of(q))

    def block_of(self, q, c):
        return self.block(self.xs(q), self.z_of(q), c)

    def barrier(self):
        barrier = pltpu.get_barrier_semaphore()

        def greet(d, _):
            pl.semaphore_signal(
                barrier, inc=1, device_id=(self.ctx, self.head_peer(d)), device_id_type=MESH
            )
            return 0

        lax.fori_loop(1, self.nh, greet, 0)
        near = (
            self.z_up(),
            self.z_down(),
            self.x_partner(),
            self.sibling(),
            self.ctx_next(),
            self.ctx_prev(),
        )
        for device in near:
            pl.semaphore_signal(barrier, inc=1, device_id=device, device_id_type=MESH)
        pl.semaphore_wait(barrier, self.nh - 1 + len(near))


def nt_dot(a, b):
    return lax.dot_general(a, b, (((1,), (1,)), ((), ())), preferred_element_type=jnp.float32)


def nn_dot(a, b):
    return jnp.dot(a, b, preferred_element_type=jnp.float32)


def by_sublane(x):
    return x.reshape(x.shape[0] // 8, 8, x.shape[1])


def kernel(
    dims,
    len_ref,
    q_ref,
    k_ref,
    v_ref,
    o_ref,
    c_ref,
    gq,
    gk,
    gv,
    q_in,
    c_in,
    d_in,
    kvd,
    kvq,
    delta,
    qs,
    cs,
    dd,
    turn,
    weights,
    peak,
    total,
    final_max,
    inverse,
    dqt,
    low_p,
    low_s,
    dkv,
    dx,
    dq,
    from_core,
    sums,
    chain,
    from_x,
    from_next,
    result,
    kv_send,
    kv_recv,
    q_send,
    q_recv,
    c_send,
    c_recv,
    d_send,
    d_recv,
    g_send,
    g_recv,
    t_send,
    t_recv,
    core_send,
    core_recv,
    hop_send,
    hop_recv,
    x_send,
    x_recv,
    n_send,
    n_recv,
    o_send,
    o_recv,
    r_send,
    r_recv,
    local_sem,
):
    nctx, nh, tok, gw, bl, nhead = dims
    me = Place(nctx, nh)
    npair = me.npair
    last = 4 * me.half + 1
    group = gw // HD
    rows = group * bl
    tile = 2 * bl
    own_pair = me.ctx // 2
    chunks = [pl.ds(r * CHUNK, CHUNK) for r in range(rows // CHUNK)]
    me.barrier()

    def rows_of(p):
        return pl.ds(pl.multiple_of(p * tok, tok), tok)

    own_rows = rows_of(me.h)

    def head_slice(ref, p, width):
        return ref.at[:, :, pl.ds(pl.multiple_of(p * width, width), width)]

    def over_peers(make, act):
        def step(d, _):
            p = me.head_peer(d)
            made = make(d, p, (me.ctx, p))
            for copy in made if isinstance(made, list) else [made]:
                act(copy)
            return 0

        lax.fori_loop(1, nh, step, 0)

    def start(copy):
        copy.start()

    def wait(copy):
        copy.wait()

    def wait_send(copy):
        copy.wait_send()

    def wait_recv(copy):
        copy.wait_recv()

    def kv_targets(i):
        return kvd.at[i, me.ctx, own_rows], kvq.at[i, 1, own_rows]

    def kv_copies(d, p, device):
        cols = pl.ds(pl.multiple_of(p * HD, HD), HD)
        return [
            remote(
                ref.at[j, :, cols],
                kv_targets(i)[j],
                kv_send.at[2 * i + j, d],
                kv_recv.at[2 * i + j, d],
                device,
            )
            for i, ref in enumerate((k_ref, v_ref))
            for j in range(2)
        ]

    def kv_arrivals(d, p, device):
        return [
            remote(
                kv_targets(i)[j],
                kv_targets(i)[j],
                kv_send.at[2 * i + j, d],
                kv_recv.at[2 * i + j, d],
                device,
            )
            for i in range(2)
            for j in range(2)
        ]

    def q_copy(d, p, device):
        return remote(
            head_slice(q_ref, p, gw), q_in.at[:, me.h], q_send.at[d], q_recv.at[d], device
        )

    def c_copy(d, p, device):
        return remote(
            head_slice(c_ref, p, gw), c_in.at[:, me.h], c_send.at[d], c_recv.at[d], device
        )

    def d_copy(d, p, device):
        return remote(delta, d_in.at[:, me.h], d_send.at[d], d_recv.at[d], device)

    over_peers(kv_copies, start)
    over_peers(q_copy, start)
    over_peers(c_copy, start)

    own_cols = pl.ds(pl.multiple_of(me.h * HD, HD), HD)
    locals_ = [
        pltpu.make_async_copy(ref.at[j, :, own_cols], kv_targets(i)[j], local_sem.at[2 * i + j])
        for i, ref in enumerate((k_ref, v_ref))
        for j in range(2)
    ]
    own_q = pltpu.make_async_copy(head_slice(q_ref, me.h, gw), q_in.at[:, me.h], local_sem.at[4])
    own_c = pltpu.make_async_copy(head_slice(c_ref, me.h, gw), c_in.at[:, me.h], local_sem.at[5])
    for copy in locals_:
        copy.start()
    own_q.start()
    own_c.start()
    for copy in locals_:
        copy.wait()
    over_peers(kv_arrivals, wait_recv)

    def gather_copy(b, kind, device):
        return remote(
            kvd.at[:, b], kvd.at[:, b], g_send.at[kind, b], g_recv.at[b], device
        )

    sent = []

    def send_block(b, kind, device):
        copy = gather_copy(b, kind, device)
        copy.start()
        sent.append(copy)

    def arrived(b):
        gather_copy(b, 0, me.sibling()).wait_recv()

    tail = pl.ds(bl - QMOST, QMOST)
    tail_copy = remote(kvq.at[:, 1, tail], kvq.at[:, 0, tail], t_send, t_recv, me.ctx_next())

    def gather_own(b):
        send_block(b, 0, me.z_up())
        send_block(b, 1, me.z_down())
        send_block(b, 2, me.sibling())

    def gather_step(q):
        b = me.block_of(q, me.c)
        arrived(b)
        if me.far(q) < me.reach(q):
            send_block(b, me.way(q), me.z_down() if me.way(q) == 0 else me.z_up())
        send_block(b, 2, me.sibling())

    send_block(me.ctx, 3, me.x_partner())
    gather_own(me.ctx)
    tail_copy.start()

    lanes = lax.broadcasted_iota(jnp.int32, (2, tok, HD), 2)

    def one_head(j, acc):
        at = pl.ds(pl.multiple_of(j * HD, HD), HD)
        prod = c_ref[:, :, at].astype(jnp.float32) * o_ref[:, :, at].astype(jnp.float32)
        return jnp.where(lanes == j, jnp.sum(prod, axis=-1, keepdims=True), acc)

    delta[...] = lax.fori_loop(0, nhead, one_head, jnp.zeros((2, tok, HD), jnp.float32))
    over_peers(d_copy, start)
    own_delta = pltpu.make_async_copy(delta, d_in.at[:, me.h], local_sem.at[6])
    own_delta.start()

    other = me.block(1 - me.xh, me.z, me.c)
    arrived(other)
    gather_own(other)

    count = len_ref.shape[1]
    lens = jnp.broadcast_to(len_ref[...].astype(jnp.float32), (8, count)).astype(jnp.bfloat16)
    i0 = lax.broadcasted_iota(jnp.int32, (count, count), 0)
    i1 = lax.broadcasted_iota(jnp.int32, (count, count), 1)
    before = jnp.where(i0 < i1, 1.0, 0.0).astype(jnp.bfloat16)
    after = jnp.where(i1 < i0, 1.0, 0.0).astype(jnp.bfloat16)
    starts_row = nn_dot(lens, before)[0:1, :]
    starts_col = nt_dot(after, lens)[:, 0:1]
    row_at = lax.broadcasted_iota(jnp.int32, (1, CHUNK), 1) % bl
    key_at = lax.broadcasted_iota(jnp.int32, (tile, 1), 0) - bl
    row_off = (row_at + me.ctx * bl).astype(jnp.float32)
    key_off = (key_at + me.ctx * bl).astype(jnp.float32)
    row_seg = jnp.sum(jnp.where(starts_col <= row_off, 1.0, 0.0), axis=0, keepdims=True)
    key_seg = jnp.sum(jnp.where(starts_row <= key_off, 1.0, 0.0), axis=1, keepdims=True)
    question_mask = (key_at <= row_at) & (key_seg == row_seg)
    doc_key = lax.broadcasted_iota(jnp.int32, (tile, 1), 0) + (own_pair * 2 - me.ctx) * bl
    doc_mask = doc_key <= row_at

    peak[...] = jnp.full(peak.shape, NEG_FILL, jnp.float32)
    total[...] = jnp.zeros(total.shape, jnp.float32)
    dqt[...] = jnp.zeros(dqt.shape, jnp.float32)

    def doc_kv(i, t):
        return kvd[i, pl.ds(2 * t, 2)].reshape(tile, HD)

    def question_kv(i):
        at = lax.broadcasted_iota(jnp.int32, (bl, HD), 0)
        prev = jnp.where(at >= bl - QMOST, kvq[i, 0].astype(jnp.float32), 0.0)
        return jnp.concatenate([prev.astype(jnp.bfloat16), kvq[i, 1]], axis=0)

    def scores_of(s, keys, mask, cols):
        scores = nt_dot(keys, qs[s, cols, :])
        return scores if mask is None else jnp.where(mask, scores, NEG_FILL)

    def peak_sweep(s, keys, mask):
        for cols in chunks:
            scores = by_sublane(scores_of(s, keys, mask, cols))
            peak[s, :, cols] = jnp.maximum(peak[s, :, cols], jnp.max(scores, axis=0))

    def weight_sweep(s, slot, keys, mask):
        for cols in chunks:
            scores = scores_of(s, keys, mask, cols)
            part = jnp.exp2((scores - final_max[s, 0:1, cols]) * EXP2_SCALE)
            weights[slot, :, cols] = part
            total[s, :, cols] = total[s, :, cols] + jnp.sum(by_sublane(part), axis=0)

    def on_pair(t, question, doc):
        question(None)

        @pl.when(t < own_pair)
        def _():
            doc(None)

        @pl.when(t == own_pair)
        def _():
            doc(doc_mask)

    for q in range(4 * me.half - 1, 4 * me.half - 5, -1):
        gather_step(q)
    for q in range(4 * me.half - 5, max(4 * me.half - 9, 1), -1):
        gather_step(q)

    own_q.wait()
    over_peers(q_copy, wait_recv)
    for s in range(2):
        for g in range(group):
            cols = slice(g * HD, (g + 1) * HD)
            qs[s, g * bl : (g + 1) * bl, :] = q_in[s, :, :, cols].reshape(bl, HD)

    def peaks(first, count):
        def step(i, _):
            q = first - i
            arrived(me.block_of(q, 1 - me.c))
            t = me.pair_of(q)
            keys = doc_kv(0, t)
            on_pair(
                t, lambda m: peak_sweep(1, keys, m), lambda m: peak_sweep(0, keys, m)
            )
            return 0

        lax.fori_loop(0, count, step, 0)

    peaks(last, 2)
    tail_copy.wait_recv()
    peak_sweep(1, question_kv(0), question_mask)
    peaks(last - 2, 4)
    for f in range(3, me.half + 1):
        top = last - 2 - 4 * (f - 1)
        for q in range(top, max(top - 4, 1), -1):
            gather_step(q)
        peaks(top + 4, 4)
    peaks(3 if me.half > 1 else 1, 2)

    for s in range(2):
        final_max[s] = jnp.max(peak[s], axis=0, keepdims=True)

    def weigh(t, _):
        keys = doc_kv(0, t)
        on_pair(
            t,
            lambda m: weight_sweep(1, npair + t, keys, m),
            lambda m: weight_sweep(0, t, keys, m),
        )
        return 0

    lax.fori_loop(0, npair, weigh, 0)
    weight_sweep(1, 2 * npair, question_kv(0), question_mask)
    for s in range(2):
        inverse[s] = 1.0 / jnp.sum(total[s], axis=0, keepdims=True)

    own_c.wait()
    own_delta.wait()
    over_peers(c_copy, wait_recv)
    over_peers(d_copy, wait_recv)
    for s in range(2):
        for g in range(group):
            cols = slice(g * HD, (g + 1) * HD)
            cs[s, g * bl : (g + 1) * bl, :] = c_in[s, :, :, cols].reshape(bl, HD)
        turn[...] = jnp.transpose(d_in[s].reshape(bl, HD))
        mine = turn[pl.ds(pl.multiple_of(me.h * group, group), group), :]
        for g in range(group):
            dd[s, 0:1, g * bl : (g + 1) * bl] = mine[g : g + 1, :]

    def backward(s, slot, keys, values):
        for cols in chunks:
            prob = weights[slot, :, cols] * inverse[s, 0:1, cols]
            d_prob = nt_dot(values, cs[s, cols, :])
            low_p[:, cols] = prob.astype(jnp.bfloat16)
            low_s[:, cols] = (prob * (d_prob - dd[s, 0:1, cols])).astype(jnp.bfloat16)
        d_value = nn_dot(low_p[...], cs[s])
        d_key = nn_dot(low_s[...], qs[s])
        keys_t = jnp.transpose(keys.astype(jnp.float32)).astype(jnp.bfloat16)
        dqt[s] += nn_dot(keys_t, low_s[...])
        return d_key, d_value

    def put(t, i, value, add):
        for c in range(2):
            part = value[c * bl : (c + 1) * bl]
            dkv[t, i, c] = dkv[t, i, c] + part if add else part

    def core_copy(t):
        return remote(
            dkv.at[t, :, 1 - me.c],
            from_core.at[t],
            core_send.at[t],
            core_recv.at[t],
            me.sibling(),
        )

    def hop_copy(way, xs, f):
        return remote(
            sums.at[me.pair(xs, me.z + f * (1 - 2 * way))],
            chain.at[way, xs, f - 1],
            hop_send.at[way, xs, f - 1],
            hop_recv.at[way, xs, f - 1],
            me.dev(me.xh, me.z + 1 - 2 * way, me.c),
        )

    def serve(q):
        f, way, xs, t = me.far(q), me.way(q), me.xs(q), me.pair_of(q)
        core_copy(t).wait_recv()
        sums[t] = dkv[t, :, me.c] + from_core[t]

        @pl.when((f > 0) & (f < me.reach(q)))
        def _():
            hop_copy(way, xs, f + 1).wait_recv()
            sums[t] = sums[t] + chain[way, xs, f]

        @pl.when(f > 0)
        def _():
            hop_copy(way, xs, f).start()

    def backward_pair(n, _):
        q = n + 2
        t = me.pair_of(q)
        keys, values = doc_kv(0, t), doc_kv(1, t)
        for i, value in enumerate(backward(1, npair + t, keys, values)):
            put(t, i, value, False)

        @pl.when(t <= own_pair)
        def _():
            for i, value in enumerate(backward(0, t, keys, values)):
                put(t, i, value, True)

        core_copy(t).start()

        @pl.when(n >= LAG)
        def _():
            serve(q - LAG)

        return 0

    lax.fori_loop(0, npair, backward_pair, 0)
    d_key, d_value = backward(1, 2 * npair, question_kv(0), question_kv(1))
    dx[0] = d_key
    dx[1] = d_value
    next_copy = remote(dx.at[:, tail], from_next, n_send, n_recv, me.ctx_prev())
    next_copy.start()

    for s in range(2):
        for g in range(group):
            part = jnp.transpose(dqt[s, :, g * bl : (g + 1) * bl])
            dq[s, :, g * HD : (g + 1) * HD] = (part * SCALE).astype(jnp.bfloat16)

    q_cols = pl.ds(pl.multiple_of(me.h * gw, gw), gw)

    def out_copy(d, p, device):
        return remote(
            dq.at[:, rows_of(p)], gq.at[:, :, q_cols], o_send.at[d], o_recv.at[d], device
        )

    own_out = pltpu.make_async_copy(dq.at[:, own_rows], gq.at[:, :, q_cols], local_sem.at[4])

    def serve_rest(n, _):
        serve(n + 2)
        return 0

    lax.fori_loop(npair - LAG, npair, serve_rest, 0)

    for way in range(2):
        for xs in range(2):
            hop_copy(way, xs, 1).wait_recv()
    for xs in range(2):
        t = me.pair(xs, me.z)
        sums[t] = sums[t] + chain[0, xs, 0] + chain[1, xs, 0]
    x_copy = remote(
        sums.at[me.pair(1 - me.xh, me.z)], from_x, x_send, x_recv, me.x_partner()
    )
    x_copy.start()
    over_peers(out_copy, start)
    own_out.start()
    next_copy.wait_recv()
    for i in range(2):
        factor = SCALE if i == 0 else 1.0
        result[i, 1, 0 : bl - QMOST] = dx[i, bl : 2 * bl - QMOST] * factor
        result[i, 1, bl - QMOST : bl] = (
            dx[i, 2 * bl - QMOST : 2 * bl] + from_next[i]
        ) * factor

    def r_copies(s):
        def made(d, p, device):
            return [
                remote(
                    result.at[i, s, rows_of(p)],
                    (gk, gv)[i].at[s, :, own_cols],
                    r_send.at[2 * i + s, d],
                    r_recv.at[2 * i + s, d],
                    device,
                )
                for i in range(2)
            ]

        return made

    def own_r(i, s):
        return pltpu.make_async_copy(
            result.at[i, s, own_rows], (gk, gv)[i].at[s, :, own_cols], local_sem.at[2 * i + s]
        )

    over_peers(r_copies(1), start)
    for i in range(2):
        own_r(i, 1).start()
    x_copy.wait_recv()
    own = me.pair(me.xh, me.z)
    for i in range(2):
        factor = SCALE if i == 0 else 1.0
        result[i, 0] = (sums[own, i] + from_x[i]) * factor
    over_peers(r_copies(0), start)
    for i in range(2):
        own_r(i, 0).start()

    for copy in sent:
        copy.wait_send()
    for make in (kv_copies, q_copy, c_copy, d_copy):
        over_peers(make, wait_send)
    tail_copy.wait_send()

    def core_done(t, _):
        core_copy(t).wait_send()
        return 0

    lax.fori_loop(0, npair, core_done, 0)
    for way in range(2):
        for xs in range(2):
            for f in range(1, me.half + (way + xs) % 2):
                hop_copy(way, xs, f).wait_send()
    x_copy.wait_send()
    next_copy.wait_send()
    for make in (out_copy, r_copies(0), r_copies(1)):
        over_peers(make, wait)
    own_out.wait()
    for i in range(2):
        for s in range(2):
            own_r(i, s).wait()


def shards(queries, keys, values, outputs, cotangent, lengths):
    nctx, nh = lax.axis_size("ctx"), lax.axis_size("head")
    tok = queries.shape[1]
    gw = queries.shape[2] // nh
    bl = tok * nh
    nhead = queries.shape[2] // HD
    dims = (nctx, nh, tok, gw, bl, nhead)
    npair = nctx // 2
    rows = gw // HD * bl
    hbm = pl.BlockSpec(memory_space=pl.ANY)
    vmem = pl.BlockSpec(memory_space=pltpu.VMEM)
    dma = pltpu.SemaphoreType.DMA
    space = pltpu.VMEM
    f32, b16 = jnp.float32, jnp.bfloat16
    shape = jax.ShapeDtypeStruct
    hops = nctx // 8
    return pl.pallas_call(
        functools.partial(kernel, dims),
        out_shape=(
            shape((2, tok, nh * gw), b16),
            shape((2, tok, nh * HD), f32),
            shape((2, tok, nh * HD), f32),
        ),
        in_specs=[vmem, hbm, hbm, hbm, vmem, vmem],
        out_specs=[hbm] * 3,
        scratch_shapes=[
            space((2, nh, tok, gw), b16),
            space((2, nh, tok, gw), b16),
            space((2, nh, tok, HD), f32),
            space((2, nctx, bl, HD), b16),
            space((2, 2, bl, HD), b16),
            space((2, tok, HD), f32),
            space((2, rows, HD), b16),
            space((2, rows, HD), b16),
            space((2, 1, rows), f32),
            space((HD, bl), f32),
            space((2 * npair + 1, 2 * bl, rows), f32),
            space((2, 8, rows), f32),
            space((2, 8, rows), f32),
            space((2, 1, rows), f32),
            space((2, 1, rows), f32),
            space((2, HD, rows), f32),
            space((2 * bl, rows), b16),
            space((2 * bl, rows), b16),
            space((npair, 2, 2, bl, HD), f32),
            space((2, 2 * bl, HD), f32),
            space((2, bl, gw), b16),
            space((npair, 2, bl, HD), f32),
            space((npair, 2, bl, HD), f32),
            space((2, 2, hops, 2, bl, HD), f32),
            space((2, bl, HD), f32),
            space((2, QMOST, HD), f32),
            space((2, 2, bl, HD), f32),
            dma((4, nh)),
            dma((4, nh)),
            dma((nh,)),
            dma((nh,)),
            dma((nh,)),
            dma((nh,)),
            dma((nh,)),
            dma((nh,)),
            dma((4, nctx)),
            dma((nctx,)),
            dma,
            dma,
            dma((npair,)),
            dma((npair,)),
            dma((2, 2, hops)),
            dma((2, 2, hops)),
            dma,
            dma,
            dma,
            dma,
            dma((nh,)),
            dma((nh,)),
            dma((4, nh)),
            dma((4, nh)),
            dma((7,)),
        ],
        compiler_params=pltpu.CompilerParams(
            collective_id=0, has_side_effects=True, vmem_limit_bytes=60 * 2**20
        ),
        name="attention_backward",
    )(lengths.reshape(1, -1), queries, keys, values, outputs, cotangent)


def solution(mesh):
    spec = P(None, ("ctx", "head"), None)
    return jax.shard_map(
        shards,
        mesh=mesh,
        in_specs=(spec,) * 5 + (P(),),
        out_specs=(spec,) * 3,
        check_vma=False,
    )
```

```python
import functools
import math

import jax
import jax.numpy as jnp
from jax import lax
from jax.experimental import pallas as pl
from jax.experimental.pallas import tpu as pltpu
from jax.sharding import PartitionSpec as P

HD = 128
NEG_FILL = -1e30
QMOST = 32
SCALE = HD ** (-0.5)
EXP2_SCALE = SCALE * math.log2(math.e)
MESH = pl.DeviceIdType.MESH
CHUNK = 256
LAG = 2
UNROLL = 4
WIDE = 2


def remote(src, dst, send_sem, recv_sem, device):
    return pltpu.make_async_remote_copy(
        src_ref=src,
        dst_ref=dst,
        send_sem=send_sem,
        recv_sem=recv_sem,
        device_id=device,
        device_id_type=MESH,
    )


class Place:
    def __init__(self, ctx_count, head_count):
        self.nctx = ctx_count
        self.nh = head_count
        self.nz = ctx_count // 4
        self.half = self.nz // 2
        self.npair = ctx_count // 2
        self.ctx = lax.axis_index("ctx")
        self.h = lax.axis_index("head")
        self.c = lax.rem(self.ctx, 2)
        self.z = lax.rem(self.ctx // 2, self.nz)
        self.xh = self.ctx // (2 * self.nz)

    def zmod(self, z):
        return lax.rem(z + self.nz, self.nz)

    def block(self, xh, z, c):
        return (xh * self.nz + self.zmod(z)) * 2 + c

    def pair(self, xh, z):
        return xh * self.nz + self.zmod(z)

    def dev(self, xh, z, c):
        return (self.block(xh, z, c), self.h)

    def z_up(self):
        return self.dev(self.xh, self.z + 1, self.c)

    def z_down(self):
        return self.dev(self.xh, self.z - 1, self.c)

    def across(self):
        return self.block(1 - self.xh, self.z, self.c)

    def sibling(self):
        return self.dev(self.xh, self.z, 1 - self.c)

    def ctx_next(self):
        return (lax.rem(self.ctx + 1, self.nctx), self.h)

    def ctx_prev(self):
        return (lax.rem(self.ctx + self.nctx - 1, self.nctx), self.h)

    def head_peer(self, d):
        return lax.rem(self.h + d, self.nh)

    def far(self, q):
        return self.half - q // 4

    def way(self, q):
        return q % 2

    def xs(self, q):
        return (q // 2 + q) % 2

    def reach(self, q):
        return self.half - (self.way(q) + self.xs(q) + 1) % 2

    def z_of(self, q):
        return self.z + self.far(q) * (1 - 2 * self.way(q))

    def pair_of(self, q):
        return self.pair(self.xs(q), self.z_of(q))

    def block_of(self, q, c):
        return self.block(self.xs(q), self.z_of(q), c)

    def barrier(self):
        barrier = pltpu.get_barrier_semaphore()

        def greet(d, _):
            pl.semaphore_signal(
                barrier, inc=1, device_id=(self.ctx, self.head_peer(d)), device_id_type=MESH
            )
            return 0

        def greet_across(d, _):
            device = (self.across(), self.head_peer(d))
            pl.semaphore_signal(barrier, inc=1, device_id=device, device_id_type=MESH)
            return 0

        lax.fori_loop(1, self.nh, greet, 0)
        lax.fori_loop(0, self.nh, greet_across, 0)
        near = (
            self.z_up(),
            self.z_down(),
            self.sibling(),
            self.ctx_next(),
            self.ctx_prev(),
        )
        for device in near:
            pl.semaphore_signal(barrier, inc=1, device_id=device, device_id_type=MESH)
        pl.semaphore_wait(barrier, 2 * self.nh - 1 + len(near))


def nt_dot(a, b):
    return lax.dot_general(a, b, (((1,), (1,)), ((), ())), preferred_element_type=jnp.float32)


def nn_dot(a, b):
    return jnp.dot(a, b, preferred_element_type=jnp.float32)


def by_sublane(x):
    return x.reshape(x.shape[0] // 8, 8, x.shape[1])


def kernel(
    dims,
    len_ref,
    q_ref,
    k_ref,
    v_ref,
    o_ref,
    c_ref,
    gq,
    gk,
    gv,
    q_in,
    c_in,
    d_in,
    kvd,
    kvq,
    delta,
    qs,
    cs,
    dd,
    turn,
    weights,
    peak,
    total,
    final_max,
    inverse,
    dqt,
    low_p,
    low_s,
    dkv,
    dx,
    dq,
    from_core,
    sums,
    low_sums,
    chain,
    low_chain,
    from_next,
    result,
    final,
    landed,
    owned,
    o_in,
    c_near,
    kv_send,
    kv_recv,
    kx_send,
    kx_recv,
    q_send,
    q_recv,
    c_send,
    c_recv,
    d_send,
    d_recv,
    g_send,
    g_recv,
    t_send,
    t_recv,
    core_send,
    core_recv,
    hop_send,
    hop_recv,
    n_send,
    n_recv,
    o_send,
    o_recv,
    r_send,
    r_recv,
    f_send,
    f_recv,
    local_sem,
):
    nctx, nh, tok, gw, bl, nhead = dims
    me = Place(nctx, nh)
    npair = me.npair
    last = 4 * me.half + 1
    group = gw // HD
    rows = group * bl
    tile = 2 * bl
    own_pair = me.ctx // 2
    chunks = [pl.ds(r * CHUNK, CHUNK) for r in range(rows // CHUNK)]
    fetch_o = pltpu.make_async_copy(o_ref, o_in, local_sem.at[7])
    fetch_c = pltpu.make_async_copy(c_ref, c_near, local_sem.at[8])
    fetch_o.start()
    fetch_c.start()
    me.barrier()

    def rows_of(p):
        return pl.ds(pl.multiple_of(p * tok, tok), tok)

    own_rows = rows_of(me.h)

    def head_slice(ref, p, width):
        return ref.at[:, :, pl.ds(pl.multiple_of(p * width, width), width)]

    def over_peers(make, act, across=False):
        def step(d, _):
            p = me.head_peer(d)
            made = make(d, p, (me.across() if across else me.ctx, p))
            for copy in made if isinstance(made, list) else [made]:
                act(copy)
            return 0

        lax.fori_loop(0 if across else 1, nh, step, 0)

    def start(copy):
        copy.start()

    def wait(copy):
        copy.wait()

    def wait_send(copy):
        copy.wait_send()

    def wait_recv(copy):
        copy.wait_recv()

    kv_ref = (k_ref, v_ref)

    def kv_target(i, j):
        return kvq.at[i, 1, own_rows] if j else kvd.at[i, me.ctx, own_rows]

    def kv_copies(i, j):
        def made(d, p, device):
            cols = pl.ds(pl.multiple_of(p * HD, HD), HD)
            return remote(
                kv_ref[i].at[j, :, cols],
                kv_target(i, j),
                kv_send.at[2 * i + j, d],
                kv_recv.at[2 * i + j, d],
                device,
            )

        return made

    def kx_copies(i):
        def made(d, p, device):
            cols = pl.ds(pl.multiple_of(p * HD, HD), HD)
            return remote(
                kv_ref[i].at[0, :, cols], kv_target(i, 0), kx_send.at[i, d], kx_recv.at[i, d], device
            )

        return made

    def q_copy(d, p, device):
        return remote(
            head_slice(q_ref, p, gw), q_in.at[:, me.h], q_send.at[d], q_recv.at[d], device
        )

    def c_copy(d, p, device):
        return remote(
            head_slice(c_ref, p, gw), c_in.at[:, me.h], c_send.at[d], c_recv.at[d], device
        )

    def d_copy(d, p, device):
        return remote(delta, d_in.at[:, me.h], d_send.at[d], d_recv.at[d], device)

    for i in range(2):
        over_peers(kv_copies(i, 0), start)
        over_peers(kx_copies(i), start, True)
    own_cols = pl.ds(pl.multiple_of(me.h * HD, HD), HD)
    locals_ = [
        pltpu.make_async_copy(kv_ref[i].at[j, :, own_cols], kv_target(i, j), local_sem.at[2 * i + j])
        for i in range(2)
        for j in range(2)
    ]
    own_q = pltpu.make_async_copy(head_slice(q_ref, me.h, gw), q_in.at[:, me.h], local_sem.at[4])
    own_c = pltpu.make_async_copy(head_slice(c_ref, me.h, gw), c_in.at[:, me.h], local_sem.at[5])
    for copy in locals_:
        copy.start()
    over_peers(q_copy, start)
    for i in range(2):
        over_peers(kv_copies(i, 1), start)
    over_peers(c_copy, start)
    own_q.start()
    own_c.start()

    fetch_o.wait()
    fetch_c.wait()
    lanes = lax.broadcasted_iota(jnp.int32, (2, tok, HD), 2)

    def some_heads(j, acc):
        for u in range(UNROLL):
            at = pl.ds(pl.multiple_of((j * UNROLL + u) * HD, HD), HD)
            prod = c_near[:, :, at].astype(jnp.float32) * o_in[:, :, at].astype(jnp.float32)
            part = jnp.sum(prod, axis=-1, keepdims=True)
            acc = jnp.where(lanes == j * UNROLL + u, part, acc)
        return acc

    delta[...] = lax.fori_loop(
        0, nhead // UNROLL, some_heads, jnp.zeros((2, tok, HD), jnp.float32)
    )
    over_peers(d_copy, start)
    own_delta = pltpu.make_async_copy(delta, d_in.at[:, me.h], local_sem.at[6])
    own_delta.start()

    def gather_copy(i, b, kind, device):
        return remote(
            kvd.at[i, b], kvd.at[i, b], g_send.at[i, kind, b], g_recv.at[i, b], device
        )

    sent = []

    def send_block(i, b, kind, device):
        copy = gather_copy(i, b, kind, device)
        copy.start()
        sent.append(copy)

    def arrived(i, b):
        gather_copy(i, b, 0, me.sibling()).wait_recv()

    tail = pl.ds(bl - QMOST, QMOST)
    tail_copy = remote(kvq.at[:, 1, tail], kvq.at[:, 0, tail], t_send, t_recv, me.ctx_next())

    def gather_own(i, b):
        send_block(i, b, 0, me.z_up())
        send_block(i, b, 1, me.z_down())

    def gather_step(f):
        qs_at = [q for q in range(last - 1, 1, -1) if me.far(q) == f]
        for i in range(2):
            for q in qs_at:
                b = me.block_of(q, me.c)
                arrived(i, b)
                if f < me.reach(q):
                    way = me.way(q)
                    send_block(i, b, way, me.z_down() if way == 0 else me.z_up())
                send_block(i, b, 2, me.sibling())

    for i in range(2):
        locals_[2 * i].wait()
        over_peers(kv_copies(i, 0), wait_recv)
        gather_own(i, me.ctx)
        over_peers(kx_copies(i), wait_recv, True)
        gather_own(i, me.across())
        send_block(i, me.ctx, 2, me.sibling())
        send_block(i, me.across(), 2, me.sibling())

    count = len_ref.shape[1]
    lens = jnp.broadcast_to(len_ref[...].astype(jnp.float32), (8, count)).astype(jnp.bfloat16)
    i0 = lax.broadcasted_iota(jnp.int32, (count, count), 0)
    i1 = lax.broadcasted_iota(jnp.int32, (count, count), 1)
    before = jnp.where(i0 < i1, 1.0, 0.0).astype(jnp.bfloat16)
    after = jnp.where(i1 < i0, 1.0, 0.0).astype(jnp.bfloat16)
    starts_row = nn_dot(lens, before)[0:1, :]
    starts_col = nt_dot(after, lens)[:, 0:1]
    row_at = lax.broadcasted_iota(jnp.int32, (1, CHUNK), 1) % bl
    key_at = lax.broadcasted_iota(jnp.int32, (tile, 1), 0) - bl
    row_off = (row_at + me.ctx * bl).astype(jnp.float32)
    key_off = (key_at + me.ctx * bl).astype(jnp.float32)
    row_seg = jnp.sum(jnp.where(starts_col <= row_off, 1.0, 0.0), axis=0, keepdims=True)
    key_seg = jnp.sum(jnp.where(starts_row <= key_off, 1.0, 0.0), axis=1, keepdims=True)
    question_mask = (key_at <= row_at) & (key_seg == row_seg)
    doc_key = lax.broadcasted_iota(jnp.int32, (tile, 1), 0) + (own_pair * 2 - me.ctx) * bl
    doc_mask = doc_key <= row_at

    peak[...] = jnp.full(peak.shape, NEG_FILL, jnp.float32)
    total[...] = jnp.zeros(total.shape, jnp.float32)
    dqt[...] = jnp.zeros(dqt.shape, jnp.float32)

    def doc_kv(i, t):
        return kvd[i, pl.ds(2 * t, 2)].reshape(tile, HD)

    def question_kv(i):
        at = lax.broadcasted_iota(jnp.int32, (bl, HD), 0)
        prev = jnp.where(at >= bl - QMOST, kvq[i, 0].astype(jnp.float32), 0.0)
        return jnp.concatenate([prev.astype(jnp.bfloat16), kvq[i, 1]], axis=0)

    def scores_of(s, keys, mask, cols):
        scores = nt_dot(keys, qs[s, cols, :])
        return scores if mask is None else jnp.where(mask, scores, NEG_FILL)

    def peak_sweep(s, keys, mask):
        for cols in chunks:
            scores = by_sublane(scores_of(s, keys, mask, cols))
            peak[s, :, cols] = jnp.maximum(peak[s, :, cols], jnp.max(scores, axis=0))

    def weight_sweep(s, slot, keys, mask):
        for cols in chunks:
            scores = scores_of(s, keys, mask, cols)
            part = jnp.exp2((scores - final_max[s, 0:1, cols]) * EXP2_SCALE)
            weights[slot, :, cols] = part
            total[s, :, cols] = total[s, :, cols] + jnp.sum(by_sublane(part), axis=0)

    def on_pair(t, question, doc):
        question(None)

        @pl.when(t < own_pair)
        def _():
            doc(None)

        @pl.when(t == own_pair)
        def _():
            doc(doc_mask)

    gather_step(1)
    for i in range(2):
        locals_[2 * i + 1].wait()
        over_peers(kv_copies(i, 1), wait_recv)
    tail_copy.start()
    gather_step(2)

    own_q.wait()
    over_peers(q_copy, wait_recv)
    for s in range(2):
        for g in range(group):
            cols = slice(g * HD, (g + 1) * HD)
            qs[s, g * bl : (g + 1) * bl, :] = q_in[s, :, :, cols].reshape(bl, HD)

    def peaks(first, count):
        def step(i, _):
            q = first - i
            for i in range(2):
                arrived(i, me.block_of(q, 1 - me.c))
            t = me.pair_of(q)
            keys = doc_kv(0, t)
            on_pair(
                t, lambda m: peak_sweep(1, keys, m), lambda m: peak_sweep(0, keys, m)
            )
            return 0

        lax.fori_loop(0, count, step, 0)

    peaks(last, 2)
    tail_copy.wait_recv()
    peak_sweep(1, question_kv(0), question_mask)
    peaks(last - 2, 4)
    for f in range(3, me.half + 1):
        gather_step(f)
        peaks(last - 2 - 4 * (f - 2), 4)
    peaks(3, 2)

    for s in range(2):
        final_max[s] = jnp.max(peak[s], axis=0, keepdims=True)

    def weigh(t, _):
        keys = doc_kv(0, t)
        on_pair(
            t,
            lambda m: weight_sweep(1, npair + t, keys, m),
            lambda m: weight_sweep(0, t, keys, m),
        )
        return 0

    lax.fori_loop(0, npair, weigh, 0)
    weight_sweep(1, 2 * npair, question_kv(0), question_mask)
    for s in range(2):
        inverse[s] = 1.0 / jnp.sum(total[s], axis=0, keepdims=True)

    own_c.wait()
    own_delta.wait()
    over_peers(c_copy, wait_recv)
    over_peers(d_copy, wait_recv)
    for s in range(2):
        for g in range(group):
            cols = slice(g * HD, (g + 1) * HD)
            cs[s, g * bl : (g + 1) * bl, :] = c_in[s, :, :, cols].reshape(bl, HD)
        turn[...] = jnp.transpose(d_in[s].reshape(bl, HD))
        mine = turn[pl.ds(pl.multiple_of(me.h * group, group), group), :]
        for g in range(group):
            dd[s, 0:1, g * bl : (g + 1) * bl] = mine[g : g + 1, :]

    def backward(s, slot, keys, values):
        for cols in chunks:
            prob = weights[slot, :, cols] * inverse[s, 0:1, cols]
            d_prob = nt_dot(values, cs[s, cols, :])
            low_p[:, cols] = prob.astype(jnp.bfloat16)
            low_s[:, cols] = (prob * (d_prob - dd[s, 0:1, cols])).astype(jnp.bfloat16)
        d_value = nn_dot(low_p[...], cs[s])
        d_key = nn_dot(low_s[...], qs[s])
        keys_t = jnp.transpose(keys.astype(jnp.float32)).astype(jnp.bfloat16)
        dqt[s] += nn_dot(keys_t, low_s[...])
        return d_key, d_value

    def put(t, i, value, add):
        for c in range(2):
            part = value[c * bl : (c + 1) * bl]
            dkv[t, i, c] = dkv[t, i, c] + part if add else part

    def core_copy(t):
        return remote(
            dkv.at[t, :, 1 - me.c],
            from_core.at[t],
            core_send.at[t],
            core_recv.at[t],
            me.sibling(),
        )

    def hop_copy(way, xs, f, wide):
        source = sums if wide else low_sums
        return remote(
            source.at[me.pair(xs, me.z + f * (1 - 2 * way))],
            chain.at[way, xs] if wide else low_chain.at[way, xs, f - 1],
            hop_send.at[way, xs, f - 1],
            hop_recv.at[way, xs, f - 1],
            me.dev(me.xh, me.z + 1 - 2 * way, me.c),
        )

    def serve(q):
        f, way, xs, t = me.far(q), me.way(q), me.xs(q), me.pair_of(q)
        core_copy(t).wait_recv()
        sums[t] = dkv[t, :, me.c] + from_core[t]
        met = (f > 0) & (f < me.reach(q))

        @pl.when(met & (f + 1 == WIDE))
        def _():
            hop_copy(way, xs, f + 1, True).wait_recv()
            sums[t] = sums[t] + chain[way, xs]

        @pl.when(met & (f + 1 != WIDE))
        def _():
            hop_copy(way, xs, f + 1, False).wait_recv()
            sums[t] = sums[t] + low_chain[way, xs, f].astype(jnp.float32)

        @pl.when(f == WIDE)
        def _():
            hop_copy(way, xs, f, True).start()

        @pl.when((f > 0) & (f != WIDE))
        def _():
            low_sums[t] = sums[t].astype(jnp.bfloat16)
            hop_copy(way, xs, f, False).start()

    def backward_pair(n, _):
        q = n + 2
        t = me.pair_of(q)
        keys, values = doc_kv(0, t), doc_kv(1, t)
        for i, value in enumerate(backward(1, npair + t, keys, values)):
            put(t, i, value, False)

        @pl.when(t <= own_pair)
        def _():
            for i, value in enumerate(backward(0, t, keys, values)):
                put(t, i, value, True)

        core_copy(t).start()

        @pl.when(n >= LAG)
        def _():
            serve(q - LAG)

        return 0

    lax.fori_loop(0, npair, backward_pair, 0)
    d_key, d_value = backward(1, 2 * npair, question_kv(0), question_kv(1))
    dx[0] = d_key
    dx[1] = d_value
    next_copy = remote(dx.at[:, tail], from_next, n_send, n_recv, me.ctx_prev())
    next_copy.start()

    for s in range(2):
        for g in range(group):
            part = jnp.transpose(dqt[s, :, g * bl : (g + 1) * bl])
            dq[s, :, g * HD : (g + 1) * HD] = (part * SCALE).astype(jnp.bfloat16)

    q_cols = pl.ds(pl.multiple_of(me.h * gw, gw), gw)

    def out_copy(d, p, device):
        return remote(
            dq.at[:, rows_of(p)], gq.at[:, :, q_cols], o_send.at[d], o_recv.at[d], device
        )

    own_out = pltpu.make_async_copy(dq.at[:, own_rows], gq.at[:, :, q_cols], local_sem.at[4])

    def serve_rest(n, _):
        serve(n + 2)
        return 0

    lax.fori_loop(npair - LAG, npair, serve_rest, 0)

    over_peers(out_copy, start)
    own_out.start()
    next_copy.wait_recv()
    for i in range(2):
        factor = SCALE if i == 0 else 1.0
        result[i, 0 : bl - QMOST] = dx[i, bl : 2 * bl - QMOST] * factor
        result[i, bl - QMOST : bl] = (
            dx[i, 2 * bl - QMOST : 2 * bl] + from_next[i]
        ) * factor

    def r_copies(d, p, device):
        return [
            remote(
                result.at[i, rows_of(p)],
                (gk, gv)[i].at[1, :, own_cols],
                r_send.at[i, d],
                r_recv.at[i, d],
                device,
            )
            for i in range(2)
        ]

    own_r = [
        pltpu.make_async_copy(
            result.at[i, own_rows], (gk, gv)[i].at[1, :, own_cols], local_sem.at[i]
        )
        for i in range(2)
    ]
    over_peers(r_copies, start)
    for copy in own_r:
        copy.start()

    def final_copies(kind):
        def made(d, p, device):
            return [
                remote(
                    final.at[kind, i, rows_of(p)],
                    landed.at[kind, i, me.h],
                    f_send.at[kind, i, d],
                    f_recv.at[kind, i, d],
                    device,
                )
                for i in range(2)
            ]

        return made

    for way in range(2):
        for xs in range(2):
            hop_copy(way, xs, 1, False).wait_recv()
    for kind in (1, 0):
        xs = me.xh if kind == 0 else 1 - me.xh
        t = me.pair(xs, me.z)
        for i in range(2):
            factor = SCALE if i == 0 else 1.0
            final[kind, i] = (
                sums[t, i]
                + low_chain[0, xs, 0, i].astype(jnp.float32)
                + low_chain[1, xs, 0, i].astype(jnp.float32)
            ) * factor
        over_peers(final_copies(kind), start, kind == 1)
    for i in range(2):
        landed[0, i, me.h] = final[0, i, own_rows]
    over_peers(final_copies(0), wait_recv)
    over_peers(final_copies(1), wait_recv, True)
    for i in range(2):
        for h in range(nh):
            owned[i, :, h * HD : (h + 1) * HD] = landed[0, i, h] + landed[1, i, h]
    last_out = [
        pltpu.make_async_copy(owned.at[i], (gk, gv)[i].at[0], local_sem.at[2 + i])
        for i in range(2)
    ]
    for copy in last_out:
        copy.start()

    for copy in sent:
        copy.wait_send()
    for i in range(2):
        over_peers(kx_copies(i), wait_send, True)
        for j in range(2):
            over_peers(kv_copies(i, j), wait_send)
    for make in (q_copy, c_copy, d_copy, final_copies(0)):
        over_peers(make, wait_send)
    over_peers(final_copies(1), wait_send, True)
    tail_copy.wait_send()

    def core_done(t, _):
        core_copy(t).wait_send()
        return 0

    lax.fori_loop(0, npair, core_done, 0)
    for way in range(2):
        for xs in range(2):
            for f in range(1, me.half + (way + xs) % 2):
                hop_copy(way, xs, f, f == WIDE).wait_send()
    next_copy.wait_send()
    over_peers(out_copy, wait)
    over_peers(r_copies, wait)
    own_out.wait()
    for copy in own_r + last_out:
        copy.wait()


def place_results(*refs):
    sources, targets, held, sem = refs[:3], refs[3:6], refs[6:9], refs[9]
    reads = [pltpu.make_async_copy(sources[i], held[i], sem.at[0, i]) for i in range(3)]
    writes = [pltpu.make_async_copy(held[i], targets[i], sem.at[1, i]) for i in range(3)]
    for copy in reads:
        copy.start()
    for i in range(3):
        reads[i].wait()
        writes[i].start()
    for copy in writes:
        copy.wait()


def shards(queries, keys, values, outputs, cotangent, lengths):
    nctx, nh = lax.axis_size("ctx"), lax.axis_size("head")
    tok = queries.shape[1]
    gw = queries.shape[2] // nh
    bl = tok * nh
    nhead = queries.shape[2] // HD
    dims = (nctx, nh, tok, gw, bl, nhead)
    npair = nctx // 2
    rows = gw // HD * bl
    hbm = pl.BlockSpec(memory_space=pl.ANY)
    vmem = pl.BlockSpec(memory_space=pltpu.VMEM)
    dma = pltpu.SemaphoreType.DMA
    space = pltpu.VMEM
    f32, b16 = jnp.float32, jnp.bfloat16
    shape = jax.ShapeDtypeStruct
    hops = nctx // 8
    made = (
        shape((2, tok, nh * gw), b16),
        shape((2, tok, nh * HD), f32),
        shape((2, tok, nh * HD), f32),
    )
    results = pl.pallas_call(
        functools.partial(kernel, dims),
        out_shape=made,
        in_specs=[vmem, hbm, hbm, hbm, hbm, hbm],
        out_specs=[hbm] * 3,
        scratch_shapes=[
            space((2, nh, tok, gw), b16),
            space((2, nh, tok, gw), b16),
            space((2, nh, tok, HD), f32),
            space((2, nctx, bl, HD), b16),
            space((2, 2, bl, HD), b16),
            space((2, tok, HD), f32),
            space((2, rows, HD), b16),
            space((2, rows, HD), b16),
            space((2, 1, rows), f32),
            space((HD, bl), f32),
            space((2 * npair + 1, 2 * bl, rows), f32),
            space((2, 8, rows), f32),
            space((2, 8, rows), f32),
            space((2, 1, rows), f32),
            space((2, 1, rows), f32),
            space((2, HD, rows), f32),
            space((2 * bl, rows), b16),
            space((2 * bl, rows), b16),
            space((npair, 2, 2, bl, HD), f32),
            space((2, 2 * bl, HD), f32),
            space((2, bl, gw), b16),
            space((npair, 2, bl, HD), f32),
            space((npair, 2, bl, HD), f32),
            space((npair, 2, bl, HD), b16),
            space((2, 2, 2, bl, HD), f32),
            space((2, 2, hops, 2, bl, HD), b16),
            space((2, QMOST, HD), f32),
            space((2, bl, HD), f32),
            space((2, 2, bl, HD), f32),
            space((2, 2, nh, tok, HD), f32),
            space((2, tok, nh * HD), f32),
            space((2, tok, nh * gw), b16),
            space((2, tok, nh * gw), b16),
            dma((4, nh)),
            dma((4, nh)),
            dma((2, nh)),
            dma((2, nh)),
            dma((nh,)),
            dma((nh,)),
            dma((nh,)),
            dma((nh,)),
            dma((nh,)),
            dma((nh,)),
            dma((2, 3, nctx)),
            dma((2, nctx)),
            dma,
            dma,
            dma((npair,)),
            dma((npair,)),
            dma((2, 2, hops)),
            dma((2, 2, hops)),
            dma,
            dma,
            dma((nh,)),
            dma((nh,)),
            dma((2, nh)),
            dma((2, nh)),
            dma((2, 2, nh)),
            dma((2, 2, nh)),
            dma((9,)),
        ],
        compiler_params=pltpu.CompilerParams(
            collective_id=0, has_side_effects=True, vmem_limit_bytes=60 * 2**20
        ),
        name="attention_backward",
    )(lengths.reshape(1, -1), queries, keys, values, outputs, cotangent)
    return pl.pallas_call(
        place_results,
        out_shape=made,
        in_specs=[hbm] * 3,
        out_specs=[hbm] * 3,
        scratch_shapes=[space(m.shape, m.dtype) for m in made] + [dma((2, 3))],
        name="place_results",
    )(*results)


def solution(mesh):
    spec = P(None, ("ctx", "head"), None)
    return jax.shard_map(
        shards,
        mesh=mesh,
        in_specs=(spec,) * 5 + (P(),),
        out_specs=(spec,) * 3,
        check_vma=False,
    )
```

```python
import functools
import math

import jax
import jax.numpy as jnp
from jax import lax
from jax.experimental import pallas as pl
from jax.experimental.pallas import tpu as pltpu
from jax.sharding import PartitionSpec as P

HD = 128
NEG_FILL = -1e30
QMOST = 32
SCALE = HD ** (-0.5)
EXP2_SCALE = SCALE * math.log2(math.e)
MESH = pl.DeviceIdType.MESH
LAG = 2
UNROLL = 4


def remote(src, dst, send_sem, recv_sem, device):
    return pltpu.make_async_remote_copy(
        src_ref=src,
        dst_ref=dst,
        send_sem=send_sem,
        recv_sem=recv_sem,
        device_id=device,
        device_id_type=MESH,
    )


class Place:
    def __init__(self, ctx_count, head_count):
        self.nctx = ctx_count
        self.nh = head_count
        self.nz = ctx_count // 4
        self.half = self.nz // 2
        self.npair = ctx_count // 2
        self.ctx = lax.axis_index("ctx")
        self.h = lax.axis_index("head")
        self.c = lax.rem(self.ctx, 2)
        self.z = lax.rem(self.ctx // 2, self.nz)
        self.xh = self.ctx // (2 * self.nz)

    def zmod(self, z):
        return lax.rem(z + self.nz, self.nz)

    def block(self, xh, z, c):
        return (xh * self.nz + self.zmod(z)) * 2 + c

    def pair(self, xh, z):
        return xh * self.nz + self.zmod(z)

    def dev(self, xh, z, c):
        return (self.block(xh, z, c), self.h)

    def z_up(self):
        return self.dev(self.xh, self.z + 1, self.c)

    def z_down(self):
        return self.dev(self.xh, self.z - 1, self.c)

    def across(self):
        return self.block(1 - self.xh, self.z, self.c)

    def sibling(self):
        return self.dev(self.xh, self.z, 1 - self.c)

    def ctx_next(self):
        return (lax.rem(self.ctx + 1, self.nctx), self.h)

    def ctx_prev(self):
        return (lax.rem(self.ctx + self.nctx - 1, self.nctx), self.h)

    def head_peer(self, d):
        return lax.rem(self.h + d, self.nh)

    def far(self, q):
        return self.half - q // 4

    def way(self, q):
        return q % 2

    def xs(self, q):
        return (q // 2 + q) % 2

    def reach(self, q):
        return self.half - (self.way(q) + self.xs(q) + 1) % 2

    def z_of(self, q):
        return self.z + self.far(q) * (1 - 2 * self.way(q))

    def pair_of(self, q):
        return self.pair(self.xs(q), self.z_of(q))

    def block_of(self, q, c):
        return self.block(self.xs(q), self.z_of(q), c)

    def barrier(self):
        barrier = pltpu.get_barrier_semaphore()

        def greet(d, _):
            pl.semaphore_signal(
                barrier, inc=1, device_id=(self.ctx, self.head_peer(d)), device_id_type=MESH
            )
            return 0

        def greet_across(d, _):
            device = (self.across(), self.head_peer(d))
            pl.semaphore_signal(barrier, inc=1, device_id=device, device_id_type=MESH)
            return 0

        lax.fori_loop(1, self.nh, greet, 0)
        lax.fori_loop(0, self.nh, greet_across, 0)
        near = (
            self.z_up(),
            self.z_down(),
            self.sibling(),
            self.ctx_next(),
            self.ctx_prev(),
        )
        for device in near:
            pl.semaphore_signal(barrier, inc=1, device_id=device, device_id_type=MESH)
        pl.semaphore_wait(barrier, 2 * self.nh - 1 + len(near))


def nt_dot(a, b):
    return lax.dot_general(a, b, (((1,), (1,)), ((), ())), preferred_element_type=jnp.float32)


def nn_dot(a, b):
    return jnp.dot(a, b, preferred_element_type=jnp.float32)


def by_sublane(x):
    return x.reshape(x.shape[0] // 8, 8, x.shape[1])


def kernel(
    dims,
    len_ref,
    q_ref,
    k_ref,
    v_ref,
    o_ref,
    c_ref,
    gq,
    gk,
    gv,
    q_in,
    c_in,
    d_in,
    kvd,
    kvq,
    delta,
    delta_t,
    qs,
    cs,
    dd,
    turn,
    weights,
    peak,
    total,
    first_max,
    final_max,
    inverse,
    dqt,
    keys_t,
    low_p,
    low_s,
    dkv,
    dx,
    dq,
    from_core,
    sums,
    low_sums,
    chain,
    from_next,
    result,
    final,
    landed,
    owned,
    o_in,
    c_near,
    kv_send,
    kv_recv,
    q_send,
    q_recv,
    c_send,
    c_recv,
    d_send,
    d_recv,
    g_send,
    g_recv,
    s_send,
    s_recv,
    t_send,
    t_recv,
    core_send,
    core_recv,
    hop_send,
    hop_recv,
    n_send,
    n_recv,
    o_send,
    o_recv,
    r_send,
    r_recv,
    f_send,
    f_recv,
    local_sem,
):
    nctx, nh, tok, gw, bl, nhead = dims
    me = Place(nctx, nh)
    npair = me.npair
    last = 4 * me.half + 1
    group = gw // HD
    rows = group * bl
    tile = 2 * bl
    own_pair = me.ctx // 2
    chunk = min(256, rows)
    every = [pl.ds(r * chunk, chunk) for r in range(rows // chunk)]
    fetch_o = pltpu.make_async_copy(o_ref, o_in, local_sem.at[7])
    fetch_c = pltpu.make_async_copy(c_ref, c_near, local_sem.at[8])
    fetch_o.start()
    fetch_c.start()
    me.barrier()

    def rows_of(p):
        return pl.ds(pl.multiple_of(p * tok, tok), tok)

    own_rows = rows_of(me.h)

    def over_peers(make, act, across=False):
        def step(d, _):
            p = me.head_peer(d)
            made = make(d, p, (me.across() if across else me.ctx, p))
            for copy in made if isinstance(made, list) else [made]:
                act(copy)
            return 0

        lax.fori_loop(0 if across else 1, nh, step, 0)

    def sent_all(like, sem):
        remote(like, like, sem, sem, me.sibling()).wait_send()

    def received_all(like, sem):
        remote(like, like, sem, sem, me.sibling()).wait_recv()

    peers = nh - 1
    peer_rows = pl.ds(0, peers * tok)

    def start(copy):
        copy.start()

    kv_ref = (k_ref, v_ref)

    def kv_target(i, j):
        return kvq.at[i, 1, own_rows] if j else kvd.at[i, me.ctx, own_rows]

    def kv_copies(i, j):
        def made(d, p, device):
            cols = pl.ds(pl.multiple_of(p * HD, HD), HD)
            return remote(
                kv_ref[i].at[j, :, cols],
                kv_target(i, j),
                kv_send.at[i, j],
                kv_recv.at[i, j],
                device,
            )

        return made

    def kx_copies(i):
        def made(d, p, device):
            cols = pl.ds(pl.multiple_of(p * HD, HD), HD)
            return remote(
                kv_ref[i].at[0, :, cols], kv_target(i, 0), kv_send.at[i, 2], kv_recv.at[i, 2], device
            )

        return made

    def head_part(kind, ref, p):
        return ref.at[1 - kind, :, pl.ds(pl.multiple_of(p * gw, gw), gw)]

    def place_of(kind, ref):
        return ref.at[1 - kind, me.h]

    def row_copies(kind, source, target, send, recv):
        def made(d, p, device):
            return remote(
                head_part(kind, source, p),
                place_of(kind, target),
                send.at[kind],
                recv.at[kind],
                device,
            )

        return made

    def q_copies(kind):
        return row_copies(kind, q_ref, q_in, q_send, q_recv)

    def c_copies(kind):
        return row_copies(kind, c_ref, c_in, c_send, c_recv)

    def over_rows(copies, act):
        for kind in range(2):
            over_peers(copies(kind), act)

    def d_copy(d, p, device):
        return remote(
            delta_t.at[pl.ds(pl.multiple_of(p * group, group), group)],
            d_in.at[me.h],
            d_send,
            d_recv,
            device,
        )

    for i in range(2):
        over_peers(kv_copies(i, 0), start)
        over_peers(kx_copies(i), start, True)
    own_cols = pl.ds(pl.multiple_of(me.h * HD, HD), HD)
    locals_ = [
        pltpu.make_async_copy(kv_ref[i].at[j, :, own_cols], kv_target(i, j), local_sem.at[2 * i + j])
        for i in range(2)
        for j in range(2)
    ]
    own_q = [
        pltpu.make_async_copy(head_part(k, q_ref, me.h), place_of(k, q_in), local_sem.at[4 + k])
        for k in range(2)
    ]
    own_c = [
        pltpu.make_async_copy(head_part(k, c_ref, me.h), place_of(k, c_in), local_sem.at[9 + k])
        for k in range(2)
    ]
    for copy in locals_:
        copy.start()
    over_rows(q_copies, start)
    for i in range(2):
        over_peers(kv_copies(i, 1), start)
    for copy in own_q + own_c:
        copy.start()

    fetch_o.wait()
    fetch_c.wait()
    lanes = lax.broadcasted_iota(jnp.int32, (2, tok, HD), 2)

    def some_heads(j, acc):
        for u in range(UNROLL):
            at = pl.ds(pl.multiple_of((j * UNROLL + u) * HD, HD), HD)
            prod = c_near[:, :, at].astype(jnp.float32) * o_in[:, :, at].astype(jnp.float32)
            part = jnp.sum(prod, axis=-1, keepdims=True)
            acc = jnp.where(lanes == j * UNROLL + u, part, acc)
        return acc

    delta[...] = lax.fori_loop(
        0, nhead // UNROLL, some_heads, jnp.zeros((2, tok, HD), jnp.float32)
    )
    delta_t[:, 0 : 2 * tok] = jnp.transpose(delta[...].reshape(2 * tok, HD))
    over_peers(d_copy, start)
    d_in[me.h] = delta_t[pl.ds(pl.multiple_of(me.h * group, group), group)]

    n_sent = {"ring": 0, "core": 0}

    def ring_copy(i, b, f, way, xs, device):
        return remote(kvd.at[i, b], kvd.at[i, b], g_send, g_recv.at[i, f - 1, way, xs], device)

    def ring_send(i, b, f, way, xs):
        ring_copy(i, b, f, way, xs, me.z_down() if way == 0 else me.z_up()).start()
        n_sent["ring"] += 1

    def core_send_block(i, b, f):
        sem = s_recv.at[f if i == 0 else me.half + 1]
        remote(kvd.at[i, b], kvd.at[i, b], s_send, sem, me.sibling()).start()
        n_sent["core"] += 1

    tail = pl.ds(bl - QMOST, QMOST)
    tail_copy = remote(kvq.at[:, 1, tail], kvq.at[:, 0, tail], t_send, t_recv, me.ctx_next())

    def gather_own(i, b, xs):
        ring_send(i, b, 1, 1, xs)
        ring_send(i, b, 1, 0, xs)

    def gather_step(f, kv=(0, 1)):
        qs_at = [q for q in range(last - 1, 1, -1) if me.far(q) == f]
        for i in kv:
            for q in qs_at:
                b, way, xs = me.block_of(q, me.c), me.way(q), me.xs(q)
                ring_copy(i, b, f, way, xs, me.sibling()).wait_recv()
                if f < me.reach(q):
                    ring_send(i, b, f + 1, way, xs)
                core_send_block(i, b, f)

    for i in range(2):
        locals_[2 * i].wait()
        received_all(kvd.at[i, me.ctx, peer_rows], kv_recv.at[i, 0])
        gather_own(i, me.ctx, me.xh)
        received_all(kvd.at[i, me.across()], kv_recv.at[i, 2])
        gather_own(i, me.across(), 1 - me.xh)
        core_send_block(i, me.ctx, 0)
        core_send_block(i, me.across(), 0)

    count = len_ref.shape[1]
    lens = jnp.broadcast_to(len_ref[...].astype(jnp.float32), (8, count)).astype(jnp.bfloat16)
    i0 = lax.broadcasted_iota(jnp.int32, (count, count), 0)
    i1 = lax.broadcasted_iota(jnp.int32, (count, count), 1)
    before = jnp.where(i0 < i1, 1.0, 0.0).astype(jnp.bfloat16)
    after = jnp.where(i1 < i0, 1.0, 0.0).astype(jnp.bfloat16)
    starts_row = nn_dot(lens, before)[0:1, :]
    starts_col = nt_dot(after, lens)[:, 0:1]
    row_at = lax.broadcasted_iota(jnp.int32, (1, chunk), 1) % bl
    key_at = lax.broadcasted_iota(jnp.int32, (tile, 1), 0) - bl
    row_off = (row_at + me.ctx * bl).astype(jnp.float32)
    key_off = (key_at + me.ctx * bl).astype(jnp.float32)
    row_seg = jnp.sum(jnp.where(starts_col <= row_off, 1.0, 0.0), axis=0, keepdims=True)
    key_seg = jnp.sum(jnp.where(starts_row <= key_off, 1.0, 0.0), axis=1, keepdims=True)
    question_mask = (key_at <= row_at) & (key_seg == row_seg)
    doc_key = lax.broadcasted_iota(jnp.int32, (tile, 1), 0) + (own_pair * 2 - me.ctx) * bl
    doc_mask = doc_key <= row_at

    peak[...] = jnp.full(peak.shape, NEG_FILL, jnp.float32)
    total[...] = jnp.zeros(total.shape, jnp.float32)
    dqt[...] = jnp.zeros(dqt.shape, jnp.float32)

    def doc_kv(i, t):
        return kvd[i, pl.ds(2 * t, 2)].reshape(tile, HD)

    def question_kv(i):
        at = lax.broadcasted_iota(jnp.int32, (bl, HD), 0)
        prev = jnp.where(at >= bl - QMOST, kvq[i, 0].astype(jnp.float32), 0.0)
        return jnp.concatenate([prev.astype(jnp.bfloat16), kvq[i, 1]], axis=0)

    def scores_of(s, keys, mask, cols):
        scores = nt_dot(keys, qs[s, cols, :])
        return scores if mask is None else jnp.where(mask, scores, NEG_FILL)

    def peak_sweep(s, keys, mask, at):
        for cols in at:
            scores = by_sublane(scores_of(s, keys, mask, cols))
            peak[s, :, cols] = jnp.maximum(peak[s, :, cols], jnp.max(scores, axis=0))

    def weight_sweep(s, slot, keys, mask, at, known):
        for cols in at:
            scores = scores_of(s, keys, mask, cols)
            part = jnp.exp2((scores - known[s, 0:1, cols]) * EXP2_SCALE)
            weights[slot, :, cols] = part
            total[s, :, cols] = total[s, :, cols] + jnp.sum(by_sublane(part), axis=0)

    def on_pair(t, sweep):
        sweep(1, None, every)

        @pl.when(t < own_pair)
        def _():
            sweep(0, None, every)

        @pl.when(t == own_pair)
        def _():
            sweep(0, doc_mask, every)

    def sort_rows(target, source, s):
        for g in range(group):
            cols = slice(g * HD, (g + 1) * HD)
            target[s, g * bl : (g + 1) * bl, :] = source[s, :, :, cols].reshape(bl, HD)

    def peaks(f):
        count = 4 if 0 < f < me.half else 2
        received_all(kvd.at[0, pl.ds(0, count)], s_recv.at[f])

        def step(i, _):
            q = last - i if f == 0 else last - 2 - 4 * (f - 1) - i
            t = me.pair_of(q)
            keys = doc_kv(0, t)

            def sweep(s, mask, at):
                peak_sweep(s, keys, mask, at)

            on_pair(t, sweep)
            return 0

        lax.fori_loop(0, count, step, 0)

    def weigh(low, high, known):
        def step(q, _):
            t = me.pair_of(q)
            keys = doc_kv(0, t)

            def sweep(s, mask, at):
                weight_sweep(s, s * npair + t, keys, mask, at, known)

            on_pair(t, sweep)
            return 0

        lax.fori_loop(low, high, step, 0)

    gather_step(1)
    for i in range(2):
        locals_[2 * i + 1].wait()
        received_all(kvq.at[i, 1, peer_rows], kv_recv.at[i, 1])
    tail_copy.start()
    gather_step(2)
    for copy in own_q:
        copy.wait()
    for kind in range(2):
        received_all(q_in.at[kind, pl.ds(0, peers)], q_recv.at[kind])
    over_rows(c_copies, start)
    for s in range(2):
        sort_rows(qs, q_in, s)

    peaks(0)
    tail_copy.wait_recv()
    peak_sweep(1, question_kv(0), question_mask, every)
    for f in range(1, me.half - 1):
        if f + 1 > 2:
            gather_step(f + 1)
        peaks(f)
    for s in range(2):
        first_max[s] = jnp.max(peak[s], axis=0, keepdims=True)
    weight_sweep(1, 2 * npair, question_kv(0), question_mask, every, first_max)
    near = max(8, 4 * me.half - 4)
    weigh(near, last + 1, first_max)
    if me.half > 2:
        gather_step(me.half, (0,))
    weigh(8, near, first_max)
    if me.half > 2:
        gather_step(me.half, (1,))
    peaks(me.half - 1)
    peaks(me.half)
    for s in range(2):
        final_max[s] = jnp.max(peak[s], axis=0, keepdims=True)
        total[s] = total[s] * jnp.exp2((first_max[s] - final_max[s]) * EXP2_SCALE)
    weigh(2, 8, final_max)
    for s in range(2):
        whole = 1.0 / jnp.sum(total[s], axis=0, keepdims=True)
        nearer = whole * jnp.exp2((first_max[s] - final_max[s]) * EXP2_SCALE)
        inverse[0, s] = whole
        inverse[1, s] = nearer
        inverse[2, s] = nearer

    received_all(kvd.at[1, pl.ds(0, npair)], s_recv.at[me.half + 1])

    for copy in own_c:
        copy.wait()
    for kind in range(2):
        received_all(c_in.at[kind, pl.ds(0, peers)], c_recv.at[kind])
    received_all(d_in.at[pl.ds(0, peers)], d_recv)
    for s in range(2):
        sort_rows(cs, c_in, s)
        for j in range(nh):
            turn[:, j * tok : (j + 1) * tok] = d_in[j, :, s * tok : (s + 1) * tok]
        for g in range(group):
            dd[s, 0:1, g * bl : (g + 1) * bl] = turn[g : g + 1, :]

    def backward(s, slot, values, scale_at):
        for cols in every:
            prob = weights[slot, :, cols] * inverse[scale_at, s, 0:1, cols]
            d_prob = nt_dot(values, cs[s, cols, :])
            low_p[:, cols] = prob.astype(jnp.bfloat16)
            low_s[:, cols] = (prob * (d_prob - dd[s, 0:1, cols])).astype(jnp.bfloat16)
        d_value = nn_dot(low_p[...], cs[s])
        d_key = nn_dot(low_s[...], qs[s])
        dqt[s] += nn_dot(keys_t[...], low_s[...])
        return d_key, d_value

    def turn_keys(keys):
        keys_t[...] = jnp.transpose(keys.astype(jnp.float32)).astype(jnp.bfloat16)

    def put(t, i, value, add):
        for c in range(2):
            part = value[c * bl : (c + 1) * bl]
            dkv[t, i, c] = dkv[t, i, c] + part if add else part

    def core_copy(t):
        return remote(
            dkv.at[t, :, 1 - me.c],
            from_core.at[t],
            core_send,
            core_recv.at[t],
            me.sibling(),
        )

    def hop_copy(way, xs, f):
        return remote(
            low_sums.at[me.pair(xs, me.z + f * (1 - 2 * way))],
            chain.at[way, xs, f - 1],
            hop_send,
            hop_recv.at[way, xs, f - 1],
            me.dev(me.xh, me.z + 1 - 2 * way, me.c),
        )

    def serve(q):
        f, way, xs, t = me.far(q), me.way(q), me.xs(q), me.pair_of(q)
        core_copy(t).wait_recv()
        sums[t] = dkv[t, :, me.c] + from_core[t]

        @pl.when((f > 0) & (f < me.reach(q)))
        def _():
            hop_copy(way, xs, f + 1).wait_recv()
            sums[t] = sums[t] + chain[way, xs, f].astype(jnp.float32)

        @pl.when(f > 0)
        def _():
            low_sums[t] = sums[t].astype(jnp.bfloat16)
            hop_copy(way, xs, f).start()

    turn_keys(question_kv(0))
    dx[0], dx[1] = backward(1, 2 * npair, question_kv(1), 1)
    next_copy = remote(dx.at[:, tail], from_next, n_send, n_recv, me.ctx_prev())
    next_copy.start()

    def r_copies(d, p, device):
        return [
            remote(
                result.at[i, rows_of(p)],
                (gk, gv)[i].at[1, :, own_cols],
                r_send.at[i],
                r_recv.at[i],
                device,
            )
            for i in range(2)
        ]

    own_r = [
        pltpu.make_async_copy(
            result.at[i, own_rows], (gk, gv)[i].at[1, :, own_cols], local_sem.at[i]
        )
        for i in range(2)
    ]

    def send_questions():
        next_copy.wait_recv()
        for i in range(2):
            factor = SCALE if i == 0 else 1.0
            result[i, 0 : bl - QMOST] = dx[i, bl : 2 * bl - QMOST] * factor
            result[i, bl - QMOST : bl] = (
                dx[i, 2 * bl - QMOST : 2 * bl] + from_next[i]
            ) * factor
        over_peers(r_copies, start)
        for copy in own_r:
            copy.start()

    def backward_pair(n, _):
        q = n + 2
        t = me.pair_of(q)
        turn_keys(doc_kv(0, t))
        for i, value in enumerate(backward(1, npair + t, doc_kv(1, t), q // 8)):
            put(t, i, value, False)

        @pl.when(t <= own_pair)
        def _():
            for i, value in enumerate(backward(0, t, doc_kv(1, t), q // 8)):
                put(t, i, value, True)

        core_copy(t).start()

        @pl.when(n >= LAG)
        def _():
            serve(q - LAG)

        @pl.when(n == npair // 2)
        def _():
            send_questions()

        return 0

    lax.fori_loop(0, npair, backward_pair, 0)

    for s in range(2):
        for g in range(group):
            part = jnp.transpose(dqt[s, :, g * bl : (g + 1) * bl])
            dq[s, :, g * HD : (g + 1) * HD] = (part * SCALE).astype(jnp.bfloat16)

    def out_part(kind, p):
        return dq.at[1 - kind, rows_of(p)]

    def out_copies(kind):
        def made(d, p, device):
            return remote(
                out_part(kind, p),
                head_part(kind, gq, me.h),
                o_send.at[kind],
                o_recv.at[kind],
                device,
            )

        return made

    own_out = [
        pltpu.make_async_copy(out_part(k, me.h), head_part(k, gq, me.h), local_sem.at[4 + k])
        for k in range(2)
    ]
    over_rows(out_copies, start)
    for copy in own_out:
        copy.start()

    def serve_rest(n, _):
        serve(n + 2)
        return 0

    lax.fori_loop(npair - LAG, npair, serve_rest, 0)

    def final_copies(kind):
        def made(d, p, device):
            return [
                remote(
                    final.at[kind, i, rows_of(p)],
                    landed.at[kind, i, me.h],
                    f_send.at[kind, i],
                    f_recv.at[kind, i],
                    device,
                )
                for i in range(2)
            ]

        return made

    for way in range(2):
        for xs in range(2):
            hop_copy(way, xs, 1).wait_recv()
    for kind in (1, 0):
        xs = me.xh if kind == 0 else 1 - me.xh
        t = me.pair(xs, me.z)
        for i in range(2):
            factor = SCALE if i == 0 else 1.0
            final[kind, i] = (
                sums[t, i]
                + chain[0, xs, 0, i].astype(jnp.float32)
                + chain[1, xs, 0, i].astype(jnp.float32)
            ) * factor
        over_peers(final_copies(kind), start, kind == 1)
    for i in range(2):
        landed[0, i, me.h] = final[0, i, own_rows]
    for i in range(2):
        received_all(landed.at[0, i, pl.ds(0, peers)], f_recv.at[0, i])
        received_all(landed.at[1, i], f_recv.at[1, i])
    for i in range(2):
        for h in range(nh):
            owned[i, :, h * HD : (h + 1) * HD] = landed[0, i, h] + landed[1, i, h]
    last_out = [
        pltpu.make_async_copy(owned.at[i], (gk, gv)[i].at[0], local_sem.at[2 + i])
        for i in range(2)
    ]
    for copy in last_out:
        copy.start()

    sent_all(kvd.at[0, pl.ds(0, n_sent["ring"])], g_send)
    sent_all(kvd.at[0, pl.ds(0, n_sent["core"])], s_send)
    for i in range(2):
        sent_all(kvd.at[i, 0, peer_rows], kv_send.at[i, 0])
        sent_all(kvd.at[i, 0, peer_rows], kv_send.at[i, 1])
        sent_all(kvd.at[i, 0], kv_send.at[i, 2])
        sent_all(result.at[i, peer_rows], r_send.at[i])
        sent_all(final.at[0, i, peer_rows], f_send.at[0, i])
        sent_all(final.at[1, i], f_send.at[1, i])
        sent_all(q_in.at[i, pl.ds(0, peers)], q_send.at[i])
        sent_all(c_in.at[i, pl.ds(0, peers)], c_send.at[i])
        sent_all(dq.at[i, peer_rows], o_send.at[i])
        received_all(dq.at[i, peer_rows], o_recv.at[i])
        received_all(result.at[i, peer_rows], r_recv.at[i])
    sent_all(d_in.at[pl.ds(0, peers)], d_send)
    tail_copy.wait_send()
    sent_all(from_core, core_send)
    sent_all(low_sums.at[pl.ds(0, 4 * me.half - 2)], hop_send)
    next_copy.wait_send()
    for copy in own_out + own_r + last_out:
        copy.wait()


def place_results(*refs):
    sources, targets, held, sem = refs[:3], refs[3:6], refs[6:9], refs[9]
    reads = [pltpu.make_async_copy(sources[i], held[i], sem.at[0, i]) for i in range(3)]
    writes = [pltpu.make_async_copy(held[i], targets[i], sem.at[1, i]) for i in range(3)]
    for copy in reads:
        copy.start()
    for i in range(3):
        reads[i].wait()
        writes[i].start()
    for copy in writes:
        copy.wait()


def shards(queries, keys, values, outputs, cotangent, lengths):
    nctx, nh = lax.axis_size("ctx"), lax.axis_size("head")
    tok = queries.shape[1]
    gw = queries.shape[2] // nh
    bl = tok * nh
    nhead = queries.shape[2] // HD
    dims = (nctx, nh, tok, gw, bl, nhead)
    npair = nctx // 2
    group = gw // HD
    rows = group * bl
    hbm = pl.BlockSpec(memory_space=pl.ANY)
    vmem = pl.BlockSpec(memory_space=pltpu.VMEM)
    dma = pltpu.SemaphoreType.DMA
    space = pltpu.VMEM
    f32, b16 = jnp.float32, jnp.bfloat16
    shape = jax.ShapeDtypeStruct
    hops = nctx // 8
    made = (
        shape((2, tok, nh * gw), b16),
        shape((2, tok, nh * HD), f32),
        shape((2, tok, nh * HD), f32),
    )
    results = pl.pallas_call(
        functools.partial(kernel, dims),
        out_shape=made,
        in_specs=[vmem, hbm, hbm, hbm, hbm, hbm],
        out_specs=[hbm] * 3,
        scratch_shapes=[
            space((2, nh, tok, gw), b16),
            space((2, nh, tok, gw), b16),
            space((nh, group, HD), f32),
            space((2, nctx, bl, HD), b16),
            space((2, 2, bl, HD), b16),
            space((2, tok, HD), f32),
            space((HD, HD), f32),
            space((2, rows, HD), b16),
            space((2, rows, HD), b16),
            space((2, 1, rows), f32),
            space((group, bl), f32),
            space((2 * npair + 1, 2 * bl, rows), f32),
            space((2, 8, rows), f32),
            space((2, 8, rows), f32),
            space((2, 1, rows), f32),
            space((2, 1, rows), f32),
            space((3, 2, 1, rows), f32),
            space((2, HD, rows), f32),
            space((HD, 2 * bl), b16),
            space((2 * bl, rows), b16),
            space((2 * bl, rows), b16),
            space((npair, 2, 2, bl, HD), f32),
            space((2, 2 * bl, HD), f32),
            space((2, bl, gw), b16),
            space((npair, 2, bl, HD), f32),
            space((npair, 2, bl, HD), f32),
            space((npair, 2, bl, HD), b16),
            space((2, 2, hops, 2, bl, HD), b16),
            space((2, QMOST, HD), f32),
            space((2, bl, HD), f32),
            space((2, 2, bl, HD), f32),
            space((2, 2, nh, tok, HD), f32),
            space((2, tok, nh * HD), f32),
            space((2, tok, nh * gw), b16),
            space((2, tok, nh * gw), b16),
            dma((2, 3)),
            dma((2, 3)),
            dma((2,)),
            dma((2,)),
            dma((2,)),
            dma((2,)),
            dma,
            dma,
            dma,
            dma((2, hops, 2, 2)),
            dma,
            dma((hops + 2,)),
            dma,
            dma,
            dma,
            dma((npair,)),
            dma,
            dma((2, 2, hops)),
            dma,
            dma,
            dma((2,)),
            dma((2,)),
            dma((2,)),
            dma((2,)),
            dma((2, 2)),
            dma((2, 2)),
            dma((11,)),
        ],
        compiler_params=pltpu.CompilerParams(
            collective_id=0, has_side_effects=True, vmem_limit_bytes=60 * 2**20
        ),
        name="attention_backward",
    )(lengths.reshape(1, -1), queries, keys, values, outputs, cotangent)
    return pl.pallas_call(
        place_results,
        out_shape=made,
        in_specs=[hbm] * 3,
        out_specs=[hbm] * 3,
        scratch_shapes=[space(m.shape, m.dtype) for m in made] + [dma((2, 3))],
        name="place_results",
    )(*results)


def solution(mesh):
    spec = P(None, ("ctx", "head"), None)
    return jax.shard_map(
        shards,
        mesh=mesh,
        in_specs=(spec,) * 5 + (P(),),
        out_specs=(spec,) * 3,
        check_vma=False,
    )
```

```python
import functools
import math

import jax
import jax.numpy as jnp
from jax import lax
from jax.experimental import pallas as pl
from jax.experimental.pallas import tpu as pltpu
from jax.sharding import PartitionSpec as P

HD = 128
NEG_FILL = -1e30
QMOST = 32
SCALE = HD ** (-0.5)
EXP2_SCALE = SCALE * math.log2(math.e)
MESH = pl.DeviceIdType.MESH
LAG = 2
UNROLL = 4


def remote(src, dst, send_sem, recv_sem, device):
    return pltpu.make_async_remote_copy(
        src_ref=src,
        dst_ref=dst,
        send_sem=send_sem,
        recv_sem=recv_sem,
        device_id=device,
        device_id_type=MESH,
    )


class Place:
    def __init__(self, ctx_count, head_count):
        self.nctx = ctx_count
        self.nh = head_count
        self.nz = ctx_count // 4
        self.half = self.nz // 2
        self.npair = ctx_count // 2
        self.ctx = lax.axis_index("ctx")
        self.h = lax.axis_index("head")
        self.c = lax.rem(self.ctx, 2)
        self.z = lax.rem(self.ctx // 2, self.nz)
        self.xh = self.ctx // (2 * self.nz)

    def zmod(self, z):
        return lax.rem(z + self.nz, self.nz)

    def block(self, xh, z, c):
        return (xh * self.nz + self.zmod(z)) * 2 + c

    def pair(self, xh, z):
        return xh * self.nz + self.zmod(z)

    def dev(self, xh, z, c):
        return (self.block(xh, z, c), self.h)

    def z_up(self):
        return self.dev(self.xh, self.z + 1, self.c)

    def z_down(self):
        return self.dev(self.xh, self.z - 1, self.c)

    def across(self):
        return self.block(1 - self.xh, self.z, self.c)

    def sibling(self):
        return self.dev(self.xh, self.z, 1 - self.c)

    def ctx_next(self):
        return (lax.rem(self.ctx + 1, self.nctx), self.h)

    def ctx_prev(self):
        return (lax.rem(self.ctx + self.nctx - 1, self.nctx), self.h)

    def head_peer(self, d):
        return lax.rem(self.h + d, self.nh)

    def far(self, q):
        return self.half - q // 4

    def way(self, q):
        return q % 2

    def xs(self, q):
        return (q // 2 + q) % 2

    def reach(self, q):
        return self.half - (self.way(q) + self.xs(q) + 1) % 2

    def z_of(self, q):
        return self.z + self.far(q) * (1 - 2 * self.way(q))

    def pair_of(self, q):
        return self.pair(self.xs(q), self.z_of(q))

    def block_of(self, q, c):
        return self.block(self.xs(q), self.z_of(q), c)

    def barrier(self):
        barrier = pltpu.get_barrier_semaphore()

        def greet(d, _):
            pl.semaphore_signal(
                barrier, inc=1, device_id=(self.ctx, self.head_peer(d)), device_id_type=MESH
            )
            return 0

        def greet_across(d, _):
            device = (self.across(), self.head_peer(d))
            pl.semaphore_signal(barrier, inc=1, device_id=device, device_id_type=MESH)
            return 0

        lax.fori_loop(1, self.nh, greet, 0)
        lax.fori_loop(0, self.nh, greet_across, 0)
        near = (
            self.z_up(),
            self.z_down(),
            self.sibling(),
            self.ctx_next(),
            self.ctx_prev(),
        )
        for device in near:
            pl.semaphore_signal(barrier, inc=1, device_id=device, device_id_type=MESH)
        pl.semaphore_wait(barrier, 2 * self.nh - 1 + len(near))


def nt_dot(a, b):
    return lax.dot_general(a, b, (((1,), (1,)), ((), ())), preferred_element_type=jnp.float32)


def nn_dot(a, b):
    return jnp.dot(a, b, preferred_element_type=jnp.float32)


def by_sublane(x):
    return x.reshape(x.shape[0] // 8, 8, x.shape[1])


def kernel(
    dims,
    len_ref,
    q_ref,
    k_ref,
    v_ref,
    o_ref,
    c_ref,
    gq,
    gk,
    gv,
    q_in,
    c_in,
    d_in,
    kvd,
    kvq,
    delta,
    delta_t,
    qs,
    cs,
    dd,
    turn,
    weights,
    peak,
    total,
    first_max,
    final_max,
    inverse,
    dqt,
    keys_t,
    low_p,
    low_s,
    dkv,
    dx,
    dq,
    from_core,
    sums,
    low_sums,
    chain,
    from_next,
    result,
    final,
    landed,
    owned,
    o_in,
    c_near,
    kv_send,
    kv_recv,
    q_send,
    q_recv,
    c_send,
    c_recv,
    d_send,
    d_recv,
    g_send,
    g_recv,
    s_send,
    s_recv,
    t_send,
    t_recv,
    core_send,
    core_recv,
    hop_send,
    hop_recv,
    n_send,
    n_recv,
    o_send,
    o_recv,
    r_send,
    r_recv,
    f_send,
    f_recv,
    local_sem,
):
    nctx, nh, tok, gw, bl, nhead = dims
    me = Place(nctx, nh)
    npair = me.npair
    last = 4 * me.half + 1
    group = gw // HD
    rows = group * bl
    tile = 2 * bl
    own_pair = me.ctx // 2
    chunk = min(256, rows)
    every = [pl.ds(r * chunk, chunk) for r in range(rows // chunk)]
    fetch_o = pltpu.make_async_copy(o_ref, o_in, local_sem.at[7])
    fetch_c = pltpu.make_async_copy(c_ref, c_near, local_sem.at[8])
    fetch_o.start()
    fetch_c.start()
    me.barrier()

    def rows_of(p):
        return pl.ds(pl.multiple_of(p * tok, tok), tok)

    own_rows = rows_of(me.h)

    def over_peers(make, act, across=False):
        def step(d, _):
            p = me.head_peer(d)
            made = make(d, p, (me.across() if across else me.ctx, p))
            for copy in made if isinstance(made, list) else [made]:
                act(copy)
            return 0

        lax.fori_loop(0 if across else 1, nh, step, 0)

    def sent_all(like, sem):
        remote(like, like, sem, sem, me.sibling()).wait_send()

    def received_all(like, sem):
        remote(like, like, sem, sem, me.sibling()).wait_recv()

    peers = nh - 1
    peer_rows = pl.ds(0, peers * tok)

    def start(copy):
        copy.start()

    kv_ref = (k_ref, v_ref)

    def kv_target(i, j):
        return kvq.at[i, 1, own_rows] if j else kvd.at[i, me.ctx, own_rows]

    def kv_copies(i, j):
        def made(d, p, device):
            cols = pl.ds(pl.multiple_of(p * HD, HD), HD)
            return remote(
                kv_ref[i].at[j, :, cols],
                kv_target(i, j),
                kv_send.at[i, j],
                kv_recv.at[i, j],
                device,
            )

        return made

    def kx_copies(i):
        def made(d, p, device):
            cols = pl.ds(pl.multiple_of(p * HD, HD), HD)
            return remote(
                kv_ref[i].at[0, :, cols], kv_target(i, 0), kv_send.at[i, 2], kv_recv.at[i, 2], device
            )

        return made

    def head_part(kind, ref, p):
        return ref.at[1 - kind, :, pl.ds(pl.multiple_of(p * gw, gw), gw)]

    def place_of(kind, ref):
        return ref.at[1 - kind, me.h]

    def row_copies(kind, source, target, send, recv):
        def made(d, p, device):
            return remote(
                head_part(kind, source, p),
                place_of(kind, target),
                send.at[kind],
                recv.at[kind],
                device,
            )

        return made

    def q_copies(kind):
        return row_copies(kind, q_ref, q_in, q_send, q_recv)

    def c_copies(kind):
        return row_copies(kind, c_ref, c_in, c_send, c_recv)

    def over_rows(copies, act):
        for kind in range(2):
            over_peers(copies(kind), act)

    def d_copy(d, p, device):
        return remote(
            delta_t.at[pl.ds(pl.multiple_of(p * group, group), group)],
            d_in.at[me.h],
            d_send,
            d_recv,
            device,
        )

    for i in range(2):
        over_peers(kv_copies(i, 0), start)
        over_peers(kx_copies(i), start, True)
    own_cols = pl.ds(pl.multiple_of(me.h * HD, HD), HD)
    locals_ = [
        pltpu.make_async_copy(kv_ref[i].at[j, :, own_cols], kv_target(i, j), local_sem.at[2 * i + j])
        for i in range(2)
        for j in range(2)
    ]
    own_q = [
        pltpu.make_async_copy(head_part(k, q_ref, me.h), place_of(k, q_in), local_sem.at[4 + k])
        for k in range(2)
    ]
    own_c = [
        pltpu.make_async_copy(head_part(k, c_ref, me.h), place_of(k, c_in), local_sem.at[9 + k])
        for k in range(2)
    ]
    for copy in locals_:
        copy.start()
    over_rows(q_copies, start)
    for i in range(2):
        over_peers(kv_copies(i, 1), start)
    for copy in own_q + own_c:
        copy.start()

    fetch_o.wait()
    fetch_c.wait()
    lanes = lax.broadcasted_iota(jnp.int32, (2, tok, HD), 2)

    def some_heads(j, acc):
        for u in range(UNROLL):
            at = pl.ds(pl.multiple_of((j * UNROLL + u) * HD, HD), HD)
            prod = c_near[:, :, at].astype(jnp.float32) * o_in[:, :, at].astype(jnp.float32)
            part = jnp.sum(prod, axis=-1, keepdims=True)
            acc = jnp.where(lanes == j * UNROLL + u, part, acc)
        return acc

    delta[...] = lax.fori_loop(
        0, nhead // UNROLL, some_heads, jnp.zeros((2, tok, HD), jnp.float32)
    )
    delta_t[:, 0 : 2 * tok] = jnp.transpose(delta[...].reshape(2 * tok, HD))
    over_peers(d_copy, start)
    d_in[me.h] = delta_t[pl.ds(pl.multiple_of(me.h * group, group), group)]

    n_sent = {"ring": 0, "core": 0}

    def ring_copy(i, b, f, way, xs, device):
        return remote(kvd.at[i, b], kvd.at[i, b], g_send, g_recv.at[i, f - 1, way, xs], device)

    def ring_send(i, b, f, way, xs):
        ring_copy(i, b, f, way, xs, me.z_down() if way == 0 else me.z_up()).start()
        n_sent["ring"] += 1

    def core_send_block(i, b, f):
        sem = s_recv.at[f if i == 0 else me.half + 1]
        remote(kvd.at[i, b], kvd.at[i, b], s_send, sem, me.sibling()).start()
        n_sent["core"] += 1

    tail = pl.ds(bl - QMOST, QMOST)
    tail_copy = remote(kvq.at[:, 1, tail], kvq.at[:, 0, tail], t_send, t_recv, me.ctx_next())

    def gather_own(i, b, xs):
        ring_send(i, b, 1, 1, xs)
        ring_send(i, b, 1, 0, xs)

    def gather_step(f, kv=(0, 1)):
        qs_at = [q for q in range(last - 1, 1, -1) if me.far(q) == f]
        for i in kv:
            for q in qs_at:
                b, way, xs = me.block_of(q, me.c), me.way(q), me.xs(q)
                ring_copy(i, b, f, way, xs, me.sibling()).wait_recv()
                if f < me.reach(q):
                    ring_send(i, b, f + 1, way, xs)
                core_send_block(i, b, f)

    for i in range(2):
        locals_[2 * i].wait()
        received_all(kvd.at[i, me.ctx, peer_rows], kv_recv.at[i, 0])
        gather_own(i, me.ctx, me.xh)
        received_all(kvd.at[i, me.across()], kv_recv.at[i, 2])
        gather_own(i, me.across(), 1 - me.xh)
        core_send_block(i, me.ctx, 0)
        core_send_block(i, me.across(), 0)

    count = len_ref.shape[1]
    lens = jnp.broadcast_to(len_ref[...].astype(jnp.float32), (8, count)).astype(jnp.bfloat16)
    i0 = lax.broadcasted_iota(jnp.int32, (count, count), 0)
    i1 = lax.broadcasted_iota(jnp.int32, (count, count), 1)
    before = jnp.where(i0 < i1, 1.0, 0.0).astype(jnp.bfloat16)
    after = jnp.where(i1 < i0, 1.0, 0.0).astype(jnp.bfloat16)
    starts_row = nn_dot(lens, before)[0:1, :]
    starts_col = nt_dot(after, lens)[:, 0:1]
    row_at = lax.broadcasted_iota(jnp.int32, (1, chunk), 1) % bl
    key_at = lax.broadcasted_iota(jnp.int32, (tile, 1), 0) - bl
    row_off = (row_at + me.ctx * bl).astype(jnp.float32)
    key_off = (key_at + me.ctx * bl).astype(jnp.float32)
    row_seg = jnp.sum(jnp.where(starts_col <= row_off, 1.0, 0.0), axis=0, keepdims=True)
    key_seg = jnp.sum(jnp.where(starts_row <= key_off, 1.0, 0.0), axis=1, keepdims=True)
    question_mask = (key_at <= row_at) & (key_seg == row_seg)
    doc_key = lax.broadcasted_iota(jnp.int32, (tile, 1), 0) + (own_pair * 2 - me.ctx) * bl
    doc_mask = doc_key <= row_at

    peak[...] = jnp.full(peak.shape, NEG_FILL, jnp.float32)
    total[...] = jnp.zeros(total.shape, jnp.float32)
    dqt[...] = jnp.zeros(dqt.shape, jnp.float32)

    def doc_kv(i, t):
        return kvd[i, pl.ds(2 * t, 2)].reshape(tile, HD)

    def question_kv(i):
        at = lax.broadcasted_iota(jnp.int32, (bl, HD), 0)
        prev = jnp.where(at >= bl - QMOST, kvq[i, 0].astype(jnp.float32), 0.0)
        return jnp.concatenate([prev.astype(jnp.bfloat16), kvq[i, 1]], axis=0)

    def scores_of(s, keys, mask, cols):
        scores = nt_dot(keys, qs[s, cols, :])
        return scores if mask is None else jnp.where(mask, scores, NEG_FILL)

    def peak_sweep(s, keys, mask, at):
        for cols in at:
            scores = by_sublane(scores_of(s, keys, mask, cols))
            peak[s, :, cols] = jnp.maximum(peak[s, :, cols], jnp.max(scores, axis=0))

    def weight_sweep(s, slot, keys, mask, at, known):
        for cols in at:
            scores = scores_of(s, keys, mask, cols)
            part = jnp.exp2((scores - known[s, 0:1, cols]) * EXP2_SCALE)
            weights[slot, :, cols] = part
            total[s, :, cols] = total[s, :, cols] + jnp.sum(by_sublane(part), axis=0)

    def on_pair(t, sweep):
        sweep(1, None, every)

        @pl.when(t < own_pair)
        def _():
            sweep(0, None, every)

        @pl.when(t == own_pair)
        def _():
            sweep(0, doc_mask, every)

    def sort_rows(target, source, s):
        for g in range(group):
            cols = slice(g * HD, (g + 1) * HD)
            target[s, g * bl : (g + 1) * bl, :] = source[s, :, :, cols].reshape(bl, HD)

    def peaks(f):
        count = 4 if 0 < f < me.half else 2
        received_all(kvd.at[0, pl.ds(0, count)], s_recv.at[f])

        def step(i, _):
            q = last - i if f == 0 else last - 2 - 4 * (f - 1) - i
            t = me.pair_of(q)
            keys = doc_kv(0, t)

            def sweep(s, mask, at):
                peak_sweep(s, keys, mask, at)

            on_pair(t, sweep)
            return 0

        lax.fori_loop(0, count, step, 0)

    def weigh(low, high, known):
        def step(q, _):
            t = me.pair_of(q)
            keys = doc_kv(0, t)

            def sweep(s, mask, at):
                weight_sweep(s, s * npair + t, keys, mask, at, known)

            on_pair(t, sweep)
            return 0

        lax.fori_loop(low, high, step, 0)

    gather_step(1)
    for i in range(2):
        locals_[2 * i + 1].wait()
        received_all(kvq.at[i, 1, peer_rows], kv_recv.at[i, 1])
    tail_copy.start()
    gather_step(2)
    for copy in own_q:
        copy.wait()
    for kind in range(2):
        received_all(q_in.at[kind, pl.ds(0, peers)], q_recv.at[kind])
    over_rows(c_copies, start)
    for s in range(2):
        sort_rows(qs, q_in, s)

    peaks(0)
    tail_copy.wait_recv()
    peak_sweep(1, question_kv(0), question_mask, every)
    for f in range(1, me.half - 1):
        if f + 1 > 2:
            gather_step(f + 1)
        peaks(f)
    for s in range(2):
        first_max[s] = jnp.max(peak[s], axis=0, keepdims=True)
    weight_sweep(1, 2 * npair, question_kv(0), question_mask, every, first_max)
    near = max(8, 4 * me.half - 4)
    weigh(near, last + 1, first_max)
    if me.half > 2:
        gather_step(me.half, (0,))
    weigh(8, near, first_max)
    if me.half > 2:
        gather_step(me.half, (1,))
    peaks(me.half - 1)
    peaks(me.half)
    for s in range(2):
        final_max[s] = jnp.max(peak[s], axis=0, keepdims=True)
        total[s] = total[s] * jnp.exp2((first_max[s] - final_max[s]) * EXP2_SCALE)
    weigh(2, 8, final_max)
    for s in range(2):
        whole = 1.0 / jnp.sum(total[s], axis=0, keepdims=True)
        nearer = whole * jnp.exp2((first_max[s] - final_max[s]) * EXP2_SCALE)
        inverse[0, s] = whole
        inverse[1, s] = nearer
        inverse[2, s] = nearer

    received_all(kvd.at[1, pl.ds(0, npair)], s_recv.at[me.half + 1])

    for copy in own_c:
        copy.wait()
    for kind in range(2):
        received_all(c_in.at[kind, pl.ds(0, peers)], c_recv.at[kind])
    received_all(d_in.at[pl.ds(0, peers)], d_recv)
    for s in range(2):
        sort_rows(cs, c_in, s)
        for j in range(nh):
            turn[:, j * tok : (j + 1) * tok] = d_in[j, :, s * tok : (s + 1) * tok]
        for g in range(group):
            dd[s, 0:1, g * bl : (g + 1) * bl] = turn[g : g + 1, :]

    def low_chunk(s, slot, cols, values, scale_at):
        prob = weights[slot, :, cols] * inverse[scale_at, s, 0:1, cols]
        d_prob = nt_dot(values, cs[s, cols, :])
        low_p[s, :, cols] = prob.astype(jnp.bfloat16)
        low_s[s, :, cols] = (prob * (d_prob - dd[s, 0:1, cols])).astype(jnp.bfloat16)

    def d_value(s):
        return nn_dot(low_p[s], cs[s])

    def d_key(s):
        return nn_dot(low_s[s], qs[s])

    def d_query(s):
        dqt[s] += nn_dot(keys_t[...], low_s[s])

    def backward(s, slot, values, scale_at):
        for cols in every:
            low_chunk(s, slot, cols, values, scale_at)
        made = d_key(s), d_value(s)
        d_query(s)
        return made

    def backward_both(t, values, scale_at):
        for cols in every:
            low_chunk(1, npair + t, cols, values, scale_at)
        todo = [d_key, d_value, d_query]
        made = []
        for cols in every:
            low_chunk(0, t, cols, values, scale_at)
            if todo:
                made.append(todo.pop(0)(1))
        for product in todo:
            made.append(product(1))
        made = made[0] + d_key(0), made[1] + d_value(0)
        d_query(0)
        return made

    def turn_keys(keys):
        keys_t[...] = jnp.transpose(keys.astype(jnp.float32)).astype(jnp.bfloat16)

    def put(t, i, value):
        for c in range(2):
            dkv[t, i, c] = value[c * bl : (c + 1) * bl]

    def core_copy(t):
        return remote(
            dkv.at[t, :, 1 - me.c],
            from_core.at[t],
            core_send,
            core_recv.at[t],
            me.sibling(),
        )

    def hop_copy(way, xs, f):
        return remote(
            low_sums.at[me.pair(xs, me.z + f * (1 - 2 * way))],
            chain.at[way, xs, f - 1],
            hop_send,
            hop_recv.at[way, xs, f - 1],
            me.dev(me.xh, me.z + 1 - 2 * way, me.c),
        )

    def serve(q):
        f, way, xs, t = me.far(q), me.way(q), me.xs(q), me.pair_of(q)
        core_copy(t).wait_recv()
        sums[t] = dkv[t, :, me.c] + from_core[t]

        @pl.when((f > 0) & (f < me.reach(q)))
        def _():
            hop_copy(way, xs, f + 1).wait_recv()
            sums[t] = sums[t] + chain[way, xs, f].astype(jnp.float32)

        @pl.when(f > 0)
        def _():
            low_sums[t] = sums[t].astype(jnp.bfloat16)
            hop_copy(way, xs, f).start()

    turn_keys(question_kv(0))
    dx[0], dx[1] = backward(1, 2 * npair, question_kv(1), 1)
    next_copy = remote(dx.at[:, tail], from_next, n_send, n_recv, me.ctx_prev())
    next_copy.start()

    def r_copies(d, p, device):
        return [
            remote(
                result.at[i, rows_of(p)],
                (gk, gv)[i].at[1, :, own_cols],
                r_send.at[i],
                r_recv.at[i],
                device,
            )
            for i in range(2)
        ]

    own_r = [
        pltpu.make_async_copy(
            result.at[i, own_rows], (gk, gv)[i].at[1, :, own_cols], local_sem.at[i]
        )
        for i in range(2)
    ]

    def send_questions():
        next_copy.wait_recv()
        for i in range(2):
            factor = SCALE if i == 0 else 1.0
            result[i, 0 : bl - QMOST] = dx[i, bl : 2 * bl - QMOST] * factor
            result[i, bl - QMOST : bl] = (
                dx[i, 2 * bl - QMOST : 2 * bl] + from_next[i]
            ) * factor
        over_peers(r_copies, start)
        for copy in own_r:
            copy.start()

    def backward_pair(n, _):
        q = n + 2
        t = me.pair_of(q)
        turn_keys(doc_kv(0, t))
        @pl.when(t > own_pair)
        def _():
            for i, value in enumerate(backward(1, npair + t, doc_kv(1, t), q // 8)):
                put(t, i, value)

        @pl.when(t <= own_pair)
        def _():
            for i, value in enumerate(backward_both(t, doc_kv(1, t), q // 8)):
                put(t, i, value)

        core_copy(t).start()

        @pl.when(n >= LAG)
        def _():
            serve(q - LAG)

        @pl.when(n == npair // 2)
        def _():
            send_questions()

        return 0

    lax.fori_loop(0, npair, backward_pair, 0)

    for s in range(2):
        for g in range(group):
            part = jnp.transpose(dqt[s, :, g * bl : (g + 1) * bl])
            dq[s, :, g * HD : (g + 1) * HD] = (part * SCALE).astype(jnp.bfloat16)

    def out_part(kind, p):
        return dq.at[1 - kind, rows_of(p)]

    def out_copies(kind):
        def made(d, p, device):
            return remote(
                out_part(kind, p),
                head_part(kind, gq, me.h),
                o_send.at[kind],
                o_recv.at[kind],
                device,
            )

        return made

    own_out = [
        pltpu.make_async_copy(out_part(k, me.h), head_part(k, gq, me.h), local_sem.at[4 + k])
        for k in range(2)
    ]
    over_rows(out_copies, start)
    for copy in own_out:
        copy.start()

    def serve_rest(n, _):
        serve(n + 2)
        return 0

    lax.fori_loop(npair - LAG, npair, serve_rest, 0)

    def final_copies(kind):
        def made(d, p, device):
            return [
                remote(
                    final.at[kind, i, rows_of(p)],
                    landed.at[kind, i, me.h],
                    f_send.at[kind, i],
                    f_recv.at[kind, i],
                    device,
                )
                for i in range(2)
            ]

        return made

    for way in range(2):
        for xs in range(2):
            hop_copy(way, xs, 1).wait_recv()
    for kind in (1, 0):
        xs = me.xh if kind == 0 else 1 - me.xh
        t = me.pair(xs, me.z)
        for i in range(2):
            factor = SCALE if i == 0 else 1.0
            final[kind, i] = (
                sums[t, i]
                + chain[0, xs, 0, i].astype(jnp.float32)
                + chain[1, xs, 0, i].astype(jnp.float32)
            ) * factor
        over_peers(final_copies(kind), start, kind == 1)
    for i in range(2):
        landed[0, i, me.h] = final[0, i, own_rows]
    for i in range(2):
        received_all(landed.at[0, i, pl.ds(0, peers)], f_recv.at[0, i])
        received_all(landed.at[1, i], f_recv.at[1, i])
    for i in range(2):
        for h in range(nh):
            owned[i, :, h * HD : (h + 1) * HD] = landed[0, i, h] + landed[1, i, h]
    last_out = [
        pltpu.make_async_copy(owned.at[i], (gk, gv)[i].at[0], local_sem.at[2 + i])
        for i in range(2)
    ]
    for copy in last_out:
        copy.start()

    sent_all(kvd.at[0, pl.ds(0, n_sent["ring"])], g_send)
    sent_all(kvd.at[0, pl.ds(0, n_sent["core"])], s_send)
    for i in range(2):
        sent_all(kvd.at[i, 0, peer_rows], kv_send.at[i, 0])
        sent_all(kvd.at[i, 0, peer_rows], kv_send.at[i, 1])
        sent_all(kvd.at[i, 0], kv_send.at[i, 2])
        sent_all(result.at[i, peer_rows], r_send.at[i])
        sent_all(final.at[0, i, peer_rows], f_send.at[0, i])
        sent_all(final.at[1, i], f_send.at[1, i])
        sent_all(q_in.at[i, pl.ds(0, peers)], q_send.at[i])
        sent_all(c_in.at[i, pl.ds(0, peers)], c_send.at[i])
        sent_all(dq.at[i, peer_rows], o_send.at[i])
        received_all(dq.at[i, peer_rows], o_recv.at[i])
        received_all(result.at[i, peer_rows], r_recv.at[i])
    sent_all(d_in.at[pl.ds(0, peers)], d_send)
    tail_copy.wait_send()
    sent_all(from_core, core_send)
    sent_all(low_sums.at[pl.ds(0, 4 * me.half - 2)], hop_send)
    next_copy.wait_send()
    for copy in own_out + own_r + last_out:
        copy.wait()


def place_results(*refs):
    sources, targets, held, sem = refs[:3], refs[3:6], refs[6:9], refs[9]
    reads = [pltpu.make_async_copy(sources[i], held[i], sem.at[0, i]) for i in range(3)]
    writes = [pltpu.make_async_copy(held[i], targets[i], sem.at[1, i]) for i in range(3)]
    for copy in reads:
        copy.start()
    for i in range(3):
        reads[i].wait()
        writes[i].start()
    for copy in writes:
        copy.wait()


def shards(queries, keys, values, outputs, cotangent, lengths):
    nctx, nh = lax.axis_size("ctx"), lax.axis_size("head")
    tok = queries.shape[1]
    gw = queries.shape[2] // nh
    bl = tok * nh
    nhead = queries.shape[2] // HD
    dims = (nctx, nh, tok, gw, bl, nhead)
    npair = nctx // 2
    group = gw // HD
    rows = group * bl
    hbm = pl.BlockSpec(memory_space=pl.ANY)
    vmem = pl.BlockSpec(memory_space=pltpu.VMEM)
    dma = pltpu.SemaphoreType.DMA
    space = pltpu.VMEM
    f32, b16 = jnp.float32, jnp.bfloat16
    shape = jax.ShapeDtypeStruct
    hops = nctx // 8
    made = (
        shape((2, tok, nh * gw), b16),
        shape((2, tok, nh * HD), f32),
        shape((2, tok, nh * HD), f32),
    )
    results = pl.pallas_call(
        functools.partial(kernel, dims),
        out_shape=made,
        in_specs=[vmem, hbm, hbm, hbm, hbm, hbm],
        out_specs=[hbm] * 3,
        scratch_shapes=[
            space((2, nh, tok, gw), b16),
            space((2, nh, tok, gw), b16),
            space((nh, group, HD), f32),
            space((2, nctx, bl, HD), b16),
            space((2, 2, bl, HD), b16),
            space((2, tok, HD), f32),
            space((HD, HD), f32),
            space((2, rows, HD), b16),
            space((2, rows, HD), b16),
            space((2, 1, rows), f32),
            space((group, bl), f32),
            space((2 * npair + 1, 2 * bl, rows), f32),
            space((2, 8, rows), f32),
            space((2, 8, rows), f32),
            space((2, 1, rows), f32),
            space((2, 1, rows), f32),
            space((3, 2, 1, rows), f32),
            space((2, HD, rows), f32),
            space((HD, 2 * bl), b16),
            space((2, 2 * bl, rows), b16),
            space((2, 2 * bl, rows), b16),
            space((npair, 2, 2, bl, HD), f32),
            space((2, 2 * bl, HD), f32),
            space((2, bl, gw), b16),
            space((npair, 2, bl, HD), f32),
            space((npair, 2, bl, HD), f32),
            space((npair, 2, bl, HD), b16),
            space((2, 2, hops, 2, bl, HD), b16),
            space((2, QMOST, HD), f32),
            space((2, bl, HD), f32),
            space((2, 2, bl, HD), f32),
            space((2, 2, nh, tok, HD), f32),
            space((2, tok, nh * HD), f32),
            space((2, tok, nh * gw), b16),
            space((2, tok, nh * gw), b16),
            dma((2, 3)),
            dma((2, 3)),
            dma((2,)),
            dma((2,)),
            dma((2,)),
            dma((2,)),
            dma,
            dma,
            dma,
            dma((2, hops, 2, 2)),
            dma,
            dma((hops + 2,)),
            dma,
            dma,
            dma,
            dma((npair,)),
            dma,
            dma((2, 2, hops)),
            dma,
            dma,
            dma((2,)),
            dma((2,)),
            dma((2,)),
            dma((2,)),
            dma((2, 2)),
            dma((2, 2)),
            dma((11,)),
        ],
        compiler_params=pltpu.CompilerParams(
            collective_id=0, has_side_effects=True, vmem_limit_bytes=60 * 2**20
        ),
        name="attention_backward",
    )(lengths.reshape(1, -1), queries, keys, values, outputs, cotangent)
    return pl.pallas_call(
        place_results,
        out_shape=made,
        in_specs=[hbm] * 3,
        out_specs=[hbm] * 3,
        scratch_shapes=[space(m.shape, m.dtype) for m in made] + [dma((2, 3))],
        name="place_results",
    )(*results)


def solution(mesh):
    spec = P(None, ("ctx", "head"), None)
    return jax.shard_map(
        shards,
        mesh=mesh,
        in_specs=(spec,) * 5 + (P(),),
        out_specs=(spec,) * 3,
        check_vma=False,
    )
```

```python
import functools
import math

import jax
import jax.numpy as jnp
from jax import lax
from jax.experimental import pallas as pl
from jax.experimental.pallas import tpu as pltpu
from jax.sharding import PartitionSpec as P

HD = 128
NEG_FILL = -1e30
QMOST = 32
SCALE = HD ** (-0.5)
EXP2_SCALE = SCALE * math.log2(math.e)
MESH = pl.DeviceIdType.MESH
LAG = 2
UNROLL = 4


def remote(src, dst, send_sem, recv_sem, device):
    return pltpu.make_async_remote_copy(
        src_ref=src,
        dst_ref=dst,
        send_sem=send_sem,
        recv_sem=recv_sem,
        device_id=device,
        device_id_type=MESH,
    )


class Place:
    def __init__(self, ctx_count, head_count):
        self.nctx = ctx_count
        self.nh = head_count
        self.nz = ctx_count // 4
        self.half = self.nz // 2
        self.npair = ctx_count // 2
        self.ctx = lax.axis_index("ctx")
        self.h = lax.axis_index("head")
        self.c = lax.rem(self.ctx, 2)
        self.z = lax.rem(self.ctx // 2, self.nz)
        self.xh = self.ctx // (2 * self.nz)

    def zmod(self, z):
        return lax.rem(z + self.nz, self.nz)

    def block(self, xh, z, c):
        return (xh * self.nz + self.zmod(z)) * 2 + c

    def pair(self, xh, z):
        return xh * self.nz + self.zmod(z)

    def dev(self, xh, z, c):
        return (self.block(xh, z, c), self.h)

    def z_up(self):
        return self.dev(self.xh, self.z + 1, self.c)

    def z_down(self):
        return self.dev(self.xh, self.z - 1, self.c)

    def across(self):
        return self.block(1 - self.xh, self.z, self.c)

    def sibling(self):
        return self.dev(self.xh, self.z, 1 - self.c)

    def ctx_next(self):
        return (lax.rem(self.ctx + 1, self.nctx), self.h)

    def ctx_prev(self):
        return (lax.rem(self.ctx + self.nctx - 1, self.nctx), self.h)

    def head_peer(self, d):
        return lax.rem(self.h + d, self.nh)

    def far(self, q):
        return self.half - q // 4

    def way(self, q):
        return q % 2

    def xs(self, q):
        return (q // 2 + q) % 2

    def reach(self, q):
        return self.half - (self.way(q) + self.xs(q) + 1) % 2

    def z_of(self, q):
        return self.z + self.far(q) * (1 - 2 * self.way(q))

    def pair_of(self, q):
        return self.pair(self.xs(q), self.z_of(q))

    def block_of(self, q, c):
        return self.block(self.xs(q), self.z_of(q), c)

    def barrier(self):
        barrier = pltpu.get_barrier_semaphore()

        def greet(d, _):
            pl.semaphore_signal(
                barrier, inc=1, device_id=(self.ctx, self.head_peer(d)), device_id_type=MESH
            )
            return 0

        def greet_across(d, _):
            device = (self.across(), self.head_peer(d))
            pl.semaphore_signal(barrier, inc=1, device_id=device, device_id_type=MESH)
            return 0

        lax.fori_loop(1, self.nh, greet, 0)
        lax.fori_loop(0, self.nh, greet_across, 0)
        near = (
            self.z_up(),
            self.z_down(),
            self.sibling(),
            self.ctx_next(),
            self.ctx_prev(),
        )
        for device in near:
            pl.semaphore_signal(barrier, inc=1, device_id=device, device_id_type=MESH)
        pl.semaphore_wait(barrier, 2 * self.nh - 1 + len(near))


def nt_dot(a, b):
    return lax.dot_general(a, b, (((1,), (1,)), ((), ())), preferred_element_type=jnp.float32)


def nn_dot(a, b):
    return jnp.dot(a, b, preferred_element_type=jnp.float32)


def by_sublane(x):
    return x.reshape(x.shape[0] // 8, 8, x.shape[1])


def kernel(
    dims,
    len_ref,
    q_ref,
    k_ref,
    v_ref,
    o_ref,
    c_ref,
    gq,
    gk,
    gv,
    q_in,
    c_in,
    d_in,
    kvd,
    kvq,
    delta,
    delta_t,
    qs,
    cs,
    dd,
    turn,
    weights,
    peak,
    total,
    first_max,
    final_max,
    inverse,
    dqt,
    keys_t,
    low_p,
    low_s,
    dkv,
    dx,
    dq,
    from_core,
    sums,
    low_sums,
    chain,
    from_next,
    result,
    final,
    landed,
    owned,
    o_in,
    c_near,
    kv_send,
    kv_recv,
    q_send,
    q_recv,
    c_send,
    c_recv,
    d_send,
    d_recv,
    g_send,
    g_recv,
    s_send,
    s_recv,
    t_send,
    t_recv,
    core_send,
    core_recv,
    hop_send,
    hop_recv,
    n_send,
    n_recv,
    o_send,
    o_recv,
    r_send,
    r_recv,
    f_send,
    f_recv,
    local_sem,
):
    nctx, nh, tok, gw, bl, nhead = dims
    me = Place(nctx, nh)
    npair = me.npair
    last = 4 * me.half + 1
    group = gw // HD
    rows = group * bl
    tile = 2 * bl
    own_pair = me.ctx // 2
    chunk = min(256, rows)
    every = [pl.ds(r * chunk, chunk) for r in range(rows // chunk)]
    fetch_o = pltpu.make_async_copy(o_ref, o_in, local_sem.at[7])
    fetch_c = pltpu.make_async_copy(c_ref, c_near, local_sem.at[8])
    fetch_o.start()
    fetch_c.start()
    me.barrier()

    def rows_of(p):
        return pl.ds(pl.multiple_of(p * tok, tok), tok)

    own_rows = rows_of(me.h)

    def over_peers(make, act, across=False):
        def step(d, _):
            p = me.head_peer(d)
            made = make(d, p, (me.across() if across else me.ctx, p))
            for copy in made if isinstance(made, list) else [made]:
                act(copy)
            return 0

        lax.fori_loop(0 if across else 1, nh, step, 0)

    def sent_all(like, sem):
        remote(like, like, sem, sem, me.sibling()).wait_send()

    def received_all(like, sem):
        remote(like, like, sem, sem, me.sibling()).wait_recv()

    peers = nh - 1
    peer_rows = pl.ds(0, peers * tok)

    def start(copy):
        copy.start()

    kv_ref = (k_ref, v_ref)

    def kv_target(i, j):
        return kvq.at[i, 1, own_rows] if j else kvd.at[i, me.ctx, own_rows]

    def kv_copies(i, j):
        def made(d, p, device):
            cols = pl.ds(pl.multiple_of(p * HD, HD), HD)
            return remote(
                kv_ref[i].at[j, :, cols],
                kv_target(i, j),
                kv_send.at[i, j],
                kv_recv.at[i, j],
                device,
            )

        return made

    def kx_copies(i):
        def made(d, p, device):
            cols = pl.ds(pl.multiple_of(p * HD, HD), HD)
            return remote(
                kv_ref[i].at[0, :, cols], kv_target(i, 0), kv_send.at[i, 2], kv_recv.at[i, 2], device
            )

        return made

    def head_part(kind, ref, p):
        return ref.at[1 - kind, :, pl.ds(pl.multiple_of(p * gw, gw), gw)]

    def place_of(kind, ref):
        return ref.at[1 - kind, me.h]

    def row_copies(kind, source, target, send, recv):
        def made(d, p, device):
            return remote(
                head_part(kind, source, p),
                place_of(kind, target),
                send.at[kind],
                recv.at[kind],
                device,
            )

        return made

    def q_copies(kind):
        return row_copies(kind, q_ref, q_in, q_send, q_recv)

    def c_copies(kind):
        return row_copies(kind, c_ref, c_in, c_send, c_recv)

    def over_rows(copies, act):
        for kind in range(2):
            over_peers(copies(kind), act)

    def d_copy(d, p, device):
        return remote(
            delta_t.at[pl.ds(pl.multiple_of(p * group, group), group)],
            d_in.at[me.h],
            d_send,
            d_recv,
            device,
        )

    for i in range(2):
        over_peers(kv_copies(i, 0), start)
        over_peers(kx_copies(i), start, True)
    own_cols = pl.ds(pl.multiple_of(me.h * HD, HD), HD)
    locals_ = [
        pltpu.make_async_copy(kv_ref[i].at[j, :, own_cols], kv_target(i, j), local_sem.at[2 * i + j])
        for i in range(2)
        for j in range(2)
    ]
    own_q = [
        pltpu.make_async_copy(head_part(k, q_ref, me.h), place_of(k, q_in), local_sem.at[4 + k])
        for k in range(2)
    ]
    own_c = [
        pltpu.make_async_copy(head_part(k, c_ref, me.h), place_of(k, c_in), local_sem.at[9 + k])
        for k in range(2)
    ]
    for copy in locals_:
        copy.start()
    over_rows(q_copies, start)
    for i in range(2):
        over_peers(kv_copies(i, 1), start)
    for copy in own_q + own_c:
        copy.start()

    fetch_o.wait()
    fetch_c.wait()
    lanes = lax.broadcasted_iota(jnp.int32, (2, tok, HD), 2)

    def some_heads(j, acc):
        for u in range(UNROLL):
            at = pl.ds(pl.multiple_of((j * UNROLL + u) * HD, HD), HD)
            prod = c_near[:, :, at].astype(jnp.float32) * o_in[:, :, at].astype(jnp.float32)
            part = jnp.sum(prod, axis=-1, keepdims=True)
            acc = jnp.where(lanes == j * UNROLL + u, part, acc)
        return acc

    delta[...] = lax.fori_loop(
        0, nhead // UNROLL, some_heads, jnp.zeros((2, tok, HD), jnp.float32)
    )
    delta_t[:, 0 : 2 * tok] = jnp.transpose(delta[...].reshape(2 * tok, HD))
    over_peers(d_copy, start)
    d_in[me.h] = delta_t[pl.ds(pl.multiple_of(me.h * group, group), group)]

    n_sent = {"ring": 0, "core": 0}

    def ring_copy(i, b, f, way, xs, device):
        return remote(kvd.at[i, b], kvd.at[i, b], g_send, g_recv.at[i, f - 1, way, xs], device)

    def ring_send(i, b, f, way, xs):
        ring_copy(i, b, f, way, xs, me.z_down() if way == 0 else me.z_up()).start()
        n_sent["ring"] += 1

    def core_send_block(i, b, f):
        sem = s_recv.at[f if i == 0 else me.half + 1]
        remote(kvd.at[i, b], kvd.at[i, b], s_send, sem, me.sibling()).start()
        n_sent["core"] += 1

    tail = pl.ds(bl - QMOST, QMOST)
    tail_copy = remote(kvq.at[:, 1, tail], kvq.at[:, 0, tail], t_send, t_recv, me.ctx_next())

    def gather_own(i, b, xs):
        ring_send(i, b, 1, 1, xs)
        ring_send(i, b, 1, 0, xs)

    def gather_step(f, kv=(0, 1)):
        qs_at = [q for q in range(last - 1, 1, -1) if me.far(q) == f]
        for i in kv:
            for q in qs_at:
                b, way, xs = me.block_of(q, me.c), me.way(q), me.xs(q)
                ring_copy(i, b, f, way, xs, me.sibling()).wait_recv()
                if f < me.reach(q):
                    ring_send(i, b, f + 1, way, xs)
                core_send_block(i, b, f)

    for i in range(2):
        locals_[2 * i].wait()
        received_all(kvd.at[i, me.ctx, peer_rows], kv_recv.at[i, 0])
        gather_own(i, me.ctx, me.xh)
        received_all(kvd.at[i, me.across()], kv_recv.at[i, 2])
        gather_own(i, me.across(), 1 - me.xh)
        core_send_block(i, me.ctx, 0)
        core_send_block(i, me.across(), 0)

    count = len_ref.shape[1]
    lens = jnp.broadcast_to(len_ref[...].astype(jnp.float32), (8, count)).astype(jnp.bfloat16)
    i0 = lax.broadcasted_iota(jnp.int32, (count, count), 0)
    i1 = lax.broadcasted_iota(jnp.int32, (count, count), 1)
    before = jnp.where(i0 < i1, 1.0, 0.0).astype(jnp.bfloat16)
    after = jnp.where(i1 < i0, 1.0, 0.0).astype(jnp.bfloat16)
    starts_row = nn_dot(lens, before)[0:1, :]
    starts_col = nt_dot(after, lens)[:, 0:1]
    row_at = lax.broadcasted_iota(jnp.int32, (1, chunk), 1) % bl
    key_at = lax.broadcasted_iota(jnp.int32, (tile, 1), 0) - bl
    row_off = (row_at + me.ctx * bl).astype(jnp.float32)
    key_off = (key_at + me.ctx * bl).astype(jnp.float32)
    row_seg = jnp.sum(jnp.where(starts_col <= row_off, 1.0, 0.0), axis=0, keepdims=True)
    key_seg = jnp.sum(jnp.where(starts_row <= key_off, 1.0, 0.0), axis=1, keepdims=True)
    question_mask = (key_at <= row_at) & (key_seg == row_seg)
    doc_key = lax.broadcasted_iota(jnp.int32, (tile, 1), 0) + (own_pair * 2 - me.ctx) * bl
    doc_mask = doc_key <= row_at

    peak[...] = jnp.full(peak.shape, NEG_FILL, jnp.float32)
    total[...] = jnp.zeros(total.shape, jnp.float32)
    dqt[...] = jnp.zeros(dqt.shape, jnp.float32)

    def doc_kv(i, t):
        return kvd[i, pl.ds(2 * t, 2)].reshape(tile, HD)

    def question_kv(i):
        at = lax.broadcasted_iota(jnp.int32, (bl, HD), 0)
        prev = jnp.where(at >= bl - QMOST, kvq[i, 0].astype(jnp.float32), 0.0)
        return jnp.concatenate([prev.astype(jnp.bfloat16), kvq[i, 1]], axis=0)

    def scores_of(s, keys, mask, cols):
        scores = nt_dot(keys, qs[s, cols, :])
        return scores if mask is None else jnp.where(mask, scores, NEG_FILL)

    def peak_sweep(s, keys, mask, at):
        for cols in at:
            scores = by_sublane(scores_of(s, keys, mask, cols))
            peak[s, :, cols] = jnp.maximum(peak[s, :, cols], jnp.max(scores, axis=0))

    def weight_sweep(s, slot, keys, mask, at, known):
        for cols in at:
            scores = scores_of(s, keys, mask, cols)
            part = jnp.exp2((scores - known[s, 0:1, cols]) * EXP2_SCALE)
            weights[slot, :, cols] = part
            total[s, :, cols] = total[s, :, cols] + jnp.sum(by_sublane(part), axis=0)

    def on_pair(t, sweep):
        sweep(1, None, every)

        @pl.when(t < own_pair)
        def _():
            sweep(0, None, every)

        @pl.when(t == own_pair)
        def _():
            sweep(0, doc_mask, every)

    def sort_rows(target, source, s):
        for g in range(group):
            cols = slice(g * HD, (g + 1) * HD)
            target[s, g * bl : (g + 1) * bl, :] = source[s, :, :, cols].reshape(bl, HD)

    def peaks(f):
        count = 4 if 0 < f < me.half else 2
        received_all(kvd.at[0, pl.ds(0, count)], s_recv.at[f])

        def step(i, _):
            q = last - i if f == 0 else last - 2 - 4 * (f - 1) - i
            t = me.pair_of(q)
            keys = doc_kv(0, t)

            def sweep(s, mask, at):
                peak_sweep(s, keys, mask, at)

            on_pair(t, sweep)
            return 0

        lax.fori_loop(0, count, step, 0)

    def weigh(low, high, known):
        def step(q, _):
            t = me.pair_of(q)
            keys = doc_kv(0, t)

            def sweep(s, mask, at):
                weight_sweep(s, s * npair + t, keys, mask, at, known)

            on_pair(t, sweep)
            return 0

        lax.fori_loop(low, high, step, 0)

    gather_step(1, (0,))
    for i in range(2):
        locals_[2 * i + 1].wait()
        received_all(kvq.at[i, 1, peer_rows], kv_recv.at[i, 1])
    tail_copy.start()
    gather_step(2, (0,))
    gather_step(1, (1,))
    for copy in own_q:
        copy.wait()
    for kind in range(2):
        received_all(q_in.at[kind, pl.ds(0, peers)], q_recv.at[kind])
    over_rows(c_copies, start)
    for s in range(2):
        sort_rows(qs, q_in, s)

    peaks(0)
    tail_copy.wait_recv()
    peak_sweep(1, question_kv(0), question_mask, every)
    for f in range(1, me.half - 1):
        if f + 1 > 2:
            gather_step(f + 1, (0,))
            gather_step(f, (1,))
        peaks(f)
    for s in range(2):
        first_max[s] = jnp.max(peak[s], axis=0, keepdims=True)
    weight_sweep(1, 2 * npair, question_kv(0), question_mask, every, first_max)
    near = max(8, 4 * me.half - 4)
    weigh(near, last + 1, first_max)
    if me.half > 2:
        gather_step(me.half, (0,))
        gather_step(me.half - 1, (1,))
    weigh(8, near, first_max)
    peaks(me.half - 1)
    peaks(me.half)
    gather_step(me.half, (1,))
    for s in range(2):
        final_max[s] = jnp.max(peak[s], axis=0, keepdims=True)
        total[s] = total[s] * jnp.exp2((first_max[s] - final_max[s]) * EXP2_SCALE)
    weigh(2, 8, final_max)
    for s in range(2):
        whole = 1.0 / jnp.sum(total[s], axis=0, keepdims=True)
        nearer = whole * jnp.exp2((first_max[s] - final_max[s]) * EXP2_SCALE)
        inverse[0, s] = whole
        inverse[1, s] = nearer
        inverse[2, s] = nearer

    received_all(kvd.at[1, pl.ds(0, npair)], s_recv.at[me.half + 1])

    for copy in own_c:
        copy.wait()
    for kind in range(2):
        received_all(c_in.at[kind, pl.ds(0, peers)], c_recv.at[kind])
    received_all(d_in.at[pl.ds(0, peers)], d_recv)
    for s in range(2):
        sort_rows(cs, c_in, s)
        for j in range(nh):
            turn[:, j * tok : (j + 1) * tok] = d_in[j, :, s * tok : (s + 1) * tok]
        for g in range(group):
            dd[s, 0:1, g * bl : (g + 1) * bl] = turn[g : g + 1, :]

    def low_chunk(s, slot, cols, values, scale_at):
        prob = weights[slot, :, cols] * inverse[scale_at, s, 0:1, cols]
        d_prob = nt_dot(values, cs[s, cols, :])
        low_p[s, :, cols] = prob.astype(jnp.bfloat16)
        low_s[s, :, cols] = (prob * (d_prob - dd[s, 0:1, cols])).astype(jnp.bfloat16)

    def d_value(s):
        return nn_dot(low_p[s], cs[s])

    def d_key(s):
        return nn_dot(low_s[s], qs[s])

    def d_query(s):
        dqt[s] += nn_dot(keys_t[...], low_s[s])

    def backward(s, slot, values, scale_at):
        for cols in every:
            low_chunk(s, slot, cols, values, scale_at)
        made = d_key(s), d_value(s)
        d_query(s)
        return made

    def backward_both(t, values, scale_at):
        for cols in every:
            low_chunk(1, npair + t, cols, values, scale_at)
        todo = [d_key, d_value, d_query]
        made = []
        for cols in every:
            low_chunk(0, t, cols, values, scale_at)
            if todo:
                made.append(todo.pop(0)(1))
        for product in todo:
            made.append(product(1))
        made = made[0] + d_key(0), made[1] + d_value(0)
        d_query(0)
        return made

    def turn_keys(keys):
        keys_t[...] = jnp.transpose(keys.astype(jnp.float32)).astype(jnp.bfloat16)

    def put(t, i, value):
        for c in range(2):
            dkv[t, i, c] = value[c * bl : (c + 1) * bl]

    def core_copy(t):
        return remote(
            dkv.at[t, :, 1 - me.c],
            from_core.at[t],
            core_send,
            core_recv.at[t],
            me.sibling(),
        )

    def hop_copy(way, xs, f):
        return remote(
            low_sums.at[me.pair(xs, me.z + f * (1 - 2 * way))],
            chain.at[way, xs, f - 1],
            hop_send,
            hop_recv.at[way, xs, f - 1],
            me.dev(me.xh, me.z + 1 - 2 * way, me.c),
        )

    def serve(q):
        f, way, xs, t = me.far(q), me.way(q), me.xs(q), me.pair_of(q)
        core_copy(t).wait_recv()
        sums[t] = dkv[t, :, me.c] + from_core[t]

        @pl.when((f > 0) & (f < me.reach(q)))
        def _():
            hop_copy(way, xs, f + 1).wait_recv()
            sums[t] = sums[t] + chain[way, xs, f].astype(jnp.float32)

        @pl.when(f > 0)
        def _():
            low_sums[t] = sums[t].astype(jnp.bfloat16)
            hop_copy(way, xs, f).start()

    turn_keys(question_kv(0))
    dx[0], dx[1] = backward(1, 2 * npair, question_kv(1), 1)
    next_copy = remote(dx.at[:, tail], from_next, n_send, n_recv, me.ctx_prev())
    next_copy.start()

    def r_copies(d, p, device):
        return [
            remote(
                result.at[i, rows_of(p)],
                (gk, gv)[i].at[1, :, own_cols],
                r_send.at[i],
                r_recv.at[i],
                device,
            )
            for i in range(2)
        ]

    own_r = [
        pltpu.make_async_copy(
            result.at[i, own_rows], (gk, gv)[i].at[1, :, own_cols], local_sem.at[i]
        )
        for i in range(2)
    ]

    def send_questions():
        next_copy.wait_recv()
        for i in range(2):
            factor = SCALE if i == 0 else 1.0
            result[i, 0 : bl - QMOST] = dx[i, bl : 2 * bl - QMOST] * factor
            result[i, bl - QMOST : bl] = (
                dx[i, 2 * bl - QMOST : 2 * bl] + from_next[i]
            ) * factor
        over_peers(r_copies, start)
        for copy in own_r:
            copy.start()

    def backward_pair(n, _):
        q = n + 2
        t = me.pair_of(q)
        turn_keys(doc_kv(0, t))
        @pl.when(t > own_pair)
        def _():
            for i, value in enumerate(backward(1, npair + t, doc_kv(1, t), q // 8)):
                put(t, i, value)

        @pl.when(t <= own_pair)
        def _():
            for i, value in enumerate(backward_both(t, doc_kv(1, t), q // 8)):
                put(t, i, value)

        core_copy(t).start()

        @pl.when(n >= LAG)
        def _():
            serve(q - LAG)

        @pl.when(n == npair // 2)
        def _():
            send_questions()

        return 0

    lax.fori_loop(0, npair, backward_pair, 0)

    for s in range(2):
        for g in range(group):
            part = jnp.transpose(dqt[s, :, g * bl : (g + 1) * bl])
            dq[s, :, g * HD : (g + 1) * HD] = (part * SCALE).astype(jnp.bfloat16)

    def out_part(kind, p):
        return dq.at[1 - kind, rows_of(p)]

    def out_copies(kind):
        def made(d, p, device):
            return remote(
                out_part(kind, p),
                head_part(kind, gq, me.h),
                o_send.at[kind],
                o_recv.at[kind],
                device,
            )

        return made

    own_out = [
        pltpu.make_async_copy(out_part(k, me.h), head_part(k, gq, me.h), local_sem.at[4 + k])
        for k in range(2)
    ]
    over_rows(out_copies, start)
    for copy in own_out:
        copy.start()

    def serve_rest(n, _):
        serve(n + 2)
        return 0

    lax.fori_loop(npair - LAG, npair, serve_rest, 0)

    def final_copies(kind):
        def made(d, p, device):
            return [
                remote(
                    final.at[kind, i, rows_of(p)],
                    landed.at[kind, i, me.h],
                    f_send.at[kind, i],
                    f_recv.at[kind, i],
                    device,
                )
                for i in range(2)
            ]

        return made

    for way in range(2):
        for xs in range(2):
            hop_copy(way, xs, 1).wait_recv()
    for kind in (1, 0):
        xs = me.xh if kind == 0 else 1 - me.xh
        t = me.pair(xs, me.z)
        for i in range(2):
            factor = SCALE if i == 0 else 1.0
            final[kind, i] = (
                sums[t, i]
                + chain[0, xs, 0, i].astype(jnp.float32)
                + chain[1, xs, 0, i].astype(jnp.float32)
            ) * factor
        over_peers(final_copies(kind), start, kind == 1)
    for i in range(2):
        landed[0, i, me.h] = final[0, i, own_rows]
    for i in range(2):
        received_all(landed.at[0, i, pl.ds(0, peers)], f_recv.at[0, i])
        received_all(landed.at[1, i], f_recv.at[1, i])
    for i in range(2):
        for h in range(nh):
            owned[i, :, h * HD : (h + 1) * HD] = landed[0, i, h] + landed[1, i, h]
    last_out = [
        pltpu.make_async_copy(owned.at[i], (gk, gv)[i].at[0], local_sem.at[2 + i])
        for i in range(2)
    ]
    for copy in last_out:
        copy.start()

    sent_all(kvd.at[0, pl.ds(0, n_sent["ring"])], g_send)
    sent_all(kvd.at[0, pl.ds(0, n_sent["core"])], s_send)
    for i in range(2):
        sent_all(kvd.at[i, 0, peer_rows], kv_send.at[i, 0])
        sent_all(kvd.at[i, 0, peer_rows], kv_send.at[i, 1])
        sent_all(kvd.at[i, 0], kv_send.at[i, 2])
        sent_all(result.at[i, peer_rows], r_send.at[i])
        sent_all(final.at[0, i, peer_rows], f_send.at[0, i])
        sent_all(final.at[1, i], f_send.at[1, i])
        sent_all(q_in.at[i, pl.ds(0, peers)], q_send.at[i])
        sent_all(c_in.at[i, pl.ds(0, peers)], c_send.at[i])
        sent_all(dq.at[i, peer_rows], o_send.at[i])
        received_all(dq.at[i, peer_rows], o_recv.at[i])
        received_all(result.at[i, peer_rows], r_recv.at[i])
    sent_all(d_in.at[pl.ds(0, peers)], d_send)
    tail_copy.wait_send()
    sent_all(from_core, core_send)
    sent_all(low_sums.at[pl.ds(0, 4 * me.half - 2)], hop_send)
    next_copy.wait_send()
    for copy in own_out + own_r + last_out:
        copy.wait()


def place_results(*refs):
    sources, targets, held, sem = refs[:3], refs[3:6], refs[6:9], refs[9]
    reads = [pltpu.make_async_copy(sources[i], held[i], sem.at[0, i]) for i in range(3)]
    writes = [pltpu.make_async_copy(held[i], targets[i], sem.at[1, i]) for i in range(3)]
    for copy in reads:
        copy.start()
    for i in range(3):
        reads[i].wait()
        writes[i].start()
    for copy in writes:
        copy.wait()


def shards(queries, keys, values, outputs, cotangent, lengths):
    nctx, nh = lax.axis_size("ctx"), lax.axis_size("head")
    tok = queries.shape[1]
    gw = queries.shape[2] // nh
    bl = tok * nh
    nhead = queries.shape[2] // HD
    dims = (nctx, nh, tok, gw, bl, nhead)
    npair = nctx // 2
    group = gw // HD
    rows = group * bl
    hbm = pl.BlockSpec(memory_space=pl.ANY)
    vmem = pl.BlockSpec(memory_space=pltpu.VMEM)
    dma = pltpu.SemaphoreType.DMA
    space = pltpu.VMEM
    f32, b16 = jnp.float32, jnp.bfloat16
    shape = jax.ShapeDtypeStruct
    hops = nctx // 8
    made = (
        shape((2, tok, nh * gw), b16),
        shape((2, tok, nh * HD), f32),
        shape((2, tok, nh * HD), f32),
    )
    results = pl.pallas_call(
        functools.partial(kernel, dims),
        out_shape=made,
        in_specs=[vmem, hbm, hbm, hbm, hbm, hbm],
        out_specs=[hbm] * 3,
        scratch_shapes=[
            space((2, nh, tok, gw), b16),
            space((2, nh, tok, gw), b16),
            space((nh, group, HD), f32),
            space((2, nctx, bl, HD), b16),
            space((2, 2, bl, HD), b16),
            space((2, tok, HD), f32),
            space((HD, HD), f32),
            space((2, rows, HD), b16),
            space((2, rows, HD), b16),
            space((2, 1, rows), f32),
            space((group, bl), f32),
            space((2 * npair + 1, 2 * bl, rows), f32),
            space((2, 8, rows), f32),
            space((2, 8, rows), f32),
            space((2, 1, rows), f32),
            space((2, 1, rows), f32),
            space((3, 2, 1, rows), f32),
            space((2, HD, rows), f32),
            space((HD, 2 * bl), b16),
            space((2, 2 * bl, rows), b16),
            space((2, 2 * bl, rows), b16),
            space((npair, 2, 2, bl, HD), f32),
            space((2, 2 * bl, HD), f32),
            space((2, bl, gw), b16),
            space((npair, 2, bl, HD), f32),
            space((npair, 2, bl, HD), f32),
            space((npair, 2, bl, HD), b16),
            space((2, 2, hops, 2, bl, HD), b16),
            space((2, QMOST, HD), f32),
            space((2, bl, HD), f32),
            space((2, 2, bl, HD), f32),
            space((2, 2, nh, tok, HD), f32),
            space((2, tok, nh * HD), f32),
            space((2, tok, nh * gw), b16),
            space((2, tok, nh * gw), b16),
            dma((2, 3)),
            dma((2, 3)),
            dma((2,)),
            dma((2,)),
            dma((2,)),
            dma((2,)),
            dma,
            dma,
            dma,
            dma((2, hops, 2, 2)),
            dma,
            dma((hops + 2,)),
            dma,
            dma,
            dma,
            dma((npair,)),
            dma,
            dma((2, 2, hops)),
            dma,
            dma,
            dma((2,)),
            dma((2,)),
            dma((2,)),
            dma((2,)),
            dma((2, 2)),
            dma((2, 2)),
            dma((11,)),
        ],
        compiler_params=pltpu.CompilerParams(
            collective_id=0, has_side_effects=True, vmem_limit_bytes=60 * 2**20
        ),
        name="attention_backward",
    )(lengths.reshape(1, -1), queries, keys, values, outputs, cotangent)
    return pl.pallas_call(
        place_results,
        out_shape=made,
        in_specs=[hbm] * 3,
        out_specs=[hbm] * 3,
        scratch_shapes=[space(m.shape, m.dtype) for m in made] + [dma((2, 3))],
        name="place_results",
    )(*results)


def solution(mesh):
    spec = P(None, ("ctx", "head"), None)
    return jax.shard_map(
        shards,
        mesh=mesh,
        in_specs=(spec,) * 5 + (P(),),
        out_specs=(spec,) * 3,
        check_vma=False,
    )
```

```python
import functools
import math

import jax
import jax.numpy as jnp
from jax import lax
from jax.experimental import pallas as pl
from jax.experimental.pallas import tpu as pltpu
from jax.sharding import PartitionSpec as P

HD = 128
NEG_FILL = -1e30
QMOST = 32
SCALE = HD ** (-0.5)
EXP2_SCALE = SCALE * math.log2(math.e)
MESH = pl.DeviceIdType.MESH
LAG = 2
UNROLL = 8


def remote(src, dst, send_sem, recv_sem, device):
    return pltpu.make_async_remote_copy(
        src_ref=src,
        dst_ref=dst,
        send_sem=send_sem,
        recv_sem=recv_sem,
        device_id=device,
        device_id_type=MESH,
    )


class Place:
    def __init__(self, ctx_count, head_count):
        self.nctx = ctx_count
        self.nh = head_count
        self.nz = ctx_count // 4
        self.half = self.nz // 2
        self.npair = ctx_count // 2
        self.ctx = lax.axis_index("ctx")
        self.h = lax.axis_index("head")
        self.c = lax.rem(self.ctx, 2)
        self.z = lax.rem(self.ctx // 2, self.nz)
        self.xh = self.ctx // (2 * self.nz)

    def zmod(self, z):
        return lax.rem(z + self.nz, self.nz)

    def block(self, xh, z, c):
        return (xh * self.nz + self.zmod(z)) * 2 + c

    def pair(self, xh, z):
        return xh * self.nz + self.zmod(z)

    def dev(self, xh, z, c):
        return (self.block(xh, z, c), self.h)

    def z_up(self):
        return self.dev(self.xh, self.z + 1, self.c)

    def z_down(self):
        return self.dev(self.xh, self.z - 1, self.c)

    def across(self):
        return self.block(1 - self.xh, self.z, self.c)

    def sibling(self):
        return self.dev(self.xh, self.z, 1 - self.c)

    def ctx_next(self):
        return (lax.rem(self.ctx + 1, self.nctx), self.h)

    def ctx_prev(self):
        return (lax.rem(self.ctx + self.nctx - 1, self.nctx), self.h)

    def head_peer(self, d):
        return lax.rem(self.h + d, self.nh)

    def far(self, q):
        return self.half - q // 4

    def way(self, q):
        return q % 2

    def xs(self, q):
        return (q // 2 + q) % 2

    def reach(self, q):
        return self.half - (self.way(q) + self.xs(q) + 1) % 2

    def z_of(self, q):
        return self.z + self.far(q) * (1 - 2 * self.way(q))

    def pair_of(self, q):
        return self.pair(self.xs(q), self.z_of(q))

    def block_of(self, q, c):
        return self.block(self.xs(q), self.z_of(q), c)

    def barrier(self):
        barrier = pltpu.get_barrier_semaphore()

        def greet(d, _):
            pl.semaphore_signal(
                barrier, inc=1, device_id=(self.ctx, self.head_peer(d)), device_id_type=MESH
            )
            return 0

        def greet_across(d, _):
            device = (self.across(), self.head_peer(d))
            pl.semaphore_signal(barrier, inc=1, device_id=device, device_id_type=MESH)
            return 0

        lax.fori_loop(1, self.nh, greet, 0)
        lax.fori_loop(0, self.nh, greet_across, 0)
        near = (
            self.z_up(),
            self.z_down(),
            self.sibling(),
            self.ctx_next(),
            self.ctx_prev(),
        )
        for device in near:
            pl.semaphore_signal(barrier, inc=1, device_id=device, device_id_type=MESH)
        pl.semaphore_wait(barrier, 2 * self.nh - 1 + len(near))


def nt_dot(a, b):
    return lax.dot_general(a, b, (((1,), (1,)), ((), ())), preferred_element_type=jnp.float32)


def nn_dot(a, b):
    return jnp.dot(a, b, preferred_element_type=jnp.float32)


def by_sublane(x):
    return x.reshape(x.shape[0] // 8, 8, x.shape[1])


def kernel(
    dims,
    len_ref,
    q_ref,
    k_ref,
    v_ref,
    o_ref,
    c_ref,
    gq,
    gk,
    gv,
    q_in,
    c_in,
    d_in,
    kvd,
    kvq,
    delta,
    delta_t,
    qs,
    cs,
    dd,
    turn,
    weights,
    peak,
    total,
    first_max,
    final_max,
    inverse,
    dqt,
    keys_t,
    low_p,
    low_s,
    dkv,
    dx,
    dq,
    from_core,
    sums,
    low_sums,
    chain,
    from_next,
    result,
    final,
    landed,
    owned,
    o_in,
    c_near,
    kv_send,
    kv_recv,
    q_send,
    q_recv,
    c_send,
    c_recv,
    d_send,
    d_recv,
    g_send,
    g_recv,
    s_send,
    s_recv,
    t_send,
    t_recv,
    core_send,
    core_recv,
    hop_send,
    hop_recv,
    n_send,
    n_recv,
    o_send,
    o_recv,
    r_send,
    r_recv,
    f_send,
    f_recv,
    local_sem,
):
    nctx, nh, tok, gw, bl, nhead = dims
    me = Place(nctx, nh)
    npair = me.npair
    last = 4 * me.half + 1
    group = gw // HD
    rows = group * bl
    tile = 2 * bl
    own_pair = me.ctx // 2
    chunk = min(256, rows)
    every = [pl.ds(r * chunk, chunk) for r in range(rows // chunk)]
    fetch_o = pltpu.make_async_copy(o_ref, o_in, local_sem.at[7])
    fetch_c = pltpu.make_async_copy(c_ref, c_near, local_sem.at[8])
    fetch_o.start()
    fetch_c.start()
    me.barrier()

    def rows_of(p):
        return pl.ds(pl.multiple_of(p * tok, tok), tok)

    own_rows = rows_of(me.h)

    def over_peers(make, act, across=False):
        def step(d, _):
            p = me.head_peer(d)
            made = make(d, p, (me.across() if across else me.ctx, p))
            for copy in made if isinstance(made, list) else [made]:
                act(copy)
            return 0

        lax.fori_loop(0 if across else 1, nh, step, 0)

    def sent_all(like, sem):
        remote(like, like, sem, sem, me.sibling()).wait_send()

    def received_all(like, sem):
        remote(like, like, sem, sem, me.sibling()).wait_recv()

    peers = nh - 1
    peer_rows = pl.ds(0, peers * tok)

    def start(copy):
        copy.start()

    kv_ref = (k_ref, v_ref)

    def kv_target(i, j):
        return kvq.at[i, 1, own_rows] if j else kvd.at[i, me.ctx, own_rows]

    def kv_copies(i, j):
        def made(d, p, device):
            cols = pl.ds(pl.multiple_of(p * HD, HD), HD)
            return remote(
                kv_ref[i].at[j, :, cols],
                kv_target(i, j),
                kv_send.at[i, j],
                kv_recv.at[i, j],
                device,
            )

        return made

    def kx_copies(i):
        def made(d, p, device):
            cols = pl.ds(pl.multiple_of(p * HD, HD), HD)
            return remote(
                kv_ref[i].at[0, :, cols], kv_target(i, 0), kv_send.at[i, 2], kv_recv.at[i, 2], device
            )

        return made

    def head_part(kind, ref, p):
        return ref.at[1 - kind, :, pl.ds(pl.multiple_of(p * gw, gw), gw)]

    def place_of(kind, ref):
        return ref.at[1 - kind, me.h]

    def row_copies(kind, source, target, send, recv):
        def made(d, p, device):
            return remote(
                head_part(kind, source, p),
                place_of(kind, target),
                send.at[kind],
                recv.at[kind],
                device,
            )

        return made

    def q_copies(kind):
        return row_copies(kind, q_ref, q_in, q_send, q_recv)

    def c_copies(kind):
        return row_copies(kind, c_ref, c_in, c_send, c_recv)

    def over_rows(copies, act):
        for kind in range(2):
            over_peers(copies(kind), act)

    def d_copy(d, p, device):
        return remote(
            delta_t.at[pl.ds(pl.multiple_of(p * group, group), group)],
            d_in.at[me.h],
            d_send,
            d_recv,
            device,
        )

    for i in range(2):
        over_peers(kv_copies(i, 0), start)
        over_peers(kx_copies(i), start, True)
    own_cols = pl.ds(pl.multiple_of(me.h * HD, HD), HD)
    locals_ = [
        pltpu.make_async_copy(kv_ref[i].at[j, :, own_cols], kv_target(i, j), local_sem.at[2 * i + j])
        for i in range(2)
        for j in range(2)
    ]
    own_q = [
        pltpu.make_async_copy(head_part(k, q_ref, me.h), place_of(k, q_in), local_sem.at[4 + k])
        for k in range(2)
    ]
    own_c = [
        pltpu.make_async_copy(head_part(k, c_ref, me.h), place_of(k, c_in), local_sem.at[9 + k])
        for k in range(2)
    ]
    for copy in locals_:
        copy.start()
    over_rows(q_copies, start)
    for i in range(2):
        over_peers(kv_copies(i, 1), start)
    for copy in own_q + own_c:
        copy.start()

    fetch_o.wait()
    fetch_c.wait()
    lanes = lax.broadcasted_iota(jnp.int32, (2, tok, HD), 2)

    def some_heads(j, acc):
        for u in range(UNROLL):
            at = pl.ds(pl.multiple_of((j * UNROLL + u) * HD, HD), HD)
            prod = c_near[:, :, at].astype(jnp.float32) * o_in[:, :, at].astype(jnp.float32)
            part = jnp.sum(prod, axis=-1, keepdims=True)
            acc = jnp.where(lanes == j * UNROLL + u, part, acc)
        return acc

    delta[...] = lax.fori_loop(
        0, nhead // UNROLL, some_heads, jnp.zeros((2, tok, HD), jnp.float32)
    )
    delta_t[:, 0 : 2 * tok] = jnp.transpose(delta[...].reshape(2 * tok, HD))
    over_peers(d_copy, start)
    d_in[me.h] = delta_t[pl.ds(pl.multiple_of(me.h * group, group), group)]

    n_sent = {"ring": 0, "core": 0}

    def ring_copy(i, b, f, way, xs, device):
        return remote(kvd.at[i, b], kvd.at[i, b], g_send, g_recv.at[i, f - 1, way, xs], device)

    def ring_send(i, b, f, way, xs):
        ring_copy(i, b, f, way, xs, me.z_down() if way == 0 else me.z_up()).start()
        n_sent["ring"] += 1

    def core_send_block(i, b, f):
        sem = s_recv.at[f if i == 0 else me.half + 1]
        remote(kvd.at[i, b], kvd.at[i, b], s_send, sem, me.sibling()).start()
        n_sent["core"] += 1

    tail = pl.ds(bl - QMOST, QMOST)
    tail_copy = remote(kvq.at[:, 1, tail], kvq.at[:, 0, tail], t_send, t_recv, me.ctx_next())

    def gather_own(i, b, xs):
        ring_send(i, b, 1, 1, xs)
        ring_send(i, b, 1, 0, xs)

    def gather_step(f, kv=(0, 1)):
        qs_at = [q for q in range(last - 1, 1, -1) if me.far(q) == f]
        for i in kv:
            for q in qs_at:
                b, way, xs = me.block_of(q, me.c), me.way(q), me.xs(q)
                ring_copy(i, b, f, way, xs, me.sibling()).wait_recv()
                if f < me.reach(q):
                    ring_send(i, b, f + 1, way, xs)
                core_send_block(i, b, f)

    for i in range(2):
        locals_[2 * i].wait()
        received_all(kvd.at[i, me.ctx, peer_rows], kv_recv.at[i, 0])
        gather_own(i, me.ctx, me.xh)
        received_all(kvd.at[i, me.across()], kv_recv.at[i, 2])
        gather_own(i, me.across(), 1 - me.xh)
        core_send_block(i, me.ctx, 0)
        core_send_block(i, me.across(), 0)

    count = len_ref.shape[1]
    lens = jnp.broadcast_to(len_ref[...].astype(jnp.float32), (8, count)).astype(jnp.bfloat16)
    i0 = lax.broadcasted_iota(jnp.int32, (count, count), 0)
    i1 = lax.broadcasted_iota(jnp.int32, (count, count), 1)
    before = jnp.where(i0 < i1, 1.0, 0.0).astype(jnp.bfloat16)
    after = jnp.where(i1 < i0, 1.0, 0.0).astype(jnp.bfloat16)
    starts_row = nn_dot(lens, before)[0:1, :]
    starts_col = nt_dot(after, lens)[:, 0:1]
    row_at = lax.broadcasted_iota(jnp.int32, (1, chunk), 1) % bl
    key_at = lax.broadcasted_iota(jnp.int32, (tile, 1), 0) - bl
    row_off = (row_at + me.ctx * bl).astype(jnp.float32)
    key_off = (key_at + me.ctx * bl).astype(jnp.float32)
    row_seg = jnp.sum(jnp.where(starts_col <= row_off, 1.0, 0.0), axis=0, keepdims=True)
    key_seg = jnp.sum(jnp.where(starts_row <= key_off, 1.0, 0.0), axis=1, keepdims=True)
    question_mask = (key_at <= row_at) & (key_seg == row_seg)
    doc_key = lax.broadcasted_iota(jnp.int32, (tile, 1), 0) + (own_pair * 2 - me.ctx) * bl
    doc_mask = doc_key <= row_at

    peak[...] = jnp.full(peak.shape, NEG_FILL, jnp.float32)
    total[...] = jnp.zeros(total.shape, jnp.float32)
    dqt[...] = jnp.zeros(dqt.shape, jnp.float32)

    def doc_kv(i, t):
        return kvd[i, pl.ds(2 * t, 2)].reshape(tile, HD)

    def question_kv(i):
        at = lax.broadcasted_iota(jnp.int32, (bl, HD), 0)
        prev = jnp.where(at >= bl - QMOST, kvq[i, 0].astype(jnp.float32), 0.0)
        return jnp.concatenate([prev.astype(jnp.bfloat16), kvq[i, 1]], axis=0)

    def scores_of(s, keys, mask, cols):
        scores = nt_dot(keys, qs[s, cols, :])
        return scores if mask is None else jnp.where(mask, scores, NEG_FILL)

    def peak_sweep(s, keys, mask, at):
        for cols in at:
            scores = by_sublane(scores_of(s, keys, mask, cols))
            peak[s, :, cols] = jnp.maximum(peak[s, :, cols], jnp.max(scores, axis=0))

    def weight_sweep(s, slot, keys, mask, at, known):
        for cols in at:
            scores = scores_of(s, keys, mask, cols)
            part = jnp.exp2((scores - known[s, 0:1, cols]) * EXP2_SCALE)
            weights[slot, :, cols] = part
            total[s, :, cols] = total[s, :, cols] + jnp.sum(by_sublane(part), axis=0)

    def on_pair(t, sweep):
        sweep(1, None, every)

        @pl.when(t < own_pair)
        def _():
            sweep(0, None, every)

        @pl.when(t == own_pair)
        def _():
            sweep(0, doc_mask, every)

    def sort_rows(target, source, s):
        for g in range(group):
            cols = slice(g * HD, (g + 1) * HD)
            target[s, g * bl : (g + 1) * bl, :] = source[s, :, :, cols].reshape(bl, HD)

    def peaks(f):
        count = 4 if 0 < f < me.half else 2
        received_all(kvd.at[0, pl.ds(0, count)], s_recv.at[f])

        def step(i, _):
            q = last - i if f == 0 else last - 2 - 4 * (f - 1) - i
            t = me.pair_of(q)
            keys = doc_kv(0, t)

            def sweep(s, mask, at):
                peak_sweep(s, keys, mask, at)

            on_pair(t, sweep)
            return 0

        lax.fori_loop(0, count, step, 0)

    def weigh(low, high, known):
        def step(q, _):
            t = me.pair_of(q)
            keys = doc_kv(0, t)

            def sweep(s, mask, at):
                weight_sweep(s, s * npair + t, keys, mask, at, known)

            on_pair(t, sweep)
            return 0

        lax.fori_loop(low, high, step, 0)

    gather_step(1, (0,))
    for i in range(2):
        locals_[2 * i + 1].wait()
        received_all(kvq.at[i, 1, peer_rows], kv_recv.at[i, 1])
    tail_copy.start()
    gather_step(2, (0,))
    gather_step(1, (1,))
    for copy in own_q:
        copy.wait()
    for kind in range(2):
        received_all(q_in.at[kind, pl.ds(0, peers)], q_recv.at[kind])
    over_rows(c_copies, start)
    for s in range(2):
        sort_rows(qs, q_in, s)

    peaks(0)
    tail_copy.wait_recv()
    peak_sweep(1, question_kv(0), question_mask, every)
    for f in range(1, me.half - 1):
        if f + 1 > 2:
            gather_step(f + 1, (0,))
            gather_step(f, (1,))
        peaks(f)
    for s in range(2):
        first_max[s] = jnp.max(peak[s], axis=0, keepdims=True)
    weight_sweep(1, 2 * npair, question_kv(0), question_mask, every, first_max)
    near = max(8, 4 * me.half - 4)
    weigh(near, last + 1, first_max)
    if me.half > 2:
        gather_step(me.half, (0,))
        gather_step(me.half - 1, (1,))
    weigh(8, near, first_max)
    peaks(me.half - 1)
    peaks(me.half)
    gather_step(me.half, (1,))
    for s in range(2):
        final_max[s] = jnp.max(peak[s], axis=0, keepdims=True)
        total[s] = total[s] * jnp.exp2((first_max[s] - final_max[s]) * EXP2_SCALE)
    weigh(2, 8, final_max)
    for s in range(2):
        whole = 1.0 / jnp.sum(total[s], axis=0, keepdims=True)
        nearer = whole * jnp.exp2((first_max[s] - final_max[s]) * EXP2_SCALE)
        inverse[0, s] = whole
        inverse[1, s] = nearer
        inverse[2, s] = nearer

    received_all(kvd.at[1, pl.ds(0, npair)], s_recv.at[me.half + 1])

    for copy in own_c:
        copy.wait()
    for kind in range(2):
        received_all(c_in.at[kind, pl.ds(0, peers)], c_recv.at[kind])
    received_all(d_in.at[pl.ds(0, peers)], d_recv)
    for s in range(2):
        sort_rows(cs, c_in, s)
        for j in range(nh):
            turn[:, j * tok : (j + 1) * tok] = d_in[j, :, s * tok : (s + 1) * tok]
        for g in range(group):
            dd[s, 0:1, g * bl : (g + 1) * bl] = turn[g : g + 1, :]

    def low_chunk(s, slot, cols, values, scale_at):
        prob = weights[slot, :, cols] * inverse[scale_at, s, 0:1, cols]
        d_prob = nt_dot(values, cs[s, cols, :])
        low_p[s, :, cols] = prob.astype(jnp.bfloat16)
        low_s[s, :, cols] = (prob * (d_prob - dd[s, 0:1, cols])).astype(jnp.bfloat16)

    def d_value(s):
        return nn_dot(low_p[s], cs[s])

    def d_key(s):
        return nn_dot(low_s[s], qs[s])

    def d_query(s):
        dqt[s] += nn_dot(keys_t[...], low_s[s])

    def backward(s, slot, values, scale_at):
        for cols in every:
            low_chunk(s, slot, cols, values, scale_at)
        made = d_key(s), d_value(s)
        d_query(s)
        return made

    def backward_both(t, values, scale_at):
        for cols in every:
            low_chunk(1, npair + t, cols, values, scale_at)
        todo = [d_key, d_value, d_query]
        made = []
        for cols in every:
            low_chunk(0, t, cols, values, scale_at)
            if todo:
                made.append(todo.pop(0)(1))
        for product in todo:
            made.append(product(1))
        made = made[0] + d_key(0), made[1] + d_value(0)
        d_query(0)
        return made

    def turn_keys(keys):
        keys_t[...] = jnp.transpose(keys.astype(jnp.float32)).astype(jnp.bfloat16)

    def put(t, i, value):
        for c in range(2):
            dkv[t, i, c] = value[c * bl : (c + 1) * bl]

    def core_copy(t):
        return remote(
            dkv.at[t, :, 1 - me.c],
            from_core.at[t],
            core_send,
            core_recv.at[t],
            me.sibling(),
        )

    def hop_copy(way, xs, f):
        return remote(
            low_sums.at[me.pair(xs, me.z + f * (1 - 2 * way))],
            chain.at[way, xs, f - 1],
            hop_send,
            hop_recv.at[way, xs, f - 1],
            me.dev(me.xh, me.z + 1 - 2 * way, me.c),
        )

    def serve(q):
        f, way, xs, t = me.far(q), me.way(q), me.xs(q), me.pair_of(q)
        core_copy(t).wait_recv()
        sums[t] = dkv[t, :, me.c] + from_core[t]

        @pl.when((f > 0) & (f < me.reach(q)))
        def _():
            hop_copy(way, xs, f + 1).wait_recv()
            sums[t] = sums[t] + chain[way, xs, f].astype(jnp.float32)

        @pl.when(f > 0)
        def _():
            low_sums[t] = sums[t].astype(jnp.bfloat16)
            hop_copy(way, xs, f).start()

    turn_keys(question_kv(0))
    dx[0], dx[1] = backward(1, 2 * npair, question_kv(1), 1)
    next_copy = remote(dx.at[:, tail], from_next, n_send, n_recv, me.ctx_prev())
    next_copy.start()

    def r_copies(d, p, device):
        return [
            remote(
                result.at[i, rows_of(p)],
                (gk, gv)[i].at[1, :, own_cols],
                r_send.at[i],
                r_recv.at[i],
                device,
            )
            for i in range(2)
        ]

    own_r = [
        pltpu.make_async_copy(
            result.at[i, own_rows], (gk, gv)[i].at[1, :, own_cols], local_sem.at[i]
        )
        for i in range(2)
    ]

    def send_questions():
        next_copy.wait_recv()
        for i in range(2):
            factor = SCALE if i == 0 else 1.0
            result[i, 0 : bl - QMOST] = dx[i, bl : 2 * bl - QMOST] * factor
            result[i, bl - QMOST : bl] = (
                dx[i, 2 * bl - QMOST : 2 * bl] + from_next[i]
            ) * factor
        over_peers(r_copies, start)
        for copy in own_r:
            copy.start()

    def backward_pair(n, _):
        q = n + 2
        t = me.pair_of(q)
        turn_keys(doc_kv(0, t))
        @pl.when(t > own_pair)
        def _():
            for i, value in enumerate(backward(1, npair + t, doc_kv(1, t), q // 8)):
                put(t, i, value)

        @pl.when(t <= own_pair)
        def _():
            for i, value in enumerate(backward_both(t, doc_kv(1, t), q // 8)):
                put(t, i, value)

        core_copy(t).start()

        @pl.when(n >= LAG)
        def _():
            serve(q - LAG)

        @pl.when(n == npair // 2)
        def _():
            send_questions()

        return 0

    lax.fori_loop(0, npair, backward_pair, 0)

    for s in range(2):
        for g in range(group):
            part = jnp.transpose(dqt[s, :, g * bl : (g + 1) * bl])
            dq[s, :, g * HD : (g + 1) * HD] = (part * SCALE).astype(jnp.bfloat16)

    def out_part(kind, p):
        return dq.at[1 - kind, rows_of(p)]

    def out_copies(kind):
        def made(d, p, device):
            return remote(
                out_part(kind, p),
                head_part(kind, gq, me.h),
                o_send.at[kind],
                o_recv.at[kind],
                device,
            )

        return made

    own_out = [
        pltpu.make_async_copy(out_part(k, me.h), head_part(k, gq, me.h), local_sem.at[4 + k])
        for k in range(2)
    ]
    over_rows(out_copies, start)
    for copy in own_out:
        copy.start()

    def serve_rest(n, _):
        serve(n + 2)
        return 0

    lax.fori_loop(npair - LAG, npair, serve_rest, 0)

    def final_copies(kind):
        def made(d, p, device):
            return [
                remote(
                    final.at[kind, i, rows_of(p)],
                    landed.at[kind, i, me.h],
                    f_send.at[kind, i],
                    f_recv.at[kind, i],
                    device,
                )
                for i in range(2)
            ]

        return made

    for way in range(2):
        for xs in range(2):
            hop_copy(way, xs, 1).wait_recv()
    for kind in (1, 0):
        xs = me.xh if kind == 0 else 1 - me.xh
        t = me.pair(xs, me.z)
        for i in range(2):
            factor = SCALE if i == 0 else 1.0
            final[kind, i] = (
                sums[t, i]
                + chain[0, xs, 0, i].astype(jnp.float32)
                + chain[1, xs, 0, i].astype(jnp.float32)
            ) * factor
        over_peers(final_copies(kind), start, kind == 1)
    for i in range(2):
        landed[0, i, me.h] = final[0, i, own_rows]
    for i in range(2):
        received_all(landed.at[0, i, pl.ds(0, peers)], f_recv.at[0, i])
        received_all(landed.at[1, i], f_recv.at[1, i])
    for i in range(2):
        for h in range(nh):
            owned[i, :, h * HD : (h + 1) * HD] = landed[0, i, h] + landed[1, i, h]
    last_out = [
        pltpu.make_async_copy(owned.at[i], (gk, gv)[i].at[0], local_sem.at[2 + i])
        for i in range(2)
    ]
    for copy in last_out:
        copy.start()

    sent_all(kvd.at[0, pl.ds(0, n_sent["ring"])], g_send)
    sent_all(kvd.at[0, pl.ds(0, n_sent["core"])], s_send)
    for i in range(2):
        sent_all(kvd.at[i, 0, peer_rows], kv_send.at[i, 0])
        sent_all(kvd.at[i, 0, peer_rows], kv_send.at[i, 1])
        sent_all(kvd.at[i, 0], kv_send.at[i, 2])
        sent_all(result.at[i, peer_rows], r_send.at[i])
        sent_all(final.at[0, i, peer_rows], f_send.at[0, i])
        sent_all(final.at[1, i], f_send.at[1, i])
        sent_all(q_in.at[i, pl.ds(0, peers)], q_send.at[i])
        sent_all(c_in.at[i, pl.ds(0, peers)], c_send.at[i])
        sent_all(dq.at[i, peer_rows], o_send.at[i])
        received_all(dq.at[i, peer_rows], o_recv.at[i])
        received_all(result.at[i, peer_rows], r_recv.at[i])
    sent_all(d_in.at[pl.ds(0, peers)], d_send)
    tail_copy.wait_send()
    sent_all(from_core, core_send)
    sent_all(low_sums.at[pl.ds(0, 4 * me.half - 2)], hop_send)
    next_copy.wait_send()
    for copy in own_out + own_r + last_out:
        copy.wait()


def place_results(*refs):
    sources, targets, held, sem = refs[:3], refs[3:6], refs[6:9], refs[9]
    reads = [pltpu.make_async_copy(sources[i], held[i], sem.at[0, i]) for i in range(3)]
    writes = [pltpu.make_async_copy(held[i], targets[i], sem.at[1, i]) for i in range(3)]
    for copy in reads:
        copy.start()
    for i in range(3):
        reads[i].wait()
        writes[i].start()
    for copy in writes:
        copy.wait()


def shards(queries, keys, values, outputs, cotangent, lengths):
    nctx, nh = lax.axis_size("ctx"), lax.axis_size("head")
    tok = queries.shape[1]
    gw = queries.shape[2] // nh
    bl = tok * nh
    nhead = queries.shape[2] // HD
    dims = (nctx, nh, tok, gw, bl, nhead)
    npair = nctx // 2
    group = gw // HD
    rows = group * bl
    hbm = pl.BlockSpec(memory_space=pl.ANY)
    vmem = pl.BlockSpec(memory_space=pltpu.VMEM)
    dma = pltpu.SemaphoreType.DMA
    space = pltpu.VMEM
    f32, b16 = jnp.float32, jnp.bfloat16
    shape = jax.ShapeDtypeStruct
    hops = nctx // 8
    made = (
        shape((2, tok, nh * gw), b16),
        shape((2, tok, nh * HD), f32),
        shape((2, tok, nh * HD), f32),
    )
    results = pl.pallas_call(
        functools.partial(kernel, dims),
        out_shape=made,
        in_specs=[vmem, hbm, hbm, hbm, hbm, hbm],
        out_specs=[hbm] * 3,
        scratch_shapes=[
            space((2, nh, tok, gw), b16),
            space((2, nh, tok, gw), b16),
            space((nh, group, HD), f32),
            space((2, nctx, bl, HD), b16),
            space((2, 2, bl, HD), b16),
            space((2, tok, HD), f32),
            space((HD, HD), f32),
            space((2, rows, HD), b16),
            space((2, rows, HD), b16),
            space((2, 1, rows), f32),
            space((group, bl), f32),
            space((2 * npair + 1, 2 * bl, rows), f32),
            space((2, 8, rows), f32),
            space((2, 8, rows), f32),
            space((2, 1, rows), f32),
            space((2, 1, rows), f32),
            space((3, 2, 1, rows), f32),
            space((2, HD, rows), f32),
            space((HD, 2 * bl), b16),
            space((2, 2 * bl, rows), b16),
            space((2, 2 * bl, rows), b16),
            space((npair, 2, 2, bl, HD), f32),
            space((2, 2 * bl, HD), f32),
            space((2, bl, gw), b16),
            space((npair, 2, bl, HD), f32),
            space((npair, 2, bl, HD), f32),
            space((npair, 2, bl, HD), b16),
            space((2, 2, hops, 2, bl, HD), b16),
            space((2, QMOST, HD), f32),
            space((2, bl, HD), f32),
            space((2, 2, bl, HD), f32),
            space((2, 2, nh, tok, HD), f32),
            space((2, tok, nh * HD), f32),
            space((2, tok, nh * gw), b16),
            space((2, tok, nh * gw), b16),
            dma((2, 3)),
            dma((2, 3)),
            dma((2,)),
            dma((2,)),
            dma((2,)),
            dma((2,)),
            dma,
            dma,
            dma,
            dma((2, hops, 2, 2)),
            dma,
            dma((hops + 2,)),
            dma,
            dma,
            dma,
            dma((npair,)),
            dma,
            dma((2, 2, hops)),
            dma,
            dma,
            dma((2,)),
            dma((2,)),
            dma((2,)),
            dma((2,)),
            dma((2, 2)),
            dma((2, 2)),
            dma((11,)),
        ],
        compiler_params=pltpu.CompilerParams(
            collective_id=0, has_side_effects=True, vmem_limit_bytes=60 * 2**20
        ),
        name="attention_backward",
    )(lengths.reshape(1, -1), queries, keys, values, outputs, cotangent)
    return pl.pallas_call(
        place_results,
        out_shape=made,
        in_specs=[hbm] * 3,
        out_specs=[hbm] * 3,
        scratch_shapes=[space(m.shape, m.dtype) for m in made] + [dma((2, 3))],
        name="place_results",
    )(*results)


def solution(mesh):
    spec = P(None, ("ctx", "head"), None)
    return jax.shard_map(
        shards,
        mesh=mesh,
        in_specs=(spec,) * 5 + (P(),),
        out_specs=(spec,) * 3,
        check_vma=False,
    )
```
